32 devices in a mesh: groups: 2 (over x), gy: 16 (over z, y, core).
Axes of the slice: x: 2, y: 2, z: 4, core: 2. Of those that a mesh axis runs over, the one named last changes fastest.
Arguments:
- observed: float32 [2048, 16, 256], P(('groups', 'gy')), parts along dimension 0, may hold values from -6 to 6
- tf_table: float32 [16], replicated, may hold values from 0.2 to 2
- tilt_index: int32 [513, 129], replicated, may hold values from 0 to 15
- wedge: int32 [513, 129], replicated, may hold values 0 or 1
Outputs:
- restored: float32 [2048, 16, 256], P(('groups', 'gy')), parts along dimension 0
The draws below stay inside these ranges and needn't reach their ends.
There are 2 independent parts, one for each index of `groups`. The reference program is written for one: setup_inputs(seed, part) draws one part's arguments, and reference() takes and returns one part's arrays. A program takes and returns all parts, laid end to end along the dimension named above; an argument that names none is the same for every part. Nothing has to cross between parts.
All inputs are finite; a program needn't handle non-finite values.
Results may differ from the reference program's by a relative error of at most 0.00011.
Values sent between devices are 32-bit elements; how exact they have to be, the bound alone decides.
A program may use at most 64 MiB of HBM per device.

```python
import math
import jax
import jax.numpy as jnp
from jax import lax

NX = 1024
NZ = 256
LEVELS = 16
OUTER = 2
PASSES = 2
NY = 16
NXH = 513
NZH = 129


def with_ends(values, own_key, smallest, top_value):
    shape = values.shape
    place = [jax.random.randint(jax.random.fold_in(own_key, axis), (), 0, shape[axis]) for axis in range(len(shape))]
    values = values.at[tuple(place)].set(smallest)
    longest = shape.index(max(shape))
    place[longest] = (place[longest] + 1) % shape[longest]
    return values.at[tuple(place)].set(top_value)


def block_levels(key, extent, cuts, least, top_value):
    loudness, own = 1.0, jax.random.fold_in(key, 6)
    for dim, shards_of in cuts:
        draws = jnp.exp(jax.random.uniform(jax.random.fold_in(own, dim), (shards_of,), jnp.float32, least / len(cuts), top_value / len(cuts)))
        loudness = loudness * jnp.repeat(draws, extent[dim] // shards_of).reshape([-1 if axis == dim else 1 for axis in range(len(extent))])
    return loudness


def bell_draw(own_key, extent, scale, reach, cuts=(), kind=jnp.bfloat16):
    level = block_levels(own_key, extent, cuts, -0.22, 0.18) if cuts else 1.0
    array = jax.random.normal(own_key, extent, jnp.float32) * scale * level
    return jnp.minimum(jnp.maximum(array, -reach), reach).astype(kind)


def setup_inputs(seed: int = 0, part: int = 0) -> dict:
    splits = jax.random.split(jax.random.key(seed), 5)
    part_keys = jax.random.split(jax.random.fold_in(splits[4], part), 5)
    return {
        "observed": bell_draw(part_keys[0], (NX, NY, NZ), 1.0, 6.0, ((0, 16),), jnp.float32),
        "tf_table": jnp.clip(jnp.exp(jax.random.uniform(splits[1], (LEVELS,), jnp.float32, math.log(0.2), math.log(2.0))), 0.2, 2.0),
        "tilt_index": with_ends(jax.random.randint(splits[2], (NXH, NZH), 0, LEVELS), jax.random.fold_in(splits[2], 1), 0, LEVELS - 1).astype(jnp.int32),
        "wedge": with_ends((jax.random.randint(splits[3], (NXH, NZH), 0, 4) < 3).astype(jnp.int32), jax.random.fold_in(splits[3], 1), 0, 1),
    }


step_dual = 0.14
step_primal = 0.14
huber_eps = 0.05
bound_dual = 0.5

def curvature(field, axis):
    widths = [(0, 0), (0, 0), (0, 0)]
    widths[axis] = (1, 1)
    padded = jnp.pad(field, widths)
    upper = lax.slice_in_dim(padded, 2, padded.shape[axis], axis=axis)
    lower = lax.slice_in_dim(padded, 0, padded.shape[axis] - 2, axis=axis)
    return upper + lower - 2.0 * field

def denoise(target, duals):
    field = target
    lead = target
    for sweep in range(PASSES):
        raised = [(duals[axis] + step_dual * curvature(lead, axis)) / (1.0 + step_dual * huber_eps / bound_dual) for axis in range(3)]
        total = raised[0] * raised[0] + raised[1] * raised[1] + raised[2] * raised[2]
        shrink = jnp.sqrt(jnp.maximum(1.0, total / (bound_dual * bound_dual)))
        duals = (raised[0] / shrink, raised[1] / shrink, raised[2] / shrink)
        adjoint = curvature(duals[0], 0) + curvature(duals[1], 1) + curvature(duals[2], 2)
        updated = (field - step_primal * adjoint + step_primal * target) / (1.0 + step_primal)
        lead = 2.0 * updated - field
        field = updated
    return (field, duals)

def reference(observed, tf_table, tilt_index, wedge):
    half_rows = tf_table[tilt_index] * wedge.astype(tf_table.dtype)
    response = jnp.concatenate([half_rows, half_rows[NX // 2 - 1:0:-1]], 0)
    denom = response * response + 1.0
    g_data = (response / denom)[:, None, :]
    g_prior = (1.0 / denom)[:, None, :]
    spectrum = jnp.fft.rfft2(observed, axes=(0, 2))
    current = observed
    duals = (jnp.zeros_like(observed), jnp.zeros_like(observed), jnp.zeros_like(observed))
    for outer in range(OUTER):
        mixed = g_data * spectrum + g_prior * jnp.fft.rfft2(current, axes=(0, 2))
        target = jnp.fft.irfft2(mixed, s=(NX, NZ), axes=(0, 2)).astype(observed.dtype)
        current, duals = denoise(target, duals)
    return current
```

```python
import functools
import math

import jax
import jax.numpy as jnp
import numpy as np
from jax import lax
from jax.experimental import pallas as pl
from jax.experimental.pallas import tpu as pltpu
from jax.sharding import PartitionSpec as P

OUTER = 2
PASSES = 2
GROUP = 8
LANES = 128
REACH = 6
PAD = 12

step_dual = 0.14
step_primal = 0.14
huber_eps = 0.05
bound_dual = 0.5
relax = 1.0 / (1.0 + step_dual * huber_eps / bound_dual)
gain = step_dual * relax
MESH = pl.DeviceIdType.MESH
f32 = jnp.float32
bf16 = jnp.bfloat16


def split(value):
    high = value.astype(bf16)
    low = (value - high.astype(f32)).astype(bf16)
    return high, low


def dot3(a_high, a_low, b_high, b_low):
    dot = functools.partial(jnp.dot, preferred_element_type=f32)
    return dot(a_high, b_high) + (dot(a_high, b_low) + dot(a_low, b_high))


def kernel(
    n, rows, order,
    cells_ref, table_ref, tilt_ref, wedge_ref, cos_ref, sin_ref, cas_ref, case_ref, zh_ref, zl_ref,
    out_ref,
    gathered, total, data_term, prior_gain, x_high, x_low, m_high, m_low, back,
    target, goal, field, lead, duals, current, code,
    send_sem, recv_sem, back_send, back_recv, halo_send, halo_recv,
):
    me = lax.axis_index("gy")
    chunks, slots = len(order), len(order[0])
    groups = chunks * slots
    part = slots * GROUP
    ny, nz = out_ref.shape[1], out_ref.shape[2]
    halves = nz // LANES
    deep = groups * GROUP * halves
    share = part * halves
    nx = n * rows
    half = n // 2
    span_rows = n * part
    block = math.gcd(nx, 256)
    row_blocks = nx // block

    barrier = pltpu.get_barrier_semaphore()

    def greet(o, carry):
        pl.semaphore_signal(
            barrier, inc=1, device_id={"gy": lax.rem(me + o, n)}, device_id_type=MESH
        )
        return carry

    lax.fori_loop(1, n, greet, 0)

    def each_peer(action):
        def first(k, carry):
            action((1 - me // half) * half + lax.rem(me + k, half))
            return carry

        def second(k, carry):
            action((me // half) * half + lax.rem(me + k, half))
            return carry

        lax.fori_loop(0, half, first, 0)
        lax.fori_loop(1, half, second, 0)

    def every_other(action):
        def step(o, carry):
            action(lax.rem(me + o, n))
            return carry

        lax.fori_loop(1, n, step, 0)

    def cells_of(y, c):
        return pl.ds(pl.multiple_of(y * deep + c * share, share), share)

    def block_of(device):
        return pl.ds(pl.multiple_of(device * share, share), share)

    def cell_row(x, h):
        place = lax.rem(x // GROUP + 1, groups)
        return (place * halves + h) * GROUP + lax.rem(x, GROUP)

    def forward_copy(c, peer, owner):
        return pltpu.make_async_remote_copy(
            src_ref=current.at[cells_of(peer, c)],
            dst_ref=gathered.at[c, block_of(owner)],
            send_sem=send_sem.at[c, peer],
            recv_sem=recv_sem.at[c, owner],
            device_id={"gy": peer},
            device_id_type=MESH,
        )

    def back_copy(c, peer, owner):
        return pltpu.make_async_remote_copy(
            src_ref=back.at[c, block_of(peer)],
            dst_ref=target.at[cells_of(owner, c)],
            send_sem=back_send.at[c, peer],
            recv_sem=back_recv.at[c, owner],
            device_id={"gy": peer},
            device_id_type=MESH,
        )

    def halo_copy(side):
        return pltpu.make_async_remote_copy(
            src_ref=goal.at[pl.ds(PAD + (rows - REACH if side == 0 else 0), REACH)],
            dst_ref=goal.at[pl.ds(PAD + (-REACH if side == 0 else rows), REACH)],
            send_sem=halo_send.at[side],
            recv_sem=halo_recv.at[side],
            device_id={"gy": lax.rem(me + (1 if side == 0 else n - 1), n)},
            device_id_type=MESH,
        )

    def send_forward(c):
        each_peer(lambda peer: forward_copy(c, peer, me).start())
        gathered[c, block_of(me)] = current[cells_of(me, c)]

    def stage(y, carry):
        stride = ny * halves
        for h in range(halves):
            first = (y // GROUP * halves + h) * GROUP + y % GROUP
            lines = cells_ref[pl.ds(first, rows, stride=stride), :]
            for g in range(groups):
                at = y * deep + ((g + 1) % groups * halves + h) * GROUP
                current[pl.ds(pl.multiple_of(at, GROUP), GROUP), :] = lines[
                    g * GROUP : (g + 1) * GROUP, :
                ]
        return carry

    def make_tables():
        def body(m, carry):
            lines = jnp.concatenate(
                [
                    cos_ref[pl.ds(k, 1), :] * cas_ref[...] + sin_ref[pl.ds(k, 1), :] * case_ref[...]
                    for k in (2 * m, 2 * m + 1)
                ],
                axis=0,
            )
            at = pl.ds(pl.multiple_of(m * 2 * GROUP, 2 * GROUP), 2 * GROUP)
            x_high[at, :], x_low[at, :] = split(lines)
            return carry

        lax.fori_loop(0, nx // (2 * GROUP), body, 0)

    def make_filter():
        columns, lines = tilt_ref.shape
        code[...] = jnp.zeros_like(code)
        code[0:columns, 0:lines] = jnp.where(wedge_ref[...] == 0, 0, tilt_ref[...] + 1).astype(f32)
        width, depth = code.shape
        kz = lax.broadcasted_iota(jnp.int32, (nz, width), 0)
        pick_z = jnp.where(
            lax.broadcasted_iota(jnp.int32, (nz, width), 1) == jnp.minimum(kz, nz - kz), 1.0, 0.0
        ).astype(bf16)
        spread = jnp.dot(pick_z, code[...].astype(bf16), preferred_element_type=f32).astype(bf16)

        def body(b, carry):
            line = b * block + lax.broadcasted_iota(jnp.int32, (block, depth), 0)
            c = line // span_rows
            slot = line % part // GROUP
            group = (c * slots + slot + groups - 1) % groups
            kx = line % span_rows // part * rows + group * GROUP + line % GROUP
            column = lax.broadcasted_iota(jnp.int32, (block, depth), 1)
            pick_x = jnp.where(column == jnp.minimum(kx, nx - kx), 1.0, 0.0).astype(bf16)
            which = lax.dot_general(
                pick_x, spread, (((1,), (1,)), ((), ())), preferred_element_type=f32
            )
            response = jnp.zeros_like(which)
            for level in range(table_ref.shape[0]):
                response = jnp.where(which == level + 1.0, table_ref[level], response)
            prior = 1.0 / (response * response + 1.0)
            at = pl.ds(pl.multiple_of(b * block, block), block)
            prior_gain[at, :] = prior
            data_term[at, :] = response * prior
            return carry

        lax.fori_loop(0, row_blocks, body, 0)

    def filtered(outer):
        turns = list(range(1, chunks)) + [0]
        for c in turns:
            every_other(lambda owner: forward_copy(c, owner, owner).wait_recv())
            pieces = gathered[c].reshape(n * slots, halves, GROUP, LANES)
            lines = [pieces[:, h].reshape(span_rows, LANES) for h in range(halves)]
            high, low = split(jnp.concatenate(lines, axis=1))
            high, low = split(dot3(high, low, zh_ref[...], zl_ref[...]))

            def body(b, carry):
                at = pl.ds(pl.multiple_of(b * block, block), block)
                span = pl.ds(c * span_rows, span_rows)
                spectrum = dot3(x_high[at, span], x_low[at, span], high, low)
                if c != turns[0]:
                    spectrum = total[at, :] + spectrum
                if c != turns[-1]:
                    total[at, :] = spectrum
                    return carry
                if outer == 0:
                    spectrum = spectrum * gain
                    data_term[at, :] = data_term[at, :] * spectrum
                a_high, a_low = split(data_term[at, :] + prior_gain[at, :] * spectrum)
                m_high[at, :], m_low[at, :] = split(dot3(a_high, a_low, zh_ref[...], zl_ref[...]))
                return carry

            lax.fori_loop(0, row_blocks, body, 0)

    def send_back(c):
        step = math.gcd(span_rows, 256)

        def body(b, carry):
            line = pl.ds(pl.multiple_of(c * span_rows + b * step, step), step)
            lines = dot3(x_high[line, :], x_low[line, :], m_high[...], m_low[...])
            pieces = [
                lines[:, h * LANES : (h + 1) * LANES].reshape(step // GROUP, 1, GROUP, LANES)
                for h in range(halves)
            ]
            count = step * halves
            at = pl.ds(pl.multiple_of(b * count, count), count)
            back[c, at] = jnp.concatenate(pieces, axis=1).reshape(count, LANES)
            return carry

        lax.fori_loop(0, span_rows // step, body, 0)
        each_peer(lambda peer: back_copy(c, peer, me).start())
        target[cells_of(me, c)] = back[c, block_of(me)]

    def sum_y(value):
        pieces = [value[y : y + GROUP, :] for y in range(0, ny, GROUP)]
        nothing = jnp.zeros_like(pieces[0])
        line = lax.broadcasted_iota(jnp.int32, pieces[0].shape, 0)
        ups = [nothing] + [pltpu.roll(piece, 1, 0) for piece in pieces]
        downs = [pltpu.roll(piece, GROUP - 1, 0) for piece in pieces] + [nothing]
        return jnp.concatenate(
            [
                jnp.where(line == 0, ups[y], ups[y + 1])
                + jnp.where(line == GROUP - 1, downs[y + 1], downs[y])
                for y in range(len(pieces))
            ],
            axis=0,
        )

    def sum_z(value):
        pieces = [value[:, z : z + LANES] for z in range(0, nz, LANES)]
        nothing = jnp.zeros_like(pieces[0])
        lane = lax.broadcasted_iota(jnp.int32, pieces[0].shape, 1)
        ups = [nothing] + [pltpu.roll(piece, 1, 1) for piece in pieces]
        downs = [pltpu.roll(piece, LANES - 1, 1) for piece in pieces] + [nothing]
        return jnp.concatenate(
            [
                jnp.where(lane == 0, ups[z], ups[z + 1])
                + jnp.where(lane == LANES - 1, downs[z + 1], downs[z])
                for z in range(len(pieces))
            ],
            axis=1,
        )

    def collect(c):
        def body(r, carry):
            for g in order[c]:
                for h in range(halves):
                    for y in range(0, ny, GROUP):
                        first = y * deep + ((g + 1) % groups * halves + h) * GROUP + r
                        goal[PAD + g * GROUP + r, y : y + GROUP, h * LANES : (h + 1) * LANES] = (
                            target[pl.ds(first, GROUP, stride=deep), :]
                        )
            return carry

        lax.fori_loop(0, GROUP, body, 0)

    def rise_load(origin, x, fresh):
        here, before, after = origin[x], origin[x - 1], origin[x + 1]
        olds = None if fresh else [dual[x] for dual in duals]
        return here, before, after, olds

    def rise(loaded, keep):
        here, before, after, olds = loaded
        twice = here + here
        raised = [before + after - twice, sum_y(here) - twice, sum_z(here) - twice]
        if olds is not None:
            raised = [old + bend for old, bend in zip(olds, raised)]
        norm = raised[0] * raised[0] + raised[1] * raised[1] + raised[2] * raised[2]
        shrink = lax.rsqrt(jnp.maximum(1.0 / relax**2, norm * (1.0 / (bound_dual * relax) ** 2)))
        if keep is not None:
            shrink = shrink * keep
        return [part_of * shrink for part_of in raised]

    def fall_load(x):
        dual_x, dual_y, dual_z = duals
        return (
            dual_x[x], dual_x[x - 1], dual_x[x + 1],
            dual_y[x], dual_z[x], goal[x],
        )

    def fall(loaded):
        in_x, before, after, in_y, in_z, _ = loaded
        middle = in_x + in_y + in_z
        return (before + after + sum_y(in_y) + sum_z(in_z) - (middle + middle)) * (
            step_primal * step_dual / (1.0 + step_primal)
        )

    def sweep_rows(outer, start, stop):
        def run(first, last):
            masked = first < REACH or last > rows
            ends = first >= REACH and last <= rows + REACH

            def keep(x):
                if not masked:
                    return None
                whole = me * rows + PAD + x
                return jnp.where(jnp.logical_and(whole >= 2 * PAD, whole < nx + 2 * PAD), 1.0, 0.0)

            def body(x, carry):
                low = rise_load(goal, x, outer == 0)
                mid = fall_load(x - 2)
                high = rise_load(lead, x - 4, False)
                if ends:
                    top = fall_load(x - 6)
                    old = field[x - 6]
                fresh = rise(low, keep(x))
                updated = mid[-1] - fall(mid)
                if masked:
                    updated = updated * keep(x - 2)
                again = rise(high, keep(x - 4))
                if ends:
                    final = (
                        old * (1.0 / (1.0 + step_primal))
                        + top[-1] * (step_primal / (1.0 + step_primal))
                        - fall(top)
                    )
                for dual, value in zip(duals, fresh):
                    dual[x] = value
                lead[x - 2] = updated + updated - mid[-1]
                field[x - 2] = updated
                for dual, value in zip(duals, again):
                    dual[x - 4] = value
                if ends and outer == OUTER - 1:
                    out_ref[x - PAD - 6] = final * (1.0 / gain)
                elif ends:
                    for h in range(halves):
                        at = cell_row(x - PAD - 6, h)
                        for y in range(0, ny, GROUP):
                            current[pl.ds(at + y * deep, GROUP, stride=deep), :] = final[
                                y : y + GROUP, h * LANES : (h + 1) * LANES
                            ]
                return carry

            lax.fori_loop(first + PAD, last + PAD, body, 0)

        marks = [start] + [x for x in (REACH, rows, rows + REACH) if start < x < stop] + [stop]
        for first, last in zip(marks[:-1], marks[1:]):
            run(first, last)

    def denoise(outer, arrive):
        stop = rows + REACH + (1 if outer < OUTER - 1 else 0)
        done = -5 if outer < OUTER - 1 else -3
        ready = {}
        if outer < OUTER - 1:
            for c in range(1, chunks):
                ready[(c * slots + slots - 1) * GROUP + REACH] = c
            ready[rows + REACH] = 0
        for c in range(min(1, chunks - 1), chunks):
            if c > 0:
                arrive(c)
                collect(c)
            if c == min(1, chunks - 1):
                halo_done()
            limit = stop if c == chunks - 1 else (c * slots + slots - 1) * GROUP - 1
            for x in sorted(ready):
                if done < x <= limit:
                    sweep_rows(outer, done, x)
                    send_forward(ready[x])
                    done = x
            if done < limit:
                sweep_rows(outer, done, limit)
                done = limit

    lax.fori_loop(0, ny, stage, 0)
    pl.semaphore_wait(barrier, n - 1)
    for c in list(range(1, chunks)) + [0]:
        send_forward(c)

    @pl.when(me == 0)
    def _():
        goal[PAD - REACH : PAD] = jnp.zeros((REACH, ny, nz), f32)

    @pl.when(me == n - 1)
    def _():
        goal[PAD + rows : PAD + rows + REACH] = jnp.zeros((REACH, ny, nz), f32)

    make_tables()
    make_filter()

    def halo_done():
        @pl.when(me > 0)
        def _():
            halo_copy(0).wait_recv()

        @pl.when(me < n - 1)
        def _():
            halo_copy(1).wait_recv()

    for outer in range(OUTER):
        filtered(outer)
        for c in range(chunks):
            every_other(lambda peer: forward_copy(c, peer, me).wait_send())
        for c in range(chunks):
            send_back(c)

        def arrive(c):
            every_other(lambda owner: back_copy(c, owner, owner).wait_recv())

        arrive(0)
        collect(0)

        @pl.when(me < n - 1)
        def _():
            halo_copy(0).start()

        @pl.when(me > 0)
        def _():
            halo_copy(1).start()

        denoise(outer, arrive)

        @pl.when(me < n - 1)
        def _():
            halo_copy(0).wait_send()

        @pl.when(me > 0)
        def _():
            halo_copy(1).wait_send()

        for c in range(chunks):
            every_other(lambda peer: back_copy(c, peer, me).wait_send())


def constants(n, rows, order, nz):
    nx = n * rows
    place = np.array(
        [
            d * rows + g * GROUP + r
            for some in order
            for d in range(n)
            for g in some
            for r in range(GROUP)
        ]
    )
    turn = 2.0 * math.pi / nx
    coarse = (place[::GROUP, None] * place[None, :] % nx) * turn
    fine = (np.arange(GROUP)[:, None] * place[None, :] % nx) * turn
    norm = 1.0 / math.sqrt(nx)
    tables = (
        np.cos(coarse),
        np.sin(coarse),
        (np.cos(fine) + np.sin(fine)) * norm,
        (np.cos(fine) - np.sin(fine)) * norm,
    )
    k = np.arange(nz)
    angle = (k[:, None] * k[None, :] % nz) * (2.0 * math.pi / nz)
    cas_z = ((np.cos(angle) + np.sin(angle)) / math.sqrt(nz)).astype(np.float32)
    z_high = cas_z.astype(bf16)
    z_low = (cas_z - z_high.astype(np.float32)).astype(bf16)
    return [jnp.asarray(t, f32) for t in tables] + [jnp.asarray(z_high), jnp.asarray(z_low)]


def local(n, observed, tf_table, tilt_index, wedge):
    rows, ny, nz = observed.shape
    nx = n * rows
    groups = rows // GROUP
    line = [groups - 1] + list(range(groups - 1))
    slots = 2 if groups % 2 == 0 else groups
    order = [tuple(line[c : c + slots]) for c in range(0, groups, slots)]
    chunks = len(order)
    lines, columns = tilt_index.shape
    depth, width = -(-lines // 128) * 128, -(-columns // 128) * 128
    tables = constants(n, rows, order, nz)
    tiles = observed.reshape(rows, ny // GROUP, GROUP, nz // LANES, LANES)
    tiles = tiles.transpose(0, 1, 3, 2, 4).reshape(-1, LANES)
    vmem = pl.BlockSpec(memory_space=pltpu.VMEM)
    smem = pl.BlockSpec(memory_space=pltpu.SMEM)
    grid_rows = pltpu.VMEM((rows + 2 * PAD, ny, nz), f32)
    plane = pltpu.VMEM((nx, nz), f32)
    blocks = pltpu.VMEM((chunks, n * slots * GROUP * nz // LANES, LANES), f32)
    cells = pltpu.VMEM((rows * ny * nz // LANES, LANES), f32)
    semaphores = pltpu.SemaphoreType.DMA((chunks, n))
    result = pl.pallas_call(
        functools.partial(kernel, n, rows, order),
        out_shape=jax.ShapeDtypeStruct((rows, ny, nz), f32),
        in_specs=[vmem, smem] + [vmem] * 8,
        out_specs=vmem,
        scratch_shapes=[
            blocks,
            plane,
            plane,
            plane,
            pltpu.VMEM((nx, nx), bf16),
            pltpu.VMEM((nx, nx), bf16),
            pltpu.VMEM((nx, nz), bf16),
            pltpu.VMEM((nx, nz), bf16),
            blocks,
            cells,
            grid_rows,
            grid_rows,
            grid_rows,
            [grid_rows] * 3,
            cells,
            pltpu.VMEM((width, depth), f32),
            semaphores,
            semaphores,
            semaphores,
            semaphores,
            pltpu.SemaphoreType.DMA((2,)),
            pltpu.SemaphoreType.DMA((2,)),
        ],
        compiler_params=pltpu.CompilerParams(
            collective_id=0, has_side_effects=True, vmem_limit_bytes=60 * 1024 * 1024
        ),
    )(tiles, tf_table, tilt_index.T, wedge.T, *tables)
    return result


def solution(mesh):
    in_specs = (P(("groups", "gy"), None, None), P(), P(), P())
    out_specs = P(("groups", "gy"), None, None)
    body = functools.partial(local, mesh.shape["gy"])
    return jax.shard_map(body, mesh=mesh, in_specs=in_specs, out_specs=out_specs, check_vma=False)
```

```python
import functools
import math

import jax
import jax.numpy as jnp
import numpy as np
from jax import lax
from jax.experimental import pallas as pl
from jax.experimental.pallas import tpu as pltpu
from jax.sharding import PartitionSpec as P

OUTER = 2
PASSES = 2
GROUP = 8
LANES = 128
REACH = 6
PAD = 12

step_dual = 0.14
step_primal = 0.14
huber_eps = 0.05
bound_dual = 0.5
relax = 1.0 / (1.0 + step_dual * huber_eps / bound_dual)
gain = step_dual * relax
MESH = pl.DeviceIdType.MESH
f32 = jnp.float32
bf16 = jnp.bfloat16


def split(value):
    high = value.astype(bf16)
    low = (value - high.astype(f32)).astype(bf16)
    return high, low


def dot3(a_high, a_low, b_high, b_low):
    dot = functools.partial(jnp.dot, preferred_element_type=f32)
    return dot(a_high, b_high) + (dot(a_high, b_low) + dot(a_low, b_high))


def kernel(
    n, rows, order, cross,
    cells_ref, table_ref, tilt_ref, wedge_ref, cos_ref, sin_ref, cas_ref, case_ref, zh_ref, zl_ref,
    out_ref,
    gathered, total, data_term, prior_gain, x_high, x_low, m_high, m_low, back,
    target, goal, field, lead, duals, current, code, passing, result,
    send_sem, recv_sem, back_send, back_recv, halo_send, halo_recv,
    pass_send, pass_recv, pass_on, home_send, home_recv, own_sem,
):
    gx, gy = lax.axis_index("groups"), lax.axis_index("gy")
    half = n // 2
    high, low = gy // half, gy % half
    if cross:
        near = gx == high
        who = gx * half + low
        me = low % 2 * half + low // 2 * 2 + gx
    else:
        near = gx == gx
        who = gy
        me = gy
    far = jnp.logical_not(near)

    def owner_device(owner, first):
        if not cross:
            return {"gy": owner}
        block = gx if first else high
        return {"groups": owner // half, "gy": block * half + owner % half}

    def slab_device(slab):
        if not cross:
            return {"gy": slab}
        return {"groups": slab % 2, "gy": high * half + slab % half // 2 * 2 + slab // half}

    chunks, slots = len(order), len(order[0])
    groups = chunks * slots
    part = slots * GROUP
    ny, nz = out_ref.shape[1], out_ref.shape[2]
    halves = nz // LANES
    deep = groups * GROUP * halves
    share = part * halves
    nx = n * rows
    span_rows = n * part
    block = math.gcd(nx, 256)
    row_blocks = nx // block

    barrier = pltpu.get_barrier_semaphore()

    def greet(o, carry):
        if cross:
            other = lax.rem(gx * n + gy + o, 2 * n)
            device = {"groups": other // n, "gy": other % n}
        else:
            device = {"gy": lax.rem(gy + o, n)}
        pl.semaphore_signal(barrier, inc=1, device_id=device, device_id_type=MESH)
        return carry

    greeted = 2 * n if cross else n
    lax.fori_loop(1, greeted, greet, 0)

    def every_other(mine, action):
        def step(o, carry):
            action(lax.rem(mine + o, n))
            return carry

        lax.fori_loop(1, n, step, 0)

    def every_half(action):
        def step(o, carry):
            action(lax.rem(low + o, half))
            return carry

        lax.fori_loop(0, half, step, 0)

    def cells_of(y, c):
        return pl.ds(pl.multiple_of(y * deep + c * share, share), share)

    def block_of(device):
        return pl.ds(pl.multiple_of(device * share, share), share)

    def cell_row(x, h):
        place = lax.rem(x // GROUP + 1, groups)
        return (place * halves + h) * GROUP + lax.rem(x, GROUP)

    def forward_copy(c, owner, slab, first):
        return pltpu.make_async_remote_copy(
            src_ref=current.at[cells_of(owner, c)],
            dst_ref=gathered.at[c, block_of(slab)],
            send_sem=send_sem.at[c, owner],
            recv_sem=recv_sem.at[c, slab],
            device_id=owner_device(owner, first),
            device_id_type=MESH,
        )

    def pass_copy(c, k):
        return pltpu.make_async_remote_copy(
            src_ref=current.at[cells_of((1 - gx) * half + k, c)],
            dst_ref=passing.at[cells_of(k, c)],
            send_sem=pass_send.at[c, k],
            recv_sem=pass_recv.at[c, k],
            device_id={"groups": 1 - gx, "gy": gy},
            device_id_type=MESH,
        )

    def pass_on_copy(c, k):
        return pltpu.make_async_remote_copy(
            src_ref=passing.at[cells_of(k, c)],
            dst_ref=gathered.at[c, block_of(gy)],
            send_sem=pass_on.at[c, k],
            recv_sem=recv_sem.at[c, gy],
            device_id={"groups": gx, "gy": (1 - gx) * half + k},
            device_id_type=MESH,
        )

    def back_copy(c, slab, owner):
        return pltpu.make_async_remote_copy(
            src_ref=back.at[c, block_of(slab)],
            dst_ref=target.at[cells_of(owner, c)],
            send_sem=back_send.at[c, slab],
            recv_sem=back_recv.at[c, owner],
            device_id=slab_device(slab),
            device_id_type=MESH,
        )

    def halo_copy(side):
        return pltpu.make_async_remote_copy(
            src_ref=goal.at[pl.ds(PAD + (rows - REACH if side == 0 else 0), REACH)],
            dst_ref=goal.at[pl.ds(PAD + (-REACH if side == 0 else rows), REACH)],
            send_sem=halo_send.at[side],
            recv_sem=halo_recv.at[side],
            device_id=slab_device(lax.rem(me + (1 if side == 0 else n - 1), n)),
            device_id_type=MESH,
        )

    def home_copy(i, first, last):
        span = pl.ds(first, last - first)
        return pltpu.make_async_remote_copy(
            src_ref=result.at[span],
            dst_ref=out_ref.at[span],
            send_sem=home_send.at[i],
            recv_sem=home_recv.at[i],
            device_id={"groups": high, "gy": me},
            device_id_type=MESH,
        )

    def own_copy(i, first, last):
        span = pl.ds(first, last - first)
        return pltpu.make_async_copy(result.at[span], out_ref.at[span], own_sem.at[i])

    if cross:
        home = jnp.logical_and(gx == high, gy == me)
        away = jnp.logical_not(home)
    else:
        home, away = near, far

    def deliver(i, first, last):
        if cross:

            @pl.when(away)
            def _():
                home_copy(i, first, last).start()

        @pl.when(home)
        def _():
            own_copy(i, first, last).start()

    def delivered(i, first, last):
        if cross:

            @pl.when(away)
            def _():
                home_copy(i, first, last).wait_send()
                home_copy(i, first, last).wait_recv()

        @pl.when(home)
        def _():
            own_copy(i, first, last).wait()

    def send_first(c):
        if cross:

            @pl.when(far)
            def _():
                every_half(lambda k: pass_copy(c, k).start())
                every_half(lambda k: forward_copy(c, gx * half + k, gy, True).start())

        @pl.when(near)
        def _():
            every_other(who, lambda owner: forward_copy(c, owner, gy, True).start())
            gathered[c, block_of(gy)] = current[cells_of(who, c)]

    def pass_along(c):
        if cross:

            @pl.when(near)
            def _():
                def step(k):
                    pass_copy(c, k).wait_recv()
                    pass_on_copy(c, k).start()

                every_half(step)

    def first_arrived(c):
        every_other(gy, lambda slab: forward_copy(c, who, slab, True).wait_recv())
        if cross:

            @pl.when(far)
            def _():
                forward_copy(c, who, gy, True).wait_recv()

    def first_sent(c):
        if cross:

            @pl.when(far)
            def _():
                every_half(lambda k: pass_copy(c, k).wait_send())
                every_half(lambda k: forward_copy(c, gx * half + k, gy, True).wait_send())

        @pl.when(near)
        def _():
            every_other(who, lambda owner: forward_copy(c, owner, gy, True).wait_send())
            if cross:
                every_half(lambda k: pass_on_copy(c, k).wait_send())

    def send_forward(c):
        every_other(who, lambda owner: forward_copy(c, owner, me, False).start())
        gathered[c, block_of(me)] = current[cells_of(who, c)]

    def stage(y, carry):
        stride = ny * halves
        for h in range(halves):
            first = (y // GROUP * halves + h) * GROUP + y % GROUP
            lines = cells_ref[pl.ds(first, rows, stride=stride), :]
            for g in range(groups):
                at = y * deep + ((g + 1) % groups * halves + h) * GROUP
                current[pl.ds(pl.multiple_of(at, GROUP), GROUP), :] = lines[
                    g * GROUP : (g + 1) * GROUP, :
                ]
        return carry

    def make_tables():
        def body(m, carry):
            lines = jnp.concatenate(
                [
                    cos_ref[pl.ds(k, 1), :] * cas_ref[...] + sin_ref[pl.ds(k, 1), :] * case_ref[...]
                    for k in (2 * m, 2 * m + 1)
                ],
                axis=0,
            )
            at = pl.ds(pl.multiple_of(m * 2 * GROUP, 2 * GROUP), 2 * GROUP)
            x_high[at, :], x_low[at, :] = split(lines)
            return carry

        lax.fori_loop(0, nx // (2 * GROUP), body, 0)

    def make_filter():
        columns, lines = tilt_ref.shape
        code[...] = jnp.zeros_like(code)
        code[0:columns, 0:lines] = jnp.where(wedge_ref[...] == 0, 0, tilt_ref[...] + 1).astype(f32)
        width, depth = code.shape
        kz = lax.broadcasted_iota(jnp.int32, (nz, width), 0)
        pick_z = jnp.where(
            lax.broadcasted_iota(jnp.int32, (nz, width), 1) == jnp.minimum(kz, nz - kz), 1.0, 0.0
        ).astype(bf16)
        spread = jnp.dot(pick_z, code[...].astype(bf16), preferred_element_type=f32).astype(bf16)

        def body(b, carry):
            line = b * block + lax.broadcasted_iota(jnp.int32, (block, depth), 0)
            c = line // span_rows
            slot = line % part // GROUP
            group = (c * slots + slot + groups - 1) % groups
            kx = line % span_rows // part * rows + group * GROUP + line % GROUP
            column = lax.broadcasted_iota(jnp.int32, (block, depth), 1)
            pick_x = jnp.where(column == jnp.minimum(kx, nx - kx), 1.0, 0.0).astype(bf16)
            which = lax.dot_general(
                pick_x, spread, (((1,), (1,)), ((), ())), preferred_element_type=f32
            )
            response = jnp.zeros_like(which)
            for level in range(table_ref.shape[0]):
                response = jnp.where(which == level + 1.0, table_ref[level], response)
            prior = 1.0 / (response * response + 1.0)
            at = pl.ds(pl.multiple_of(b * block, block), block)
            prior_gain[at, :] = prior
            data_term[at, :] = response * prior
            return carry

        lax.fori_loop(0, row_blocks, body, 0)

    def filtered(outer):
        for c in turns:
            if outer == 0:
                first_arrived(c)
            else:
                every_other(me, lambda slab: forward_copy(c, who, slab, False).wait_recv())
            pieces = gathered[c].reshape(n * slots, halves, GROUP, LANES)
            lines = [pieces[:, h].reshape(span_rows, LANES) for h in range(halves)]
            high, low = split(jnp.concatenate(lines, axis=1))
            high, low = split(dot3(high, low, zh_ref[...], zl_ref[...]))

            def body(b, carry):
                at = pl.ds(pl.multiple_of(b * block, block), block)
                span = pl.ds(c * span_rows, span_rows)
                spectrum = dot3(x_high[at, span], x_low[at, span], high, low)
                if c != turns[0]:
                    spectrum = total[at, :] + spectrum
                if c != turns[-1]:
                    total[at, :] = spectrum
                    return carry
                if outer == 0:
                    spectrum = spectrum * gain
                    data_term[at, :] = data_term[at, :] * spectrum
                a_high, a_low = split(data_term[at, :] + prior_gain[at, :] * spectrum)
                m_high[at, :], m_low[at, :] = split(dot3(a_high, a_low, zh_ref[...], zl_ref[...]))
                return carry

            lax.fori_loop(0, row_blocks, body, 0)

    def send_back(c):
        step = math.gcd(span_rows, 256)

        def body(b, carry):
            line = pl.ds(pl.multiple_of(c * span_rows + b * step, step), step)
            lines = dot3(x_high[line, :], x_low[line, :], m_high[...], m_low[...])
            pieces = [
                lines[:, h * LANES : (h + 1) * LANES].reshape(step // GROUP, 1, GROUP, LANES)
                for h in range(halves)
            ]
            count = step * halves
            at = pl.ds(pl.multiple_of(b * count, count), count)
            back[c, at] = jnp.concatenate(pieces, axis=1).reshape(count, LANES)
            return carry

        lax.fori_loop(0, span_rows // step, body, 0)
        every_other(me, lambda slab: back_copy(c, slab, who).start())
        target[cells_of(who, c)] = back[c, block_of(me)]

    def sum_y(value):
        pieces = [value[y : y + GROUP, :] for y in range(0, ny, GROUP)]
        nothing = jnp.zeros_like(pieces[0])
        line = lax.broadcasted_iota(jnp.int32, pieces[0].shape, 0)
        ups = [nothing] + [pltpu.roll(piece, 1, 0) for piece in pieces]
        downs = [pltpu.roll(piece, GROUP - 1, 0) for piece in pieces] + [nothing]
        return jnp.concatenate(
            [
                jnp.where(line == 0, ups[y], ups[y + 1])
                + jnp.where(line == GROUP - 1, downs[y + 1], downs[y])
                for y in range(len(pieces))
            ],
            axis=0,
        )

    def sum_z(value):
        pieces = [value[:, z : z + LANES] for z in range(0, nz, LANES)]
        nothing = jnp.zeros_like(pieces[0])
        lane = lax.broadcasted_iota(jnp.int32, pieces[0].shape, 1)
        ups = [nothing] + [pltpu.roll(piece, 1, 1) for piece in pieces]
        downs = [pltpu.roll(piece, LANES - 1, 1) for piece in pieces] + [nothing]
        return jnp.concatenate(
            [
                jnp.where(lane == 0, ups[z], ups[z + 1])
                + jnp.where(lane == LANES - 1, downs[z + 1], downs[z])
                for z in range(len(pieces))
            ],
            axis=1,
        )

    def collect(c):
        def body(r, carry):
            for g in order[c]:
                for h in range(halves):
                    for y in range(0, ny, GROUP):
                        first = y * deep + ((g + 1) % groups * halves + h) * GROUP + r
                        goal[PAD + g * GROUP + r, y : y + GROUP, h * LANES : (h + 1) * LANES] = (
                            target[pl.ds(first, GROUP, stride=deep), :]
                        )
            return carry

        lax.fori_loop(0, GROUP, body, 0)

    def rise_load(origin, x, fresh):
        here, before, after = origin[x], origin[x - 1], origin[x + 1]
        olds = None if fresh else [dual[x] for dual in duals]
        return here, before, after, olds

    def rise(loaded, keep):
        here, before, after, olds = loaded
        twice = here + here
        raised = [before + after - twice, sum_y(here) - twice, sum_z(here) - twice]
        if olds is not None:
            raised = [old + bend for old, bend in zip(olds, raised)]
        norm = raised[0] * raised[0] + raised[1] * raised[1] + raised[2] * raised[2]
        shrink = lax.rsqrt(jnp.maximum(1.0 / relax**2, norm * (1.0 / (bound_dual * relax) ** 2)))
        if keep is not None:
            shrink = shrink * keep
        return [part_of * shrink for part_of in raised]

    def fall_load(x):
        dual_x, dual_y, dual_z = duals
        return (
            dual_x[x], dual_x[x - 1], dual_x[x + 1],
            dual_y[x], dual_z[x], goal[x],
        )

    def fall(loaded):
        in_x, before, after, in_y, in_z, _ = loaded
        middle = in_x + in_y + in_z
        return (before + after + sum_y(in_y) + sum_z(in_z) - (middle + middle)) * (
            step_primal * step_dual / (1.0 + step_primal)
        )

    def sweep_rows(outer, start, stop):
        def run(first, last):
            masked = first < REACH or last > rows
            ends = first >= REACH and last <= rows + REACH

            def keep(x):
                if not masked:
                    return None
                whole = me * rows + PAD + x
                return jnp.where(jnp.logical_and(whole >= 2 * PAD, whole < nx + 2 * PAD), 1.0, 0.0)

            def body(x, carry):
                low = rise_load(goal, x, outer == 0)
                mid = fall_load(x - 2)
                high = rise_load(lead, x - 4, False)
                if ends:
                    top = fall_load(x - 6)
                    old = field[x - 6]
                fresh = rise(low, keep(x))
                updated = mid[-1] - fall(mid)
                if masked:
                    updated = updated * keep(x - 2)
                again = rise(high, keep(x - 4))
                if ends:
                    final = (
                        old * (1.0 / (1.0 + step_primal))
                        + top[-1] * (step_primal / (1.0 + step_primal))
                        - fall(top)
                    )
                for dual, value in zip(duals, fresh):
                    dual[x] = value
                lead[x - 2] = updated + updated - mid[-1]
                field[x - 2] = updated
                for dual, value in zip(duals, again):
                    dual[x - 4] = value
                if ends and outer == OUTER - 1:
                    result[x - PAD - 6] = final * (1.0 / gain)
                elif ends:
                    for h in range(halves):
                        at = cell_row(x - PAD - 6, h)
                        for y in range(0, ny, GROUP):
                            current[pl.ds(at + y * deep, GROUP, stride=deep), :] = final[
                                y : y + GROUP, h * LANES : (h + 1) * LANES
                            ]
                return carry

            lax.fori_loop(first + PAD, last + PAD, body, 0)

        marks = [start] + [x for x in (REACH, rows, rows + REACH) if start < x < stop] + [stop]
        for first, last in zip(marks[:-1], marks[1:]):
            run(first, last)

    homes = [(x, x + GROUP) for x in range(0, rows, GROUP)]

    def denoise(outer, arrive):
        stop = rows + REACH + (1 if outer < OUTER - 1 else 0)
        done = -5 if outer < OUTER - 1 else -3
        ready = {}
        if outer < OUTER - 1:
            for c in range(1, chunks):
                ready[(c * slots + slots - 1) * GROUP + REACH] = c
            ready[rows + REACH] = 0
        else:
            ready = {last + REACH: i for i, (_, last) in enumerate(homes)}
        for c in range(min(1, chunks - 1), chunks):
            if c > 0:
                arrive(c)
                collect(c)
            if c == min(1, chunks - 1):
                halo_done()
            limit = stop if c == chunks - 1 else (c * slots + slots - 1) * GROUP - 1
            for x in sorted(ready):
                if done < x <= limit:
                    sweep_rows(outer, done, x)
                    if outer < OUTER - 1:
                        send_forward(ready[x])
                    else:
                        deliver(ready[x], *homes[ready[x]])
                    done = x
            if done < limit:
                sweep_rows(outer, done, limit)
                done = limit

    turns = list(range(1, chunks)) + [0]
    lax.fori_loop(0, ny, stage, 0)
    pl.semaphore_wait(barrier, greeted - 1)
    for c in turns:
        send_first(c)

    @pl.when(me == 0)
    def _():
        goal[PAD - REACH : PAD] = jnp.zeros((REACH, ny, nz), f32)

    @pl.when(me == n - 1)
    def _():
        goal[PAD + rows : PAD + rows + REACH] = jnp.zeros((REACH, ny, nz), f32)

    make_tables()
    for c in turns[: chunks // 2]:
        pass_along(c)
    make_filter()
    for c in turns[chunks // 2 :]:
        pass_along(c)

    def halo_done():
        @pl.when(me > 0)
        def _():
            halo_copy(0).wait_recv()

        @pl.when(me < n - 1)
        def _():
            halo_copy(1).wait_recv()

    for outer in range(OUTER):
        filtered(outer)
        for c in range(chunks):
            if outer == 0:
                first_sent(c)
            else:
                every_other(who, lambda owner: forward_copy(c, owner, me, False).wait_send())
        for c in range(chunks):
            send_back(c)

        def arrive(c):
            every_other(who, lambda owner: back_copy(c, me, owner).wait_recv())

        arrive(0)
        collect(0)

        @pl.when(me < n - 1)
        def _():
            halo_copy(0).start()

        @pl.when(me > 0)
        def _():
            halo_copy(1).start()

        denoise(outer, arrive)

        @pl.when(me < n - 1)
        def _():
            halo_copy(0).wait_send()

        @pl.when(me > 0)
        def _():
            halo_copy(1).wait_send()

        for c in range(chunks):
            every_other(me, lambda slab: back_copy(c, slab, who).wait_send())
    for i, (first, last) in enumerate(homes):
        delivered(i, first, last)


def constants(n, rows, order, nz):
    nx = n * rows
    place = np.array(
        [
            d * rows + g * GROUP + r
            for some in order
            for d in range(n)
            for g in some
            for r in range(GROUP)
        ]
    )
    turn = 2.0 * math.pi / nx
    coarse = (place[::GROUP, None] * place[None, :] % nx) * turn
    fine = (np.arange(GROUP)[:, None] * place[None, :] % nx) * turn
    norm = 1.0 / math.sqrt(nx)
    tables = (
        np.cos(coarse),
        np.sin(coarse),
        (np.cos(fine) + np.sin(fine)) * norm,
        (np.cos(fine) - np.sin(fine)) * norm,
    )
    k = np.arange(nz)
    angle = (k[:, None] * k[None, :] % nz) * (2.0 * math.pi / nz)
    cas_z = ((np.cos(angle) + np.sin(angle)) / math.sqrt(nz)).astype(np.float32)
    z_high = cas_z.astype(bf16)
    z_low = (cas_z - z_high.astype(np.float32)).astype(bf16)
    return [jnp.asarray(t, f32) for t in tables] + [jnp.asarray(z_high), jnp.asarray(z_low)]


def local(n, cross, observed, tf_table, tilt_index, wedge):
    rows, ny, nz = observed.shape
    nx = n * rows
    groups = rows // GROUP
    line = [groups - 1] + list(range(groups - 1))
    slots = 2 if groups % 2 == 0 else groups
    order = [tuple(line[c : c + slots]) for c in range(0, groups, slots)]
    chunks = len(order)
    lines, columns = tilt_index.shape
    depth, width = -(-lines // 128) * 128, -(-columns // 128) * 128
    tables = constants(n, rows, order, nz)
    tiles = observed.reshape(rows, ny // GROUP, GROUP, nz // LANES, LANES)
    tiles = tiles.transpose(0, 1, 3, 2, 4).reshape(-1, LANES)
    vmem = pl.BlockSpec(memory_space=pltpu.VMEM)
    smem = pl.BlockSpec(memory_space=pltpu.SMEM)
    grid_rows = pltpu.VMEM((rows + 2 * PAD, ny, nz), f32)
    plane = pltpu.VMEM((nx, nz), f32)
    blocks = pltpu.VMEM((chunks, n * slots * GROUP * nz // LANES, LANES), f32)
    cells = pltpu.VMEM((rows * ny * nz // LANES, LANES), f32)
    semaphores = pltpu.SemaphoreType.DMA((chunks, n))
    result = pl.pallas_call(
        functools.partial(kernel, n, rows, order, cross),
        out_shape=jax.ShapeDtypeStruct((rows, ny, nz), f32),
        in_specs=[vmem, smem] + [vmem] * 8,
        out_specs=pl.BlockSpec(memory_space=pl.ANY),
        scratch_shapes=[
            blocks,
            plane,
            plane,
            plane,
            pltpu.VMEM((nx, nx), bf16),
            pltpu.VMEM((nx, nx), bf16),
            pltpu.VMEM((nx, nz), bf16),
            pltpu.VMEM((nx, nz), bf16),
            blocks,
            cells,
            grid_rows,
            grid_rows,
            grid_rows,
            [grid_rows] * 3,
            cells,
            pltpu.VMEM((width, depth), f32),
            pltpu.VMEM((rows * ny * nz // LANES // 2, LANES), f32),
            pltpu.VMEM((rows, ny, nz), f32),
            semaphores,
            semaphores,
            semaphores,
            semaphores,
            pltpu.SemaphoreType.DMA((2,)),
            pltpu.SemaphoreType.DMA((2,)),
            pltpu.SemaphoreType.DMA((chunks, n // 2)),
            pltpu.SemaphoreType.DMA((chunks, n // 2)),
            pltpu.SemaphoreType.DMA((chunks, n // 2)),
            pltpu.SemaphoreType.DMA((groups,)),
            pltpu.SemaphoreType.DMA((groups,)),
            pltpu.SemaphoreType.DMA((groups,)),
        ],
        compiler_params=pltpu.CompilerParams(
            collective_id=0, has_side_effects=True, vmem_limit_bytes=60 * 1024 * 1024
        ),
    )(tiles, tf_table, tilt_index.T, wedge.T, *tables)
    return result


def solution(mesh):
    in_specs = (P(("groups", "gy"), None, None), P(), P(), P())
    out_specs = P(("groups", "gy"), None, None)
    n = mesh.shape["gy"]
    cross = mesh.shape["groups"] == 2 and n % 4 == 0
    body = functools.partial(local, n, cross)
    return jax.shard_map(body, mesh=mesh, in_specs=in_specs, out_specs=out_specs, check_vma=False)
```

```python
import functools
import math

import jax
import jax.numpy as jnp
import numpy as np
from jax import lax
from jax.experimental import pallas as pl
from jax.experimental.pallas import tpu as pltpu
from jax.sharding import PartitionSpec as P

OUTER = 2
PASSES = 2
GROUP = 8
LANES = 128
REACH = 6
PAD = 12

step_dual = 0.14
step_primal = 0.14
huber_eps = 0.05
bound_dual = 0.5
relax = 1.0 / (1.0 + step_dual * huber_eps / bound_dual)
gain = step_dual * relax
MESH = pl.DeviceIdType.MESH
f32 = jnp.float32
bf16 = jnp.bfloat16


def split(value):
    high = value.astype(bf16)
    low = (value - high.astype(f32)).astype(bf16)
    return high, low


def dot3(a_high, a_low, b_high, b_low):
    dot = functools.partial(jnp.dot, preferred_element_type=f32)
    return dot(a_high, b_high) + (dot(a_high, b_low) + dot(a_low, b_high))


def kernel(
    n, rows, slots, cross,
    cells_ref, table_ref, tilt_ref, wedge_ref, cos_ref, sin_ref, cas_ref, case_ref, zh_ref, zl_ref,
    out_ref,
    gathered, total, data_term, prior_gain, x_high, x_low, m_high, m_low, back,
    target, goal, field, lead, duals, current, code, passing, result,
    send_sem, recv_sem, back_send, back_recv,
    pass_send, pass_recv, pass_on, home_send, home_recv, own_sem,
):
    gx, gy = lax.axis_index("groups"), lax.axis_index("gy")
    half = n // 2
    high, low = gy // half, gy % half
    if cross:
        near = gx == high
        who = gx * half + low
        me = low % 2 * half + low // 2 * 2 + gx
    else:
        near = gx == gx
        who = gy
        me = gy
    far = jnp.logical_not(near)

    def owner_device(owner, first):
        if not cross:
            return {"gy": owner}
        block = gx if first else high
        return {"groups": owner // half, "gy": block * half + owner % half}

    def slab_device(slab):
        if not cross:
            return {"gy": slab}
        return {"groups": slab % 2, "gy": high * half + slab % half // 2 * 2 + slab // half}

    groups = rows // GROUP
    chunks = groups // slots
    extents = (groups + 2) // slots
    part = slots * GROUP
    ny, nz = out_ref.shape[1], out_ref.shape[2]
    halves = nz // LANES
    tall = GROUP * halves
    deep = groups * tall
    wide = (groups + 2) * tall
    share = slots * tall
    batches = [
        (m, max(m * slots - 1, 0), min((m + 1) * slots - 1, groups))
        for m in range(1 // slots, groups // slots + 1)
    ]
    first_turn = [batch for batch in batches if batch[0] % chunks > 0]
    first_turn += [batch for batch in batches if batch[0] % chunks == 0]
    nx = n * rows
    span_rows = n * part
    block = math.gcd(nx, 256)
    row_blocks = nx // block

    barrier = pltpu.get_barrier_semaphore()

    def greet(o, carry):
        if cross:
            other = lax.rem(gx * n + gy + o, 2 * n)
            device = {"groups": other // n, "gy": other % n}
        else:
            device = {"gy": lax.rem(gy + o, n)}
        pl.semaphore_signal(barrier, inc=1, device_id=device, device_id_type=MESH)
        return carry

    greeted = 2 * n if cross else n
    lax.fori_loop(1, greeted, greet, 0)

    def every_other(mine, action):
        def step(o, carry):
            action(lax.rem(mine + o, n))
            return carry

        lax.fori_loop(1, n, step, 0)

    def every_half(action):
        def step(o, carry):
            action(lax.rem(low + o, half))
            return carry

        lax.fori_loop(0, half, step, 0)

    def cells_of(y, batch, depth):
        _, low_group, high_group = batch
        return pl.ds(pl.multiple_of(y * depth + low_group * tall, tall), (high_group - low_group) * tall)

    def seat_of(slab, batch):
        m, low_group, high_group = batch
        line = lax.rem(slab + m // chunks, n) * slots + (low_group + 1) % slots
        return pl.ds(pl.multiple_of(line * tall, tall), (high_group - low_group) * tall)

    def block_of(j, slab):
        return pl.ds(pl.multiple_of(lax.rem(slab + j // chunks, n) * share, share), share)

    def extent_of(y, j):
        return pl.ds(pl.multiple_of(y * wide + j * share, tall), share)

    def cell_row(x, h):
        return (x // GROUP * halves + h) * GROUP + lax.rem(x, GROUP)

    def forward_copy(batch, owner, slab, first):
        m = batch[0]
        return pltpu.make_async_remote_copy(
            src_ref=current.at[cells_of(owner, batch, deep)],
            dst_ref=gathered.at[m % chunks, seat_of(slab, batch)],
            send_sem=send_sem.at[m],
            recv_sem=recv_sem.at[m],
            device_id=owner_device(owner, first),
            device_id_type=MESH,
        )

    def pass_copy(batch, k):
        m = batch[0]
        return pltpu.make_async_remote_copy(
            src_ref=current.at[cells_of((1 - gx) * half + k, batch, deep)],
            dst_ref=passing.at[cells_of(k, batch, deep)],
            send_sem=pass_send.at[m],
            recv_sem=pass_recv.at[m],
            device_id={"groups": 1 - gx, "gy": gy},
            device_id_type=MESH,
        )

    def pass_on_copy(batch, k):
        m = batch[0]
        return pltpu.make_async_remote_copy(
            src_ref=passing.at[cells_of(k, batch, deep)],
            dst_ref=gathered.at[m % chunks, seat_of(gy, batch)],
            send_sem=pass_on.at[m],
            recv_sem=recv_sem.at[m],
            device_id={"groups": gx, "gy": (1 - gx) * half + k},
            device_id_type=MESH,
        )

    def back_copy(j, slab):
        return pltpu.make_async_remote_copy(
            src_ref=back.at[j % chunks, block_of(j, slab)],
            dst_ref=target.at[extent_of(who, j)],
            send_sem=back_send.at[j],
            recv_sem=back_recv.at[j],
            device_id=slab_device(slab),
            device_id_type=MESH,
        )

    def home_copy(first, last):
        span = pl.ds(first, last - first)
        return pltpu.make_async_remote_copy(
            src_ref=result.at[span],
            dst_ref=out_ref.at[span],
            send_sem=home_send,
            recv_sem=home_recv,
            device_id={"groups": high, "gy": me},
            device_id_type=MESH,
        )

    def own_copy(first, last):
        span = pl.ds(first, last - first)
        return pltpu.make_async_copy(result.at[span], out_ref.at[span], own_sem)

    if cross:
        home = jnp.logical_and(gx == high, gy == me)
        away = jnp.logical_not(home)
    else:
        home, away = near, far

    def deliver(first, last):
        if cross:

            @pl.when(away)
            def _():
                home_copy(first, last).start()

        @pl.when(home)
        def _():
            own_copy(first, last).start()

    def delivered():
        if cross:

            @pl.when(away)
            def _():
                home_copy(0, rows).wait_send()
                home_copy(0, rows).wait_recv()

        @pl.when(home)
        def _():
            own_copy(0, rows).wait()

    def bulk(ref, lines, send, recv):
        span = ref.at[pl.ds(0, lines)]
        return pltpu.make_async_remote_copy(
            src_ref=span,
            dst_ref=span,
            send_sem=send,
            recv_sem=recv,
            device_id=owner_device(who, False),
            device_id_type=MESH,
        )

    def lines_of(batch):
        return (batch[2] - batch[1]) * tall

    def forward_bulk(batch, count):
        m = batch[0]
        return bulk(current, count * lines_of(batch), send_sem.at[m], recv_sem.at[m])

    def pass_bulk(batch):
        m = batch[0]
        return bulk(passing, half * lines_of(batch), pass_send.at[m], pass_recv.at[m])

    def pass_on_bulk(batch):
        m = batch[0]
        return bulk(passing, half * lines_of(batch), pass_on.at[m], pass_recv.at[m])

    def back_bulk(j):
        return bulk(target, (n - 1) * share, back_send.at[j], back_recv.at[j])

    def keep_own(batch, slab):
        gathered[batch[0] % chunks, seat_of(slab, batch)] = current[cells_of(who, batch, deep)]

    def send_direct(batch):
        if cross:

            @pl.when(far)
            def _():
                every_half(lambda k: forward_copy(batch, gx * half + k, gy, True).start())

        @pl.when(near)
        def _():
            every_other(who, lambda owner: forward_copy(batch, owner, gy, True).start())
            keep_own(batch, gy)

    def send_aside(batch):
        if cross:

            @pl.when(far)
            def _():
                every_half(lambda k: pass_copy(batch, k).start())

    def pass_along(batch):
        if cross:

            @pl.when(near)
            def _():
                pass_bulk(batch).wait_recv()
                every_half(lambda k: pass_on_copy(batch, k).start())

    def first_arrived(batch):
        @pl.when(near)
        def _():
            forward_bulk(batch, n - 1).wait_recv()

        if cross:

            @pl.when(far)
            def _():
                forward_bulk(batch, n).wait_recv()

    def first_sent(batch):
        @pl.when(near)
        def _():
            forward_bulk(batch, n - 1).wait_send()
            if cross:
                pass_on_bulk(batch).wait_send()

        if cross:

            @pl.when(far)
            def _():
                forward_bulk(batch, half).wait_send()
                pass_bulk(batch).wait_send()

    def send_forward(batch):
        every_other(who, lambda owner: forward_copy(batch, owner, me, False).start())
        keep_own(batch, me)

    def stage(y, carry):
        stride = ny * halves
        for h in range(halves):
            first = (y // GROUP * halves + h) * GROUP + y % GROUP
            lines = cells_ref[pl.ds(first, rows, stride=stride), :]
            for g in range(groups):
                at = y * deep + g * tall + h * GROUP
                current[pl.ds(pl.multiple_of(at, GROUP), GROUP), :] = lines[
                    g * GROUP : (g + 1) * GROUP, :
                ]
        return carry

    def make_tables():
        def body(m, carry):
            lines = jnp.concatenate(
                [
                    cos_ref[pl.ds(k, 1), :] * cas_ref[...] + sin_ref[pl.ds(k, 1), :] * case_ref[...]
                    for k in (2 * m, 2 * m + 1)
                ],
                axis=0,
            )
            at = pl.ds(pl.multiple_of(m * 2 * GROUP, 2 * GROUP), 2 * GROUP)
            x_high[at, :], x_low[at, :] = split(lines)
            return carry

        lax.fori_loop(0, nx // (2 * GROUP), body, 0)

    def make_filter():
        columns, lines = tilt_ref.shape
        code[...] = jnp.zeros_like(code)
        code[0:columns, 0:lines] = jnp.where(wedge_ref[...] == 0, 0, tilt_ref[...] + 1).astype(f32)
        width, depth = code.shape
        kz = lax.broadcasted_iota(jnp.int32, (nz, width), 0)
        pick_z = jnp.where(
            lax.broadcasted_iota(jnp.int32, (nz, width), 1) == jnp.minimum(kz, nz - kz), 1.0, 0.0
        ).astype(bf16)
        spread = jnp.dot(pick_z, code[...].astype(bf16), preferred_element_type=f32).astype(bf16)

        def body(b, carry):
            line = b * block + lax.broadcasted_iota(jnp.int32, (block, depth), 0)
            c = line // span_rows
            slot = line % part // GROUP
            place = line % span_rows // part * groups + c * slots + slot - 1
            kx = (place * GROUP + line % GROUP + nx) % nx
            column = lax.broadcasted_iota(jnp.int32, (block, depth), 1)
            pick_x = jnp.where(column == jnp.minimum(kx, nx - kx), 1.0, 0.0).astype(bf16)
            which = lax.dot_general(
                pick_x, spread, (((1,), (1,)), ((), ())), preferred_element_type=f32
            )
            response = jnp.zeros_like(which)
            for level in range(table_ref.shape[0]):
                response = jnp.where(which == level + 1.0, table_ref[level], response)
            prior = 1.0 / (response * response + 1.0)
            at = pl.ds(pl.multiple_of(b * block, block), block)
            prior_gain[at, :] = prior
            data_term[at, :] = response * prior
            return carry

        lax.fori_loop(0, row_blocks, body, 0)

    def filtered(outer):
        for c in turns:
            for batch in batches:
                if batch[0] % chunks == c and outer == 0:
                    first_arrived(batch)
                elif batch[0] % chunks == c:
                    forward_bulk(batch, n - 1).wait_recv()
            pieces = gathered[c].reshape(n * slots, halves, GROUP, LANES)
            lines = [pieces[:, h].reshape(span_rows, LANES) for h in range(halves)]
            high, low = split(jnp.concatenate(lines, axis=1))
            high, low = split(dot3(high, low, zh_ref[...], zl_ref[...]))

            def body(b, carry):
                at = pl.ds(pl.multiple_of(b * block, block), block)
                span = pl.ds(c * span_rows, span_rows)
                spectrum = dot3(x_high[at, span], x_low[at, span], high, low)
                if c != turns[0]:
                    spectrum = total[at, :] + spectrum
                if c != turns[-1]:
                    total[at, :] = spectrum
                    return carry
                if outer == 0:
                    spectrum = spectrum * gain
                    data_term[at, :] = data_term[at, :] * spectrum
                a_high, a_low = split(data_term[at, :] + prior_gain[at, :] * spectrum)
                m_high[at, :], m_low[at, :] = split(dot3(a_high, a_low, zh_ref[...], zl_ref[...]))
                return carry

            lax.fori_loop(0, row_blocks, body, 0)

    def send_back(c):
        step = math.gcd(span_rows, 256)

        def body(b, carry):
            line = pl.ds(pl.multiple_of(c * span_rows + b * step, step), step)
            lines = dot3(x_high[line, :], x_low[line, :], m_high[...], m_low[...])
            pieces = [
                lines[:, h * LANES : (h + 1) * LANES].reshape(step // GROUP, 1, GROUP, LANES)
                for h in range(halves)
            ]
            count = step * halves
            at = pl.ds(pl.multiple_of(b * count, count), count)
            back[c, at] = jnp.concatenate(pieces, axis=1).reshape(count, LANES)
            return carry

        lax.fori_loop(0, span_rows // step, body, 0)
        start_back(c)

    def start_back(j):
        every_other(me, lambda slab: back_copy(j, slab).start())
        target[extent_of(who, j)] = back[j % chunks, block_of(j, me)]

    def sum_y(value):
        pieces = [value[y : y + GROUP, :] for y in range(0, ny, GROUP)]
        nothing = jnp.zeros_like(pieces[0])
        line = lax.broadcasted_iota(jnp.int32, pieces[0].shape, 0)
        ups = [nothing] + [pltpu.roll(piece, 1, 0) for piece in pieces]
        downs = [pltpu.roll(piece, GROUP - 1, 0) for piece in pieces] + [nothing]
        return jnp.concatenate(
            [
                jnp.where(line == 0, ups[y], ups[y + 1])
                + jnp.where(line == GROUP - 1, downs[y + 1], downs[y])
                for y in range(len(pieces))
            ],
            axis=0,
        )

    def sum_z(value):
        pieces = [value[:, z : z + LANES] for z in range(0, nz, LANES)]
        nothing = jnp.zeros_like(pieces[0])
        lane = lax.broadcasted_iota(jnp.int32, pieces[0].shape, 1)
        ups = [nothing] + [pltpu.roll(piece, 1, 1) for piece in pieces]
        downs = [pltpu.roll(piece, LANES - 1, 1) for piece in pieces] + [nothing]
        return jnp.concatenate(
            [
                jnp.where(lane == 0, ups[z], ups[z + 1])
                + jnp.where(lane == LANES - 1, downs[z + 1], downs[z])
                for z in range(len(pieces))
            ],
            axis=1,
        )

    def collect(j):
        def gather(e):
            def body(r, carry):
                for h in range(halves):
                    for y in range(0, ny, GROUP):
                        goal[
                            PAD + (e - 1) * GROUP + r,
                            y : y + GROUP,
                            h * LANES : (h + 1) * LANES,
                        ] = target[pl.ds(y * wide + e * tall + h * GROUP + r, GROUP, stride=wide), :]
                return carry

            lax.fori_loop(0, GROUP, body, 0)

        for e in range(j * slots, (j + 1) * slots):
            if e == 0:
                pl.when(me > 0)(functools.partial(gather, e))
            elif e == groups + 1:
                pl.when(me < n - 1)(functools.partial(gather, e))
            else:
                gather(e)

    def rise_load(origin, x, fresh):
        here, before, after = origin[x], origin[x - 1], origin[x + 1]
        olds = None if fresh else [dual[x] for dual in duals]
        return here, before, after, olds

    def rise(loaded, keep):
        here, before, after, olds = loaded
        twice = here + here
        raised = [before + after - twice, sum_y(here) - twice, sum_z(here) - twice]
        if olds is not None:
            raised = [old + bend for old, bend in zip(olds, raised)]
        norm = raised[0] * raised[0] + raised[1] * raised[1] + raised[2] * raised[2]
        shrink = lax.rsqrt(jnp.maximum(1.0 / relax**2, norm * (1.0 / (bound_dual * relax) ** 2)))
        if keep is not None:
            shrink = shrink * keep
        return [part_of * shrink for part_of in raised]

    def fall_load(x):
        dual_x, dual_y, dual_z = duals
        return (
            dual_x[x], dual_x[x - 1], dual_x[x + 1],
            dual_y[x], dual_z[x], goal[x],
        )

    def fall(loaded):
        in_x, before, after, in_y, in_z, _ = loaded
        middle = in_x + in_y + in_z
        return (before + after + sum_y(in_y) + sum_z(in_z) - (middle + middle)) * (
            step_primal * step_dual / (1.0 + step_primal)
        )

    def sweep_rows(outer, start, stop):
        def run(first, last):
            masked = first < REACH or last > rows
            ends = first >= REACH and last <= rows + REACH

            def keep(x):
                if not masked:
                    return None
                whole = me * rows + PAD + x
                return jnp.where(jnp.logical_and(whole >= 2 * PAD, whole < nx + 2 * PAD), 1.0, 0.0)

            def body(x, carry):
                low = rise_load(goal, x, outer == 0)
                mid = fall_load(x - 2)
                high = rise_load(lead, x - 4, False)
                if ends:
                    top = fall_load(x - 6)
                    old = field[x - 6]
                fresh = rise(low, keep(x))
                updated = mid[-1] - fall(mid)
                if masked:
                    updated = updated * keep(x - 2)
                again = rise(high, keep(x - 4))
                if ends:
                    final = (
                        old * (1.0 / (1.0 + step_primal))
                        + top[-1] * (step_primal / (1.0 + step_primal))
                        - fall(top)
                    )
                for dual, value in zip(duals, fresh):
                    dual[x] = value
                lead[x - 2] = updated + updated - mid[-1]
                field[x - 2] = updated
                for dual, value in zip(duals, again):
                    dual[x - 4] = value
                if ends and outer == OUTER - 1:
                    result[x - PAD - 6] = final * (1.0 / gain)
                elif ends:
                    for h in range(halves):
                        at = cell_row(x - PAD - 6, h)
                        for y in range(0, ny, GROUP):
                            current[pl.ds(at + y * deep, GROUP, stride=deep), :] = final[
                                y : y + GROUP, h * LANES : (h + 1) * LANES
                            ]
                return carry

            lax.fori_loop(first + PAD, last + PAD, body, 0)

        marks = [start] + [x for x in (REACH, rows, rows + REACH) if start < x < stop] + [stop]
        for first, last in zip(marks[:-1], marks[1:]):
            run(first, last)

    homes = [(x, x + GROUP) for x in range(0, rows, GROUP)]

    def denoise(outer):
        stop = rows + REACH + (1 if outer < OUTER - 1 else 0)
        done = -5 if outer < OUTER - 1 else -3
        if outer < OUTER - 1:
            ready = {batch[2] * GROUP + REACH: batch for batch in batches}
        else:
            ready = {last + REACH: (first, last) for first, last in homes}
        for j in range(extents):
            back_bulk(j).wait_recv()
            collect(j)
            limit = stop if j == extents - 1 else ((j + 1) * slots - 1) * GROUP - 1
            for x in sorted(ready):
                if done < x <= limit:
                    sweep_rows(outer, done, x)
                    if outer < OUTER - 1:
                        send_forward(ready[x])
                    else:
                        deliver(*ready[x])
                    done = x
            if done < limit:
                sweep_rows(outer, done, limit)
                done = limit

    turns = list(range(1, chunks)) + [0]
    lax.fori_loop(0, ny, stage, 0)
    pl.semaphore_wait(barrier, greeted - 1)
    ahead = min(2, len(first_turn))
    for batch in first_turn[:ahead]:
        send_aside(batch)
    for i, batch in enumerate(first_turn):
        send_direct(batch)
        for later in first_turn[i + ahead : i + ahead + 1]:
            send_aside(later)

    @pl.when(me == 0)
    def _():
        goal[PAD - GROUP : PAD] = jnp.zeros((GROUP, ny, nz), f32)

    @pl.when(me == n - 1)
    def _():
        goal[PAD + rows : PAD + rows + GROUP] = jnp.zeros((GROUP, ny, nz), f32)

    make_tables()
    for batch in first_turn[: len(first_turn) // 2]:
        pass_along(batch)
    make_filter()
    for batch in first_turn[len(first_turn) // 2 :]:
        pass_along(batch)
    for outer in range(OUTER):
        filtered(outer)
        for c in range(chunks):
            send_back(c)
        for j in range(chunks, extents):
            start_back(j)
        for batch in batches:
            if outer == 0:
                first_sent(batch)
            else:
                forward_bulk(batch, n - 1).wait_send()
        denoise(outer)
        for j in range(extents):
            back_bulk(j).wait_send()
    delivered()


def constants(n, rows, slots, nz):
    nx = n * rows
    groups = rows // GROUP
    place = np.array(
        [
            ((d * groups + c + slot - 1) * GROUP + r) % nx
            for c in range(0, groups, slots)
            for d in range(n)
            for slot in range(slots)
            for r in range(GROUP)
        ]
    )
    turn = 2.0 * math.pi / nx
    coarse = (place[::GROUP, None] * place[None, :] % nx) * turn
    fine = (np.arange(GROUP)[:, None] * place[None, :] % nx) * turn
    norm = 1.0 / math.sqrt(nx)
    tables = (
        np.cos(coarse),
        np.sin(coarse),
        (np.cos(fine) + np.sin(fine)) * norm,
        (np.cos(fine) - np.sin(fine)) * norm,
    )
    k = np.arange(nz)
    angle = (k[:, None] * k[None, :] % nz) * (2.0 * math.pi / nz)
    cas_z = ((np.cos(angle) + np.sin(angle)) / math.sqrt(nz)).astype(np.float32)
    z_high = cas_z.astype(bf16)
    z_low = (cas_z - z_high.astype(np.float32)).astype(bf16)
    return [jnp.asarray(t, f32) for t in tables] + [jnp.asarray(z_high), jnp.asarray(z_low)]


def local(n, cross, observed, tf_table, tilt_index, wedge):
    rows, ny, nz = observed.shape
    nx = n * rows
    groups = rows // GROUP
    slots = 2 if groups % 2 == 0 else 1
    chunks = groups // slots
    extents = (groups + 2) // slots
    lines, columns = tilt_index.shape
    depth, width = -(-lines // 128) * 128, -(-columns // 128) * 128
    tables = constants(n, rows, slots, nz)
    tiles = observed.reshape(rows, ny // GROUP, GROUP, nz // LANES, LANES)
    tiles = tiles.transpose(0, 1, 3, 2, 4).reshape(-1, LANES)
    vmem = pl.BlockSpec(memory_space=pltpu.VMEM)
    smem = pl.BlockSpec(memory_space=pltpu.SMEM)
    grid_rows = pltpu.VMEM((rows + 2 * PAD, ny, nz), f32)
    plane = pltpu.VMEM((nx, nz), f32)
    blocks = pltpu.VMEM((chunks, n * slots * GROUP * nz // LANES, LANES), f32)
    cells = pltpu.VMEM((rows * ny * nz // LANES, LANES), f32)
    semaphores = pltpu.SemaphoreType.DMA((extents,))
    landing = pltpu.VMEM((ny * (groups + 2) * GROUP * nz // LANES, LANES), f32)
    result = pl.pallas_call(
        functools.partial(kernel, n, rows, slots, cross),
        out_shape=jax.ShapeDtypeStruct((rows, ny, nz), f32),
        in_specs=[vmem, smem] + [vmem] * 8,
        out_specs=pl.BlockSpec(memory_space=pl.ANY),
        scratch_shapes=[
            blocks,
            plane,
            plane,
            plane,
            pltpu.VMEM((nx, nx), bf16),
            pltpu.VMEM((nx, nx), bf16),
            pltpu.VMEM((nx, nz), bf16),
            pltpu.VMEM((nx, nz), bf16),
            blocks,
            landing,
            grid_rows,
            grid_rows,
            grid_rows,
            [grid_rows] * 3,
            cells,
            pltpu.VMEM((width, depth), f32),
            pltpu.VMEM((rows * ny * nz // LANES // 2, LANES), f32),
            pltpu.VMEM((rows, ny, nz), f32),
            semaphores,
            semaphores,
            semaphores,
            semaphores,
            semaphores,
            semaphores,
            semaphores,
            pltpu.SemaphoreType.DMA(()),
            pltpu.SemaphoreType.DMA(()),
            pltpu.SemaphoreType.DMA(()),
        ],
        compiler_params=pltpu.CompilerParams(
            collective_id=0, has_side_effects=True, vmem_limit_bytes=60 * 1024 * 1024
        ),
    )(tiles, tf_table, tilt_index.T, wedge.T, *tables)
    return result


def solution(mesh):
    in_specs = (P(("groups", "gy"), None, None), P(), P(), P())
    out_specs = P(("groups", "gy"), None, None)
    n = mesh.shape["gy"]
    cross = mesh.shape["groups"] == 2 and n % 4 == 0
    body = functools.partial(local, n, cross)
    return jax.shard_map(body, mesh=mesh, in_specs=in_specs, out_specs=out_specs, check_vma=False)
```

```python
import functools
import math

import jax
import jax.numpy as jnp
import numpy as np
from jax import lax
from jax.experimental import pallas as pl
from jax.experimental.pallas import tpu as pltpu
from jax.sharding import PartitionSpec as P

OUTER = 2
PASSES = 2
GROUP = 8
LANES = 128
REACH = 6
PAD = 12

step_dual = 0.14
step_primal = 0.14
huber_eps = 0.05
bound_dual = 0.5
relax = 1.0 / (1.0 + step_dual * huber_eps / bound_dual)
gain = step_dual * relax
MESH = pl.DeviceIdType.MESH
f32 = jnp.float32
bf16 = jnp.bfloat16


def split(value):
    high = value.astype(bf16)
    low = (value - high.astype(f32)).astype(bf16)
    return high, low


def dot3(a_high, a_low, b_high, b_low):
    dot = functools.partial(jnp.dot, preferred_element_type=f32)
    return dot(a_high, b_high) + (dot(a_high, b_low) + dot(a_low, b_high))


def kernel(
    n, rows, slots, cross,
    cells_ref, table_ref, tilt_ref, wedge_ref, cos_ref, sin_ref, cas_ref, case_ref, zh_ref, zl_ref,
    out_ref,
    gathered, total, data_term, prior_gain, x_high, x_low, m_high, m_low, back,
    target, goal, field, lead, duals, current, code, passing, result,
    send_sem, recv_sem, back_send, back_recv,
    pass_send, pass_recv, pass_on, home_send, home_recv, own_sem,
):
    gx, gy = lax.axis_index("groups"), lax.axis_index("gy")
    half = n // 2
    high, low = gy // half, gy % half
    if cross:
        near = gx == high
        who = gx * half + low
        me = low % 2 * half + low // 2 * 2 + gx
    else:
        near = gx == gx
        who = gy
        me = gy
    far = jnp.logical_not(near)

    def owner_device(owner, first):
        if not cross:
            return {"gy": owner}
        block = gx if first else high
        return {"groups": owner // half, "gy": block * half + owner % half}

    def slab_device(slab):
        if not cross:
            return {"gy": slab}
        return {"groups": slab % 2, "gy": high * half + slab % half // 2 * 2 + slab // half}

    groups = rows // GROUP
    chunks = groups // slots
    extents = (groups + 2) // slots
    part = slots * GROUP
    ny, nz = out_ref.shape[1], out_ref.shape[2]
    halves = nz // LANES
    tall = GROUP * halves
    deep = groups * tall
    wide = (groups + 2) * tall
    share = slots * tall
    batches = [
        (m, max(m * slots - 1, 0), min((m + 1) * slots - 1, groups))
        for m in range(1 // slots, groups // slots + 1)
    ]
    first_turn = [batch for batch in batches if batch[0] % chunks > 0]
    first_turn += [batch for batch in batches if batch[0] % chunks == 0]
    nx = n * rows
    span_rows = n * part
    block = math.gcd(nx, 256)
    row_blocks = nx // block

    barrier = pltpu.get_barrier_semaphore()

    def greet(o, carry):
        if cross:
            other = lax.rem(gx * n + gy + o, 2 * n)
            device = {"groups": other // n, "gy": other % n}
        else:
            device = {"gy": lax.rem(gy + o, n)}
        pl.semaphore_signal(barrier, inc=1, device_id=device, device_id_type=MESH)
        return carry

    greeted = 2 * n if cross else n
    lax.fori_loop(1, greeted, greet, 0)

    def every_other(mine, action):
        def step(o, carry):
            action(lax.rem(mine + o, n))
            return carry

        lax.fori_loop(1, n, step, 0)

    def every_half(action, start=0, stop=None):
        count = (half if stop is None else stop) - start

        def step(o, carry):
            action(start + lax.rem(low + o, count))
            return carry

        lax.fori_loop(0, count, step, 0)

    def straight(batch):
        return half // 2 if batch is batches[-1] else 0

    def cells_of(y, batch, depth):
        _, low_group, high_group = batch
        return pl.ds(pl.multiple_of(y * depth + low_group * tall, tall), (high_group - low_group) * tall)

    def seat_of(slab, batch):
        m, low_group, high_group = batch
        line = lax.rem(slab + m // chunks, n) * slots + (low_group + 1) % slots
        return pl.ds(pl.multiple_of(line * tall, tall), (high_group - low_group) * tall)

    def block_of(j, slab):
        return pl.ds(pl.multiple_of(lax.rem(slab + j // chunks, n) * share, share), share)

    def extent_of(y, j):
        return pl.ds(pl.multiple_of(y * wide + j * share, tall), share)

    def cell_row(x, h):
        return (x // GROUP * halves + h) * GROUP + lax.rem(x, GROUP)

    def forward_copy(batch, owner, slab, first):
        m = batch[0]
        return pltpu.make_async_remote_copy(
            src_ref=current.at[cells_of(owner, batch, deep)],
            dst_ref=gathered.at[m % chunks, seat_of(slab, batch)],
            send_sem=send_sem.at[m],
            recv_sem=recv_sem.at[m],
            device_id=owner_device(owner, first),
            device_id_type=MESH,
        )

    def pass_copy(batch, k):
        m = batch[0]
        return pltpu.make_async_remote_copy(
            src_ref=current.at[cells_of((1 - gx) * half + k, batch, deep)],
            dst_ref=passing.at[cells_of(k, batch, deep)],
            send_sem=pass_send.at[m],
            recv_sem=pass_recv.at[m],
            device_id={"groups": 1 - gx, "gy": gy},
            device_id_type=MESH,
        )

    def pass_on_copy(batch, k):
        m = batch[0]
        return pltpu.make_async_remote_copy(
            src_ref=passing.at[cells_of(k, batch, deep)],
            dst_ref=gathered.at[m % chunks, seat_of(gy, batch)],
            send_sem=pass_on.at[m],
            recv_sem=recv_sem.at[m],
            device_id={"groups": gx, "gy": (1 - gx) * half + k},
            device_id_type=MESH,
        )

    def back_copy(j, slab):
        return pltpu.make_async_remote_copy(
            src_ref=back.at[j % chunks, block_of(j, slab)],
            dst_ref=target.at[extent_of(who, j)],
            send_sem=back_send.at[j],
            recv_sem=back_recv.at[j],
            device_id=slab_device(slab),
            device_id_type=MESH,
        )

    def home_copy(first, last):
        span = pl.ds(first, last - first)
        return pltpu.make_async_remote_copy(
            src_ref=result.at[span],
            dst_ref=out_ref.at[span],
            send_sem=home_send,
            recv_sem=home_recv,
            device_id={"groups": high, "gy": me},
            device_id_type=MESH,
        )

    def own_copy(first, last):
        span = pl.ds(first, last - first)
        return pltpu.make_async_copy(result.at[span], out_ref.at[span], own_sem)

    if cross:
        home = jnp.logical_and(gx == high, gy == me)
        away = jnp.logical_not(home)
    else:
        home, away = near, far

    def deliver(first, last):
        if cross:

            @pl.when(away)
            def _():
                home_copy(first, last).start()

        @pl.when(home)
        def _():
            own_copy(first, last).start()

    def delivered():
        if cross:

            @pl.when(away)
            def _():
                home_copy(0, rows).wait_send()
                home_copy(0, rows).wait_recv()

        @pl.when(home)
        def _():
            own_copy(0, rows).wait()

    def bulk(ref, lines, send, recv):
        span = ref.at[pl.ds(0, lines)]
        return pltpu.make_async_remote_copy(
            src_ref=span,
            dst_ref=span,
            send_sem=send,
            recv_sem=recv,
            device_id=owner_device(who, False),
            device_id_type=MESH,
        )

    def lines_of(batch):
        return (batch[2] - batch[1]) * tall

    def forward_bulk(batch, count):
        m = batch[0]
        return bulk(current, count * lines_of(batch), send_sem.at[m], recv_sem.at[m])

    def pass_bulk(batch):
        m = batch[0]
        count = half - straight(batch)
        return bulk(passing, count * lines_of(batch), pass_send.at[m], pass_recv.at[m])

    def pass_on_bulk(batch):
        m = batch[0]
        count = half - straight(batch)
        return bulk(passing, count * lines_of(batch), pass_on.at[m], pass_recv.at[m])

    def back_bulk(j):
        return bulk(target, (n - 1) * share, back_send.at[j], back_recv.at[j])

    def keep_own(batch, slab):
        gathered[batch[0] % chunks, seat_of(slab, batch)] = current[cells_of(who, batch, deep)]

    def send_direct(batch):
        if cross:

            @pl.when(far)
            def _():
                every_half(lambda k: forward_copy(batch, gx * half + k, gy, True).start())
                if straight(batch):
                    every_half(
                        lambda k: forward_copy(batch, (1 - gx) * half + k, gy, True).start(),
                        0,
                        straight(batch),
                    )

        @pl.when(near)
        def _():
            every_other(who, lambda owner: forward_copy(batch, owner, gy, True).start())
            keep_own(batch, gy)

    def send_aside(batch):
        if cross:

            @pl.when(far)
            def _():
                every_half(lambda k: pass_copy(batch, k).start(), straight(batch), half)

    def pass_along(batch):
        if cross:

            @pl.when(near)
            def _():
                pass_bulk(batch).wait_recv()
                every_half(lambda k: pass_on_copy(batch, k).start(), straight(batch), half)

    def first_arrived(batch):
        @pl.when(near)
        def _():
            forward_bulk(batch, n - 1).wait_recv()

        if cross:

            @pl.when(far)
            def _():
                forward_bulk(batch, n).wait_recv()

    def first_sent(batch):
        @pl.when(near)
        def _():
            forward_bulk(batch, n - 1).wait_send()
            if cross:
                pass_on_bulk(batch).wait_send()

        if cross:

            @pl.when(far)
            def _():
                forward_bulk(batch, half + straight(batch)).wait_send()
                pass_bulk(batch).wait_send()

    def send_forward(batch):
        every_other(who, lambda owner: forward_copy(batch, owner, me, False).start())
        keep_own(batch, me)

    def stage(y, carry):
        stride = ny * halves
        for h in range(halves):
            first = (y // GROUP * halves + h) * GROUP + y % GROUP
            lines = cells_ref[pl.ds(first, rows, stride=stride), :]
            for g in range(groups):
                at = y * deep + g * tall + h * GROUP
                current[pl.ds(pl.multiple_of(at, GROUP), GROUP), :] = lines[
                    g * GROUP : (g + 1) * GROUP, :
                ]
        return carry

    def make_tables():
        def body(m, carry):
            lines = jnp.concatenate(
                [
                    cos_ref[pl.ds(k, 1), :] * cas_ref[...] + sin_ref[pl.ds(k, 1), :] * case_ref[...]
                    for k in (2 * m, 2 * m + 1)
                ],
                axis=0,
            )
            at = pl.ds(pl.multiple_of(m * 2 * GROUP, 2 * GROUP), 2 * GROUP)
            x_high[at, :], x_low[at, :] = split(lines)
            return carry

        lax.fori_loop(0, nx // (2 * GROUP), body, 0)

    def make_filter():
        columns, lines = tilt_ref.shape
        code[...] = jnp.zeros_like(code)
        code[0:columns, 0:lines] = jnp.where(wedge_ref[...] == 0, 0, tilt_ref[...] + 1).astype(f32)
        width, depth = code.shape
        kz = lax.broadcasted_iota(jnp.int32, (nz, width), 0)
        pick_z = jnp.where(
            lax.broadcasted_iota(jnp.int32, (nz, width), 1) == jnp.minimum(kz, nz - kz), 1.0, 0.0
        ).astype(bf16)
        spread = jnp.dot(pick_z, code[...].astype(bf16), preferred_element_type=f32).astype(bf16)

        def body(b, carry):
            line = b * block + lax.broadcasted_iota(jnp.int32, (block, depth), 0)
            c = line // span_rows
            slot = line % part // GROUP
            place = line % span_rows // part * groups + c * slots + slot - 1
            kx = (place * GROUP + line % GROUP + nx) % nx
            column = lax.broadcasted_iota(jnp.int32, (block, depth), 1)
            pick_x = jnp.where(column == jnp.minimum(kx, nx - kx), 1.0, 0.0).astype(bf16)
            which = lax.dot_general(
                pick_x, spread, (((1,), (1,)), ((), ())), preferred_element_type=f32
            )
            response = jnp.zeros_like(which)
            for level in range(table_ref.shape[0]):
                response = jnp.where(which == level + 1.0, table_ref[level], response)
            prior = 1.0 / (response * response + 1.0)
            at = pl.ds(pl.multiple_of(b * block, block), block)
            prior_gain[at, :] = prior
            data_term[at, :] = response * prior
            return carry

        lax.fori_loop(0, row_blocks, body, 0)

    def filtered(outer):
        for c in turns:
            for batch in batches:
                if batch[0] % chunks == c and outer == 0:
                    first_arrived(batch)
                elif batch[0] % chunks == c:
                    forward_bulk(batch, n - 1).wait_recv()
            pieces = gathered[c].reshape(n * slots, halves, GROUP, LANES)
            lines = [pieces[:, h].reshape(span_rows, LANES) for h in range(halves)]
            high, low = split(jnp.concatenate(lines, axis=1))
            high, low = split(dot3(high, low, zh_ref[...], zl_ref[...]))

            def body(b, carry):
                at = pl.ds(pl.multiple_of(b * block, block), block)
                span = pl.ds(c * span_rows, span_rows)
                spectrum = dot3(x_high[at, span], x_low[at, span], high, low)
                if c != turns[0]:
                    spectrum = total[at, :] + spectrum
                if c != turns[-1]:
                    total[at, :] = spectrum
                    return carry
                if outer == 0:
                    spectrum = spectrum * gain
                    data_term[at, :] = data_term[at, :] * spectrum
                a_high, a_low = split(data_term[at, :] + prior_gain[at, :] * spectrum)
                m_high[at, :], m_low[at, :] = split(dot3(a_high, a_low, zh_ref[...], zl_ref[...]))
                return carry

            lax.fori_loop(0, row_blocks, body, 0, unroll=True)

    def send_back(c):
        step = math.gcd(span_rows, 256)

        def body(b, carry):
            line = pl.ds(pl.multiple_of(c * span_rows + b * step, step), step)
            lines = dot3(x_high[line, :], x_low[line, :], m_high[...], m_low[...])
            pieces = [
                lines[:, h * LANES : (h + 1) * LANES].reshape(step // GROUP, 1, GROUP, LANES)
                for h in range(halves)
            ]
            count = step * halves
            at = pl.ds(pl.multiple_of(b * count, count), count)
            back[c, at] = jnp.concatenate(pieces, axis=1).reshape(count, LANES)
            return carry

        lax.fori_loop(0, span_rows // step, body, 0)
        start_back(c)

    def start_back(j):
        every_other(me, lambda slab: back_copy(j, slab).start())
        target[extent_of(who, j)] = back[j % chunks, block_of(j, me)]

    def sum_y(value):
        pieces = [value[y : y + GROUP, :] for y in range(0, ny, GROUP)]
        nothing = jnp.zeros_like(pieces[0])
        line = lax.broadcasted_iota(jnp.int32, pieces[0].shape, 0)
        ups = [nothing] + [pltpu.roll(piece, 1, 0) for piece in pieces]
        downs = [pltpu.roll(piece, GROUP - 1, 0) for piece in pieces] + [nothing]
        return jnp.concatenate(
            [
                jnp.where(line == 0, ups[y], ups[y + 1])
                + jnp.where(line == GROUP - 1, downs[y + 1], downs[y])
                for y in range(len(pieces))
            ],
            axis=0,
        )

    def sum_z(value):
        pieces = [value[:, z : z + LANES] for z in range(0, nz, LANES)]
        nothing = jnp.zeros_like(pieces[0])
        lane = lax.broadcasted_iota(jnp.int32, pieces[0].shape, 1)
        ups = [nothing] + [pltpu.roll(piece, 1, 1) for piece in pieces]
        downs = [pltpu.roll(piece, LANES - 1, 1) for piece in pieces] + [nothing]
        return jnp.concatenate(
            [
                jnp.where(lane == 0, ups[z], ups[z + 1])
                + jnp.where(lane == LANES - 1, downs[z + 1], downs[z])
                for z in range(len(pieces))
            ],
            axis=1,
        )

    def collect(j):
        def gather(e):
            def body(r, carry):
                for h in range(halves):
                    for y in range(0, ny, GROUP):
                        goal[
                            PAD + (e - 1) * GROUP + r,
                            y : y + GROUP,
                            h * LANES : (h + 1) * LANES,
                        ] = target[pl.ds(y * wide + e * tall + h * GROUP + r, GROUP, stride=wide), :]
                return carry

            lax.fori_loop(0, GROUP, body, 0)

        for e in range(j * slots, (j + 1) * slots):
            if e == 0:
                pl.when(me > 0)(functools.partial(gather, e))
            elif e == groups + 1:
                pl.when(me < n - 1)(functools.partial(gather, e))
            else:
                gather(e)

    def rise_load(origin, x, fresh):
        here, before, after = origin[x], origin[x - 1], origin[x + 1]
        olds = None if fresh else [dual[x] for dual in duals]
        return here, before, after, olds

    def rise(loaded, keep):
        here, before, after, olds = loaded
        twice = here + here
        raised = [before + after - twice, sum_y(here) - twice, sum_z(here) - twice]
        if olds is not None:
            raised = [old + bend for old, bend in zip(olds, raised)]
        norm = raised[0] * raised[0] + raised[1] * raised[1] + raised[2] * raised[2]
        shrink = lax.rsqrt(jnp.maximum(1.0 / relax**2, norm * (1.0 / (bound_dual * relax) ** 2)))
        if keep is not None:
            shrink = shrink * keep
        return [part_of * shrink for part_of in raised]

    def fall_load(x):
        dual_x, dual_y, dual_z = duals
        return (
            dual_x[x], dual_x[x - 1], dual_x[x + 1],
            dual_y[x], dual_z[x], goal[x],
        )

    def fall(loaded):
        in_x, before, after, in_y, in_z, _ = loaded
        middle = in_x + in_y + in_z
        return (before + after + sum_y(in_y) + sum_z(in_z) - (middle + middle)) * (
            step_primal * step_dual / (1.0 + step_primal)
        )

    def sweep_rows(outer, start, stop):
        def run(first, last):
            masked = first < REACH or last > rows
            ends = first >= REACH and last <= rows + REACH

            def keep(x):
                if not masked:
                    return None
                whole = me * rows + PAD + x
                return jnp.where(jnp.logical_and(whole >= 2 * PAD, whole < nx + 2 * PAD), 1.0, 0.0)

            def body(x, carry):
                low = rise_load(goal, x, outer == 0)
                mid = fall_load(x - 2)
                high = rise_load(lead, x - 4, False)
                if ends:
                    top = fall_load(x - 6)
                    old = field[x - 6]
                fresh = rise(low, keep(x))
                updated = mid[-1] - fall(mid)
                if masked:
                    updated = updated * keep(x - 2)
                again = rise(high, keep(x - 4))
                if ends:
                    final = (
                        old * (1.0 / (1.0 + step_primal))
                        + top[-1] * (step_primal / (1.0 + step_primal))
                        - fall(top)
                    )
                for dual, value in zip(duals, fresh):
                    dual[x] = value
                lead[x - 2] = updated + updated - mid[-1]
                field[x - 2] = updated
                for dual, value in zip(duals, again):
                    dual[x - 4] = value
                if ends and outer == OUTER - 1:
                    result[x - PAD - 6] = final * (1.0 / gain)
                elif ends:
                    for h in range(halves):
                        at = cell_row(x - PAD - 6, h)
                        for y in range(0, ny, GROUP):
                            current[pl.ds(at + y * deep, GROUP, stride=deep), :] = final[
                                y : y + GROUP, h * LANES : (h + 1) * LANES
                            ]
                return carry

            lax.fori_loop(first + PAD, last + PAD, body, 0)

        marks = [start] + [x for x in (REACH, rows, rows + REACH) if start < x < stop] + [stop]
        for first, last in zip(marks[:-1], marks[1:]):
            run(first, last)

    homes = [(x, x + GROUP) for x in range(0, rows, GROUP)]

    def denoise(outer):
        stop = rows + REACH + (1 if outer < OUTER - 1 else 0)
        done = -5 if outer < OUTER - 1 else -3
        if outer < OUTER - 1:
            ready = {batch[2] * GROUP + REACH: batch for batch in batches}
        else:
            ready = {last + REACH: (first, last) for first, last in homes}
        for j in range(extents):
            back_bulk(j).wait_recv()
            collect(j)
            limit = stop if j == extents - 1 else ((j + 1) * slots - 1) * GROUP - 1
            for x in sorted(ready):
                if done < x <= limit:
                    sweep_rows(outer, done, x)
                    if outer < OUTER - 1:
                        send_forward(ready[x])
                    else:
                        deliver(*ready[x])
                    done = x
            if done < limit:
                sweep_rows(outer, done, limit)
                done = limit

    turns = list(range(1, chunks)) + [0]
    lax.fori_loop(0, ny, stage, 0)
    pl.semaphore_wait(barrier, greeted - 1)
    for batch in batches[:2]:
        send_aside(batch)
    for i, batch in enumerate(first_turn):
        send_direct(batch)
        for later in batches[i + 2 : i + 3]:
            send_aside(later)

    @pl.when(me == 0)
    def _():
        goal[PAD - GROUP : PAD] = jnp.zeros((GROUP, ny, nz), f32)

    @pl.when(me == n - 1)
    def _():
        goal[PAD + rows : PAD + rows + GROUP] = jnp.zeros((GROUP, ny, nz), f32)

    make_tables()
    pass_along(batches[0])
    make_filter()
    for batch in batches[1:]:
        pass_along(batch)
    for outer in range(OUTER):
        filtered(outer)
        for c in range(chunks):
            send_back(c)
        for j in range(chunks, extents):
            start_back(j)
        for batch in batches:
            if outer == 0:
                first_sent(batch)
            else:
                forward_bulk(batch, n - 1).wait_send()
        denoise(outer)
        for j in range(extents):
            back_bulk(j).wait_send()
    delivered()


def constants(n, rows, slots, nz):
    nx = n * rows
    groups = rows // GROUP
    place = np.array(
        [
            ((d * groups + c + slot - 1) * GROUP + r) % nx
            for c in range(0, groups, slots)
            for d in range(n)
            for slot in range(slots)
            for r in range(GROUP)
        ]
    )
    turn = 2.0 * math.pi / nx
    coarse = (place[::GROUP, None] * place[None, :] % nx) * turn
    fine = (np.arange(GROUP)[:, None] * place[None, :] % nx) * turn
    norm = 1.0 / math.sqrt(nx)
    tables = (
        np.cos(coarse),
        np.sin(coarse),
        (np.cos(fine) + np.sin(fine)) * norm,
        (np.cos(fine) - np.sin(fine)) * norm,
    )
    k = np.arange(nz)
    angle = (k[:, None] * k[None, :] % nz) * (2.0 * math.pi / nz)
    cas_z = ((np.cos(angle) + np.sin(angle)) / math.sqrt(nz)).astype(np.float32)
    z_high = cas_z.astype(bf16)
    z_low = (cas_z - z_high.astype(np.float32)).astype(bf16)
    return [jnp.asarray(t, f32) for t in tables] + [jnp.asarray(z_high), jnp.asarray(z_low)]


def local(n, cross, observed, tf_table, tilt_index, wedge):
    rows, ny, nz = observed.shape
    nx = n * rows
    groups = rows // GROUP
    slots = 2 if groups % 2 == 0 else 1
    chunks = groups // slots
    extents = (groups + 2) // slots
    lines, columns = tilt_index.shape
    depth, width = -(-lines // 128) * 128, -(-columns // 128) * 128
    tables = constants(n, rows, slots, nz)
    tiles = observed.reshape(rows, ny // GROUP, GROUP, nz // LANES, LANES)
    tiles = tiles.transpose(0, 1, 3, 2, 4).reshape(-1, LANES)
    vmem = pl.BlockSpec(memory_space=pltpu.VMEM)
    smem = pl.BlockSpec(memory_space=pltpu.SMEM)
    grid_rows = pltpu.VMEM((rows + 2 * PAD, ny, nz), f32)
    plane = pltpu.VMEM((nx, nz), f32)
    blocks = pltpu.VMEM((chunks, n * slots * GROUP * nz // LANES, LANES), f32)
    cells = pltpu.VMEM((rows * ny * nz // LANES, LANES), f32)
    semaphores = pltpu.SemaphoreType.DMA((extents,))
    landing = pltpu.VMEM((ny * (groups + 2) * GROUP * nz // LANES, LANES), f32)
    result = pl.pallas_call(
        functools.partial(kernel, n, rows, slots, cross),
        out_shape=jax.ShapeDtypeStruct((rows, ny, nz), f32),
        in_specs=[vmem, smem] + [vmem] * 8,
        out_specs=pl.BlockSpec(memory_space=pl.ANY),
        scratch_shapes=[
            blocks,
            plane,
            plane,
            plane,
            pltpu.VMEM((nx, nx), bf16),
            pltpu.VMEM((nx, nx), bf16),
            pltpu.VMEM((nx, nz), bf16),
            pltpu.VMEM((nx, nz), bf16),
            blocks,
            landing,
            grid_rows,
            grid_rows,
            grid_rows,
            [grid_rows] * 3,
            cells,
            pltpu.VMEM((width, depth), f32),
            pltpu.VMEM((rows * ny * nz // LANES // 2, LANES), f32),
            pltpu.VMEM((rows, ny, nz), f32),
            semaphores,
            semaphores,
            semaphores,
            semaphores,
            semaphores,
            semaphores,
            semaphores,
            pltpu.SemaphoreType.DMA(()),
            pltpu.SemaphoreType.DMA(()),
            pltpu.SemaphoreType.DMA(()),
        ],
        compiler_params=pltpu.CompilerParams(
            collective_id=0, has_side_effects=True, vmem_limit_bytes=60 * 1024 * 1024
        ),
    )(tiles, tf_table, tilt_index.T, wedge.T, *tables)
    return result


def solution(mesh):
    in_specs = (P(("groups", "gy"), None, None), P(), P(), P())
    out_specs = P(("groups", "gy"), None, None)
    n = mesh.shape["gy"]
    cross = mesh.shape["groups"] == 2 and n % 4 == 0
    body = functools.partial(local, n, cross)
    return jax.shard_map(body, mesh=mesh, in_specs=in_specs, out_specs=out_specs, check_vma=False)
```

```python
import functools
import math

import jax
import jax.numpy as jnp
import numpy as np
from jax import lax
from jax.experimental import pallas as pl
from jax.experimental.pallas import tpu as pltpu
from jax.sharding import PartitionSpec as P

OUTER = 2
PASSES = 2
GROUP = 8
LANES = 128
REACH = 6
PAD = 12

step_dual = 0.14
step_primal = 0.14
huber_eps = 0.05
bound_dual = 0.5
relax = 1.0 / (1.0 + step_dual * huber_eps / bound_dual)
gain = step_dual * relax
MESH = pl.DeviceIdType.MESH
f32 = jnp.float32
bf16 = jnp.bfloat16


def split(value):
    high = value.astype(bf16)
    low = (value - high.astype(f32)).astype(bf16)
    return high, low


def dot3(a_high, a_low, b_high, b_low):
    dot = functools.partial(jnp.dot, preferred_element_type=f32)
    return dot(a_high, b_high) + (dot(a_high, b_low) + dot(a_low, b_high))


def kernel(
    n, rows, slots, cross,
    cells_in, table_ref, tilt_in, wedge_in, cos_in, sin_in, cas_in, case_in, zh_in, zl_in,
    out_ref,
    cells_ref, tilt_ref, wedge_ref, cos_ref, sin_ref, cas_ref, case_ref, zh_ref, zl_ref, load_sem,
    gathered, total, data_term, prior_gain, x_high, x_low, m_high, m_low, back,
    target, goal, field, lead, duals, current, code, passing, result,
    send_sem, recv_sem, back_send, back_recv,
    pass_send, pass_recv, pass_on, home_send, home_recv, own_sem,
):
    gx, gy = lax.axis_index("groups"), lax.axis_index("gy")
    half = n // 2
    high, low = gy // half, gy % half
    if cross:
        near = gx == high
        who = gx * half + low
        me = low % 2 * half + low // 2 * 2 + gx
    else:
        near = gx == gx
        who = gy
        me = gy
    far = jnp.logical_not(near)

    def owner_device(owner, first):
        if not cross:
            return {"gy": owner}
        block = gx if first else high
        return {"groups": owner // half, "gy": block * half + owner % half}

    def slab_device(slab):
        if not cross:
            return {"gy": slab}
        return {"groups": slab % 2, "gy": high * half + slab % half // 2 * 2 + slab // half}

    groups = rows // GROUP
    chunks = groups // slots
    extents = (groups + 2) // slots
    part = slots * GROUP
    ny, nz = out_ref.shape[1], out_ref.shape[2]
    halves = nz // LANES
    tall = GROUP * halves
    deep = groups * tall
    wide = (groups + 2) * tall
    share = slots * tall
    batches = [
        (m, max(m * slots - 1, 0), min((m + 1) * slots - 1, groups))
        for m in range(1 // slots, groups // slots + 1)
    ]
    aside = batches[:-1]
    first_turn = [batch for batch in batches if batch[0] % chunks > 0]
    first_turn += [batch for batch in batches if batch[0] % chunks == 0]
    nx = n * rows
    span_rows = n * part
    block = math.gcd(nx, 256)
    row_blocks = nx // block

    barrier = pltpu.get_barrier_semaphore()

    def greet(o, carry):
        if cross:
            other = lax.rem(gx * n + gy + o, 2 * n)
            device = {"groups": other // n, "gy": other % n}
        else:
            device = {"gy": lax.rem(gy + o, n)}
        pl.semaphore_signal(barrier, inc=1, device_id=device, device_id_type=MESH)
        return carry

    greeted = 2 * n if cross else n
    loads = [
        pltpu.make_async_copy(source, place, load_sem.at[i])
        for i, (source, place) in enumerate(
            [
                (cells_in, cells_ref),
                (cos_in, cos_ref),
                (sin_in, sin_ref),
                (cas_in, cas_ref),
                (case_in, case_ref),
                (tilt_in, tilt_ref),
                (wedge_in, wedge_ref),
                (zh_in, zh_ref),
                (zl_in, zl_ref),
            ]
        )
    ]
    for load in loads:
        load.start()
    lax.fori_loop(1, greeted, greet, 0)

    def every_other(mine, action):
        def step(o, carry):
            action(lax.rem(mine + o, n))
            return carry

        lax.fori_loop(1, n, step, 0)

    def every_half(side, action):
        count = half // 2

        def step(o, carry):
            action(lax.rem(low // 2 + o, count) * 2 + side)
            return carry

        lax.fori_loop(0, count, step, 0)

    def cells_of(y, batch, depth):
        _, low_group, high_group = batch
        return pl.ds(pl.multiple_of(y * depth + low_group * tall, tall), (high_group - low_group) * tall)

    def seat_of(slab, batch):
        m, low_group, high_group = batch
        line = lax.rem(slab + m // chunks, n) * slots + (low_group + 1) % slots
        return pl.ds(pl.multiple_of(line * tall, tall), (high_group - low_group) * tall)

    def block_of(j, slab):
        return pl.ds(pl.multiple_of(lax.rem(slab + j // chunks, n) * share, share), share)

    def extent_of(y, j):
        return pl.ds(pl.multiple_of(y * wide + j * share, tall), share)

    def cell_row(x, h):
        return (x // GROUP * halves + h) * GROUP + lax.rem(x, GROUP)

    def forward_copy(batch, owner, slab, first):
        m = batch[0]
        return pltpu.make_async_remote_copy(
            src_ref=current.at[cells_of(owner, batch, deep)],
            dst_ref=gathered.at[m % chunks, seat_of(slab, batch)],
            send_sem=send_sem.at[m],
            recv_sem=recv_sem.at[m],
            device_id=owner_device(owner, first),
            device_id_type=MESH,
        )

    def pass_copy(batch, side, k):
        m = batch[0]
        return pltpu.make_async_remote_copy(
            src_ref=current.at[cells_of((1 - gx) * half + k, batch, deep)],
            dst_ref=passing.at[cells_of(k, batch, deep)],
            send_sem=pass_send.at[side, m],
            recv_sem=pass_recv.at[side, m],
            device_id={"groups": 1 - gx, "gy": gy},
            device_id_type=MESH,
        )

    def pass_on_copy(batch, k):
        m = batch[0]
        return pltpu.make_async_remote_copy(
            src_ref=passing.at[cells_of(k, batch, deep)],
            dst_ref=gathered.at[m % chunks, seat_of(gy, batch)],
            send_sem=pass_on.at[m],
            recv_sem=recv_sem.at[m],
            device_id={"groups": gx, "gy": (1 - gx) * half + k},
            device_id_type=MESH,
        )

    def back_copy(j, slab):
        return pltpu.make_async_remote_copy(
            src_ref=back.at[j % chunks, block_of(j, slab)],
            dst_ref=target.at[extent_of(who, j)],
            send_sem=back_send.at[j],
            recv_sem=back_recv.at[j],
            device_id=slab_device(slab),
            device_id_type=MESH,
        )

    def home_copy(first, last):
        span = pl.ds(first, last - first)
        return pltpu.make_async_remote_copy(
            src_ref=result.at[span],
            dst_ref=out_ref.at[span],
            send_sem=home_send,
            recv_sem=home_recv,
            device_id={"groups": high, "gy": me},
            device_id_type=MESH,
        )

    def own_copy(first, last):
        span = pl.ds(first, last - first)
        return pltpu.make_async_copy(result.at[span], out_ref.at[span], own_sem)

    if cross:
        home = jnp.logical_and(gx == high, gy == me)
        away = jnp.logical_not(home)
    else:
        home, away = near, far

    def deliver(first, last):
        if cross:

            @pl.when(away)
            def _():
                home_copy(first, last).start()

        @pl.when(home)
        def _():
            own_copy(first, last).start()

    def delivered():
        if cross:

            @pl.when(away)
            def _():
                home_copy(0, rows).wait_send()
                home_copy(0, rows).wait_recv()

        @pl.when(home)
        def _():
            own_copy(0, rows).wait()

    def bulk(ref, lines, send, recv):
        span = ref.at[pl.ds(0, lines)]
        return pltpu.make_async_remote_copy(
            src_ref=span,
            dst_ref=span,
            send_sem=send,
            recv_sem=recv,
            device_id=owner_device(who, False),
            device_id_type=MESH,
        )

    def lines_of(batch):
        return (batch[2] - batch[1]) * tall

    def forward_bulk(batch, count):
        m = batch[0]
        return bulk(current, count * lines_of(batch), send_sem.at[m], recv_sem.at[m])

    def pass_bulk(batch, side):
        lines = half // 2 * lines_of(batch)
        return bulk(passing, lines, pass_send.at[side, batch[0]], pass_recv.at[side, batch[0]])

    def pass_on_bulk(batch):
        m = batch[0]
        return bulk(passing, half * lines_of(batch), pass_on.at[m], pass_recv.at[0, m])

    def back_bulk(j):
        return bulk(target, (n - 1) * share, back_send.at[j], back_recv.at[j])

    def keep_own(batch, slab):
        gathered[batch[0] % chunks, seat_of(slab, batch)] = current[cells_of(who, batch, deep)]

    def send_direct(batch, side):
        if not cross:
            if side == 0:
                every_other(who, lambda owner: forward_copy(batch, owner, gy, True).start())
                keep_own(batch, gy)
            return

        @pl.when(far)
        def _():
            every_half(side, lambda k: forward_copy(batch, gx * half + k, gy, True).start())
            if batch not in aside:
                every_half(
                    side, lambda k: forward_copy(batch, (1 - gx) * half + k, gy, True).start()
                )

        @pl.when(near)
        def _():
            every_half(side, lambda k: forward_copy(batch, (1 - gx) * half + k, gy, True).start())

            def own_row(k):
                @pl.when(k != low)
                def _():
                    forward_copy(batch, gx * half + k, gy, True).start()

            every_half(side, own_row)
            if side == 0:
                keep_own(batch, gy)

    def send_aside(batch, side):
        if cross:

            @pl.when(far)
            def _():
                every_half(side, lambda k: pass_copy(batch, side, k).start())

    def pass_along(batch, side):
        if cross:

            @pl.when(near)
            def _():
                pass_bulk(batch, side).wait_recv()
                every_half(side, lambda k: pass_on_copy(batch, k).start())

    def first_arrived(batch):
        @pl.when(near)
        def _():
            forward_bulk(batch, n - 1).wait_recv()

        if cross:

            @pl.when(far)
            def _():
                forward_bulk(batch, n).wait_recv()

    def first_sent(batch):
        relayed = cross and batch in aside

        @pl.when(near)
        def _():
            forward_bulk(batch, n - 1).wait_send()
            if relayed:
                pass_on_bulk(batch).wait_send()

        if cross:

            @pl.when(far)
            def _():
                forward_bulk(batch, half if relayed else n).wait_send()
                if relayed:
                    pass_bulk(batch, 0).wait_send()
                    pass_bulk(batch, 1).wait_send()

    def send_forward(batch):
        every_other(who, lambda owner: forward_copy(batch, owner, me, False).start())
        keep_own(batch, me)

    def stage(y, carry):
        stride = ny * halves
        for h in range(halves):
            first = (y // GROUP * halves + h) * GROUP + y % GROUP
            lines = cells_ref[pl.ds(first, rows, stride=stride), :]
            for g in range(groups):
                at = y * deep + g * tall + h * GROUP
                current[pl.ds(pl.multiple_of(at, GROUP), GROUP), :] = lines[
                    g * GROUP : (g + 1) * GROUP, :
                ]
        return carry

    def make_tables():
        def body(m, carry):
            lines = jnp.concatenate(
                [
                    cos_ref[pl.ds(k, 1), :] * cas_ref[...] + sin_ref[pl.ds(k, 1), :] * case_ref[...]
                    for k in (2 * m, 2 * m + 1)
                ],
                axis=0,
            )
            at = pl.ds(pl.multiple_of(m * 2 * GROUP, 2 * GROUP), 2 * GROUP)
            x_high[at, :], x_low[at, :] = split(lines)
            return carry

        lax.fori_loop(0, nx // (2 * GROUP), body, 0)

    def make_filter():
        columns, lines = tilt_ref.shape
        code[...] = jnp.zeros_like(code)
        code[0:columns, 0:lines] = jnp.where(wedge_ref[...] == 0, 0, tilt_ref[...] + 1).astype(f32)
        width, depth = code.shape
        kz = lax.broadcasted_iota(jnp.int32, (nz, width), 0)
        pick_z = jnp.where(
            lax.broadcasted_iota(jnp.int32, (nz, width), 1) == jnp.minimum(kz, nz - kz), 1.0, 0.0
        ).astype(bf16)
        spread = jnp.dot(pick_z, code[...].astype(bf16), preferred_element_type=f32).astype(bf16)

        def body(b, carry):
            line = b * block + lax.broadcasted_iota(jnp.int32, (block, depth), 0)
            c = line // span_rows
            slot = line % part // GROUP
            place = line % span_rows // part * groups + c * slots + slot - 1
            kx = (place * GROUP + line % GROUP + nx) % nx
            column = lax.broadcasted_iota(jnp.int32, (block, depth), 1)
            pick_x = jnp.where(column == jnp.minimum(kx, nx - kx), 1.0, 0.0).astype(bf16)
            which = lax.dot_general(
                pick_x, spread, (((1,), (1,)), ((), ())), preferred_element_type=f32
            )
            response = jnp.zeros_like(which)
            for level in range(table_ref.shape[0]):
                response = jnp.where(which == level + 1.0, table_ref[level], response)
            prior = 1.0 / (response * response + 1.0)
            at = pl.ds(pl.multiple_of(b * block, block), block)
            prior_gain[at, :] = prior
            data_term[at, :] = response * prior
            return carry

        lax.fori_loop(0, row_blocks, body, 0)

    def filtered(outer):
        for c in turns:
            for batch in batches:
                if batch[0] % chunks == c and outer == 0:
                    first_arrived(batch)
                elif batch[0] % chunks == c:
                    forward_bulk(batch, n - 1).wait_recv()
            pieces = gathered[c].reshape(n * slots, halves, GROUP, LANES)
            lines = [pieces[:, h].reshape(span_rows, LANES) for h in range(halves)]
            high, low = split(jnp.concatenate(lines, axis=1))
            high, low = split(dot3(high, low, zh_ref[...], zl_ref[...]))

            def body(b, carry):
                at = pl.ds(pl.multiple_of(b * block, block), block)
                span = pl.ds(c * span_rows, span_rows)
                spectrum = dot3(x_high[at, span], x_low[at, span], high, low)
                if c != turns[0]:
                    spectrum = total[at, :] + spectrum
                if c != turns[-1]:
                    total[at, :] = spectrum
                    return carry
                if outer == 0:
                    spectrum = spectrum * gain
                    data_term[at, :] = data_term[at, :] * spectrum
                a_high, a_low = split(data_term[at, :] + prior_gain[at, :] * spectrum)
                m_high[at, :], m_low[at, :] = split(dot3(a_high, a_low, zh_ref[...], zl_ref[...]))
                return carry

            lax.fori_loop(0, row_blocks, body, 0, unroll=True)

    def send_back(c):
        step = math.gcd(span_rows, 256)

        def body(b, carry):
            line = pl.ds(pl.multiple_of(c * span_rows + b * step, step), step)
            lines = dot3(x_high[line, :], x_low[line, :], m_high[...], m_low[...])
            pieces = [
                lines[:, h * LANES : (h + 1) * LANES].reshape(step // GROUP, 1, GROUP, LANES)
                for h in range(halves)
            ]
            count = step * halves
            at = pl.ds(pl.multiple_of(b * count, count), count)
            back[c, at] = jnp.concatenate(pieces, axis=1).reshape(count, LANES)
            return carry

        lax.fori_loop(0, span_rows // step, body, 0)
        start_back(c)

    def start_back(j):
        every_other(me, lambda slab: back_copy(j, slab).start())
        target[extent_of(who, j)] = back[j % chunks, block_of(j, me)]

    def sum_y(value):
        pieces = [value[y : y + GROUP, :] for y in range(0, ny, GROUP)]
        nothing = jnp.zeros_like(pieces[0])
        line = lax.broadcasted_iota(jnp.int32, pieces[0].shape, 0)
        ups = [nothing] + [pltpu.roll(piece, 1, 0) for piece in pieces]
        downs = [pltpu.roll(piece, GROUP - 1, 0) for piece in pieces] + [nothing]
        return jnp.concatenate(
            [
                jnp.where(line == 0, ups[y], ups[y + 1])
                + jnp.where(line == GROUP - 1, downs[y + 1], downs[y])
                for y in range(len(pieces))
            ],
            axis=0,
        )

    def sum_z(value):
        pieces = [value[:, z : z + LANES] for z in range(0, nz, LANES)]
        nothing = jnp.zeros_like(pieces[0])
        lane = lax.broadcasted_iota(jnp.int32, pieces[0].shape, 1)
        ups = [nothing] + [pltpu.roll(piece, 1, 1) for piece in pieces]
        downs = [pltpu.roll(piece, LANES - 1, 1) for piece in pieces] + [nothing]
        return jnp.concatenate(
            [
                jnp.where(lane == 0, ups[z], ups[z + 1])
                + jnp.where(lane == LANES - 1, downs[z + 1], downs[z])
                for z in range(len(pieces))
            ],
            axis=1,
        )

    def collect(j):
        def gather(e):
            def body(r, carry):
                for h in range(halves):
                    for y in range(0, ny, GROUP):
                        goal[
                            PAD + (e - 1) * GROUP + r,
                            y : y + GROUP,
                            h * LANES : (h + 1) * LANES,
                        ] = target[pl.ds(y * wide + e * tall + h * GROUP + r, GROUP, stride=wide), :]
                return carry

            lax.fori_loop(0, GROUP, body, 0)

        for e in range(j * slots, (j + 1) * slots):
            if e == 0:
                pl.when(me > 0)(functools.partial(gather, e))
            elif e == groups + 1:
                pl.when(me < n - 1)(functools.partial(gather, e))
            else:
                gather(e)

    def rise_load(origin, x, fresh):
        here, before, after = origin[x], origin[x - 1], origin[x + 1]
        olds = None if fresh else [dual[x] for dual in duals]
        return here, before, after, olds

    def rise(loaded, keep):
        here, before, after, olds = loaded
        twice = here + here
        raised = [before + after - twice, sum_y(here) - twice, sum_z(here) - twice]
        if olds is not None:
            raised = [old + bend for old, bend in zip(olds, raised)]
        norm = raised[0] * raised[0] + raised[1] * raised[1] + raised[2] * raised[2]
        shrink = lax.rsqrt(jnp.maximum(1.0 / relax**2, norm * (1.0 / (bound_dual * relax) ** 2)))
        if keep is not None:
            shrink = shrink * keep
        return [part_of * shrink for part_of in raised]

    def fall_load(x):
        dual_x, dual_y, dual_z = duals
        return (
            dual_x[x], dual_x[x - 1], dual_x[x + 1],
            dual_y[x], dual_z[x], goal[x],
        )

    def fall(loaded):
        in_x, before, after, in_y, in_z, _ = loaded
        middle = in_x + in_y + in_z
        return (before + after + sum_y(in_y) + sum_z(in_z) - (middle + middle)) * (
            step_primal * step_dual / (1.0 + step_primal)
        )

    def sweep_rows(outer, start, stop):
        def run(first, last):
            masked = first < REACH or last > rows
            ends = first >= REACH and last <= rows + REACH

            def keep(x):
                if not masked:
                    return None
                whole = me * rows + PAD + x
                return jnp.where(jnp.logical_and(whole >= 2 * PAD, whole < nx + 2 * PAD), 1.0, 0.0)

            def body(x, carry):
                low = rise_load(goal, x, outer == 0)
                mid = fall_load(x - 2)
                high = rise_load(lead, x - 4, False)
                if ends:
                    top = fall_load(x - 6)
                    old = field[x - 6]
                fresh = rise(low, keep(x))
                updated = mid[-1] - fall(mid)
                if masked:
                    updated = updated * keep(x - 2)
                again = rise(high, keep(x - 4))
                if ends:
                    final = (
                        old * (1.0 / (1.0 + step_primal))
                        + top[-1] * (step_primal / (1.0 + step_primal))
                        - fall(top)
                    )
                for dual, value in zip(duals, fresh):
                    dual[x] = value
                lead[x - 2] = updated + updated - mid[-1]
                field[x - 2] = updated
                for dual, value in zip(duals, again):
                    dual[x - 4] = value
                if ends and outer == OUTER - 1:
                    result[x - PAD - 6] = final * (1.0 / gain)
                elif ends:
                    for h in range(halves):
                        at = cell_row(x - PAD - 6, h)
                        for y in range(0, ny, GROUP):
                            current[pl.ds(at + y * deep, GROUP, stride=deep), :] = final[
                                y : y + GROUP, h * LANES : (h + 1) * LANES
                            ]
                return carry

            lax.fori_loop(first + PAD, last + PAD, body, 0)

        marks = [start] + [x for x in (REACH, rows, rows + REACH) if start < x < stop] + [stop]
        for first, last in zip(marks[:-1], marks[1:]):
            run(first, last)

    homes = [(x, x + GROUP) for x in range(0, rows, GROUP)]

    def denoise(outer):
        stop = rows + REACH + (1 if outer < OUTER - 1 else 0)
        done = -5 if outer < OUTER - 1 else -3
        if outer < OUTER - 1:
            ready = {batch[2] * GROUP + REACH: batch for batch in batches}
        else:
            ready = {last + REACH: (first, last) for first, last in homes}
        for j in range(extents):
            back_bulk(j).wait_recv()
            collect(j)
            limit = stop if j == extents - 1 else ((j + 1) * slots - 1) * GROUP - 1
            for x in sorted(ready):
                if done < x <= limit:
                    sweep_rows(outer, done, x)
                    if outer < OUTER - 1:
                        send_forward(ready[x])
                    else:
                        deliver(*ready[x])
                    done = x
            if done < limit:
                sweep_rows(outer, done, limit)
                done = limit

    turns = list(range(1, chunks)) + [0]
    loads[0].wait()
    lax.fori_loop(0, ny, stage, 0)
    pl.semaphore_wait(barrier, greeted - 1)
    asides = [(batch, side) for side in range(2) for batch in aside]
    for turn in asides[:2]:
        send_aside(*turn)
    for side in range(2):
        for i, batch in enumerate(first_turn):
            send_direct(batch, side)
            at = side * len(aside) + i + 2
            for turn in asides[at : at + 1] if i < len(aside) else []:
                send_aside(*turn)

    @pl.when(me == 0)
    def _():
        goal[PAD - GROUP : PAD] = jnp.zeros((GROUP, ny, nz), f32)

    @pl.when(me == n - 1)
    def _():
        goal[PAD + rows : PAD + rows + GROUP] = jnp.zeros((GROUP, ny, nz), f32)

    for load in loads[1:]:
        load.wait()
    make_tables()
    for turn in asides[:1]:
        pass_along(*turn)
    make_filter()
    for turn in asides[1:]:
        pass_along(*turn)
    for outer in range(OUTER):
        filtered(outer)
        for c in range(chunks):
            send_back(c)
        for j in range(chunks, extents):
            start_back(j)
        for batch in batches:
            if outer == 0:
                first_sent(batch)
            else:
                forward_bulk(batch, n - 1).wait_send()
        denoise(outer)
        for j in range(extents):
            back_bulk(j).wait_send()
    delivered()


def constants(n, rows, slots, nz):
    nx = n * rows
    groups = rows // GROUP
    place = np.array(
        [
            ((d * groups + c + slot - 1) * GROUP + r) % nx
            for c in range(0, groups, slots)
            for d in range(n)
            for slot in range(slots)
            for r in range(GROUP)
        ]
    )
    turn = 2.0 * math.pi / nx
    coarse = (place[::GROUP, None] * place[None, :] % nx) * turn
    fine = (np.arange(GROUP)[:, None] * place[None, :] % nx) * turn
    norm = 1.0 / math.sqrt(nx)
    tables = (
        np.cos(coarse),
        np.sin(coarse),
        (np.cos(fine) + np.sin(fine)) * norm,
        (np.cos(fine) - np.sin(fine)) * norm,
    )
    k = np.arange(nz)
    angle = (k[:, None] * k[None, :] % nz) * (2.0 * math.pi / nz)
    cas_z = ((np.cos(angle) + np.sin(angle)) / math.sqrt(nz)).astype(np.float32)
    z_high = cas_z.astype(bf16)
    z_low = (cas_z - z_high.astype(np.float32)).astype(bf16)
    return [jnp.asarray(t, f32) for t in tables] + [jnp.asarray(z_high), jnp.asarray(z_low)]


def local(n, cross, observed, tf_table, tilt_index, wedge):
    rows, ny, nz = observed.shape
    nx = n * rows
    groups = rows // GROUP
    slots = 2 if groups % 2 == 0 else 1
    chunks = groups // slots
    extents = (groups + 2) // slots
    lines, columns = tilt_index.shape
    depth, width = -(-lines // 128) * 128, -(-columns // 128) * 128
    tables = constants(n, rows, slots, nz)
    tiles = observed.reshape(rows, ny // GROUP, GROUP, nz // LANES, LANES)
    tiles = tiles.transpose(0, 1, 3, 2, 4).reshape(-1, LANES)
    vmem = pl.BlockSpec(memory_space=pltpu.VMEM)
    smem = pl.BlockSpec(memory_space=pltpu.SMEM)
    hbm = pl.BlockSpec(memory_space=pltpu.HBM)
    operands = (tiles, tilt_index.T, wedge.T, *tables)
    grid_rows = pltpu.VMEM((rows + 2 * PAD, ny, nz), f32)
    plane = pltpu.VMEM((nx, nz), f32)
    blocks = pltpu.VMEM((chunks, n * slots * GROUP * nz // LANES, LANES), f32)
    cells = pltpu.VMEM((rows * ny * nz // LANES, LANES), f32)
    semaphores = pltpu.SemaphoreType.DMA((extents,))
    landing = pltpu.VMEM((ny * (groups + 2) * GROUP * nz // LANES, LANES), f32)
    result = pl.pallas_call(
        functools.partial(kernel, n, rows, slots, cross),
        out_shape=pltpu.VMEM((rows, ny, nz), f32),
        in_specs=[hbm, smem] + [hbm] * 8,
        out_specs=vmem,
        scratch_shapes=[pltpu.VMEM(operand.shape, operand.dtype) for operand in operands]
        + [
            pltpu.SemaphoreType.DMA((len(operands),)),
            blocks,
            plane,
            plane,
            plane,
            pltpu.VMEM((nx, nx), bf16),
            pltpu.VMEM((nx, nx), bf16),
            pltpu.VMEM((nx, nz), bf16),
            pltpu.VMEM((nx, nz), bf16),
            blocks,
            landing,
            grid_rows,
            grid_rows,
            grid_rows,
            [grid_rows] * 3,
            cells,
            pltpu.VMEM((width, depth), f32),
            pltpu.VMEM((rows * ny * nz // LANES // 2, LANES), f32),
            pltpu.VMEM((rows, ny, nz), f32),
            semaphores,
            semaphores,
            semaphores,
            semaphores,
            pltpu.SemaphoreType.DMA((2, extents)),
            pltpu.SemaphoreType.DMA((2, extents)),
            semaphores,
            pltpu.SemaphoreType.DMA(()),
            pltpu.SemaphoreType.DMA(()),
            pltpu.SemaphoreType.DMA(()),
        ],
        compiler_params=pltpu.CompilerParams(
            collective_id=0, has_side_effects=True, vmem_limit_bytes=60 * 1024 * 1024
        ),
    )(operands[0], tf_table, *operands[1:])
    return result


def solution(mesh):
    in_specs = (P(("groups", "gy"), None, None), P(), P(), P())
    out_specs = P(("groups", "gy"), None, None)
    n = mesh.shape["gy"]
    cross = mesh.shape["groups"] == 2 and n % 4 == 0
    body = functools.partial(local, n, cross)
    return jax.shard_map(body, mesh=mesh, in_specs=in_specs, out_specs=out_specs, check_vma=False)
```

```python
import functools
import math

import jax
import jax.numpy as jnp
import numpy as np
from jax import lax
from jax.experimental import pallas as pl
from jax.experimental.pallas import tpu as pltpu
from jax.sharding import PartitionSpec as P

WAVES = 2
OUTER = 2
PASSES = 2
GROUP = 8
LANES = 128
WIDE = 2
LAG = WIDE + 1
DELAY = 3 * LAG
PAD = 12

step_dual = 0.14
step_primal = 0.14
huber_eps = 0.05
bound_dual = 0.5
relax = 1.0 / (1.0 + step_dual * huber_eps / bound_dual)
gain = step_dual * relax
MESH = pl.DeviceIdType.MESH
f32 = jnp.float32
bf16 = jnp.bfloat16


def split(value):
    high = value.astype(bf16)
    low = (value - high.astype(f32)).astype(bf16)
    return high, low


def dot3(a_high, a_low, b_high, b_low):
    dot = functools.partial(jnp.dot, preferred_element_type=f32)
    return dot(a_high, b_high) + (dot(a_high, b_low) + dot(a_low, b_high))


def kernel(
    n, rows, slots, cross,
    cells_in, table_ref, tilt_in, wedge_in, cos_in, sin_in, cas_in, case_in, zh_in, zl_in,
    out_ref,
    cells_ref, tilt_ref, wedge_ref, cos_ref, sin_ref, cas_ref, case_ref, zh_ref, zl_ref, load_sem,
    gathered, total, data_term, prior_gain, x_high, x_low, m_high, m_low, back,
    target, goal, field, lead, duals, current, code, passing, result,
    send_sem, recv_sem, back_send, back_recv,
    pass_send, pass_recv, pass_on, home_send, home_recv, own_sem,
):
    gx, gy = lax.axis_index("groups"), lax.axis_index("gy")
    half = n // 2
    high, low = gy // half, gy % half
    if cross:
        near = gx == high
        who = gx * half + low
        me = low % 2 * half + low // 2 * 2 + gx
    else:
        near = gx == gx
        who = gy
        me = gy
    far = jnp.logical_not(near)

    def owner_device(owner, first):
        if not cross:
            return {"gy": owner}
        block = gx if first else high
        return {"groups": owner // half, "gy": block * half + owner % half}

    def slab_device(slab):
        if not cross:
            return {"gy": slab}
        return {"groups": slab % 2, "gy": high * half + slab % half // 2 * 2 + slab // half}

    groups = rows // GROUP
    chunks = groups // slots
    extents = (groups + 2) // slots
    part = slots * GROUP
    ny, nz = out_ref.shape[1], out_ref.shape[2]
    halves = nz // LANES
    tall = GROUP * halves
    deep = groups * tall
    wide = (groups + 2) * tall
    share = slots * tall
    batches = [
        (m, max(m * slots - 1, 0), min((m + 1) * slots - 1, groups))
        for m in range(1 // slots, groups // slots + 1)
    ]
    aside = batches[:-1]
    first_turn = [batch for batch in batches if batch[0] % chunks > 0]
    first_turn += [batch for batch in batches if batch[0] % chunks == 0]
    nx = n * rows
    span_rows = n * part
    block = math.gcd(nx, 256)
    row_blocks = nx // block

    barrier = pltpu.get_barrier_semaphore()

    def greet(o, carry):
        if cross:
            other = lax.rem(gx * n + gy + o, 2 * n)
            device = {"groups": other // n, "gy": other % n}
        else:
            device = {"gy": lax.rem(gy + o, n)}
        pl.semaphore_signal(barrier, inc=1, device_id=device, device_id_type=MESH)
        return carry

    greeted = 2 * n if cross else n
    loads = [
        pltpu.make_async_copy(source, place, load_sem.at[i])
        for i, (source, place) in enumerate(
            [
                (cells_in, cells_ref),
                (cos_in, cos_ref),
                (sin_in, sin_ref),
                (cas_in, cas_ref),
                (case_in, case_ref),
                (tilt_in, tilt_ref),
                (wedge_in, wedge_ref),
                (zh_in, zh_ref),
                (zl_in, zl_ref),
            ]
        )
    ]
    for load in loads:
        load.start()
    lax.fori_loop(1, greeted, greet, 0)

    def every_other(mine, action):
        def step(o, carry):
            action(lax.rem(mine + o, n))
            return carry

        lax.fori_loop(1, n, step, 0)

    def every_half(side, action):
        count = half // WAVES

        def step(o, carry):
            action(lax.rem(low // WAVES + o, count) * WAVES + side)
            return carry

        lax.fori_loop(0, count, step, 0)

    def cells_of(y, batch, depth):
        _, low_group, high_group = batch
        return pl.ds(pl.multiple_of(y * depth + low_group * tall, tall), (high_group - low_group) * tall)

    def seat_of(slab, batch):
        m, low_group, high_group = batch
        line = lax.rem(slab + m // chunks, n) * slots + (low_group + 1) % slots
        return pl.ds(pl.multiple_of(line * tall, tall), (high_group - low_group) * tall)

    def block_of(j, slab):
        return pl.ds(pl.multiple_of(lax.rem(slab + j // chunks, n) * share, share), share)

    def extent_of(y, j):
        return pl.ds(pl.multiple_of(y * wide + j * share, tall), share)

    def cell_row(x, h):
        return (x // GROUP * halves + h) * GROUP + lax.rem(x, GROUP)

    def forward_copy(batch, owner, slab, first):
        m = batch[0]
        return pltpu.make_async_remote_copy(
            src_ref=current.at[cells_of(owner, batch, deep)],
            dst_ref=gathered.at[m % chunks, seat_of(slab, batch)],
            send_sem=send_sem.at[m],
            recv_sem=recv_sem.at[m],
            device_id=owner_device(owner, first),
            device_id_type=MESH,
        )

    def pass_copy(batch, side, k):
        m = batch[0]
        return pltpu.make_async_remote_copy(
            src_ref=current.at[cells_of((1 - gx) * half + k, batch, deep)],
            dst_ref=passing.at[cells_of(k, batch, deep)],
            send_sem=pass_send.at[side, m],
            recv_sem=pass_recv.at[side, m],
            device_id={"groups": 1 - gx, "gy": gy},
            device_id_type=MESH,
        )

    def pass_on_copy(batch, k):
        m = batch[0]
        return pltpu.make_async_remote_copy(
            src_ref=passing.at[cells_of(k, batch, deep)],
            dst_ref=gathered.at[m % chunks, seat_of(gy, batch)],
            send_sem=pass_on.at[m],
            recv_sem=recv_sem.at[m],
            device_id={"groups": gx, "gy": (1 - gx) * half + k},
            device_id_type=MESH,
        )

    def back_copy(j, slab):
        return pltpu.make_async_remote_copy(
            src_ref=back.at[j % chunks, block_of(j, slab)],
            dst_ref=target.at[extent_of(who, j)],
            send_sem=back_send.at[j],
            recv_sem=back_recv.at[j],
            device_id=slab_device(slab),
            device_id_type=MESH,
        )

    def home_copy(first, last):
        span = pl.ds(first, last - first)
        return pltpu.make_async_remote_copy(
            src_ref=result.at[span],
            dst_ref=out_ref.at[span],
            send_sem=home_send,
            recv_sem=home_recv,
            device_id={"groups": high, "gy": me},
            device_id_type=MESH,
        )

    def own_copy(first, last):
        span = pl.ds(first, last - first)
        return pltpu.make_async_copy(result.at[span], out_ref.at[span], own_sem)

    if cross:
        home = jnp.logical_and(gx == high, gy == me)
        away = jnp.logical_not(home)
    else:
        home, away = near, far

    def deliver(first, last):
        if cross:

            @pl.when(away)
            def _():
                home_copy(first, last).start()

        @pl.when(home)
        def _():
            own_copy(first, last).start()

    def delivered():
        if cross:

            @pl.when(away)
            def _():
                home_copy(0, rows).wait_send()
                home_copy(0, rows).wait_recv()

        @pl.when(home)
        def _():
            own_copy(0, rows).wait()

    def bulk(ref, lines, send, recv):
        span = ref.at[pl.ds(0, lines)]
        return pltpu.make_async_remote_copy(
            src_ref=span,
            dst_ref=span,
            send_sem=send,
            recv_sem=recv,
            device_id=owner_device(who, False),
            device_id_type=MESH,
        )

    def lines_of(batch):
        return (batch[2] - batch[1]) * tall

    def forward_bulk(batch, count):
        m = batch[0]
        return bulk(current, count * lines_of(batch), send_sem.at[m], recv_sem.at[m])

    def pass_bulk(batch, side):
        lines = half // WAVES * lines_of(batch)
        return bulk(passing, lines, pass_send.at[side, batch[0]], pass_recv.at[side, batch[0]])

    def pass_on_bulk(batch):
        m = batch[0]
        return bulk(passing, half * lines_of(batch), pass_on.at[m], pass_recv.at[0, m])

    def back_bulk(j):
        return bulk(target, (n - 1) * share, back_send.at[j], back_recv.at[j])

    def keep_own(batch, slab):
        gathered[batch[0] % chunks, seat_of(slab, batch)] = current[cells_of(who, batch, deep)]

    def send_direct(batch, side):
        if not cross:
            if side == 0:
                every_other(who, lambda owner: forward_copy(batch, owner, gy, True).start())
                keep_own(batch, gy)
            return

        @pl.when(far)
        def _():
            every_half(side, lambda k: forward_copy(batch, gx * half + k, gy, True).start())
            if batch not in aside:
                every_half(
                    side, lambda k: forward_copy(batch, (1 - gx) * half + k, gy, True).start()
                )

        @pl.when(near)
        def _():
            every_half(side, lambda k: forward_copy(batch, (1 - gx) * half + k, gy, True).start())

            def own_row(k):
                @pl.when(k != low)
                def _():
                    forward_copy(batch, gx * half + k, gy, True).start()

            every_half(side, own_row)
            if side == 0:
                keep_own(batch, gy)

    def send_aside(batch, side):
        if cross:

            @pl.when(far)
            def _():
                every_half(side, lambda k: pass_copy(batch, side, k).start())

    def pass_along(batch, side):
        if cross:

            @pl.when(near)
            def _():
                pass_bulk(batch, side).wait_recv()
                every_half(side, lambda k: pass_on_copy(batch, k).start())

    def first_arrived(batch):
        @pl.when(near)
        def _():
            forward_bulk(batch, n - 1).wait_recv()

        if cross:

            @pl.when(far)
            def _():
                forward_bulk(batch, n).wait_recv()

    def first_sent(batch):
        relayed = cross and batch in aside

        @pl.when(near)
        def _():
            forward_bulk(batch, n - 1).wait_send()
            if relayed:
                pass_on_bulk(batch).wait_send()

        if cross:

            @pl.when(far)
            def _():
                forward_bulk(batch, half if relayed else n).wait_send()
                if relayed:
                    for side in range(WAVES):
                        pass_bulk(batch, side).wait_send()

    def send_forward(batch, side):
        def step(o, carry):
            owner = lax.rem(who // 2 + o, half) * 2 + side

            @pl.when(owner != who)
            def _():
                forward_copy(batch, owner, me, False).start()

            return carry

        lax.fori_loop(0, half, step, 0)
        if side == 0:
            keep_own(batch, me)

    def stage(y, carry):
        stride = ny * halves
        for h in range(halves):
            first = (y // GROUP * halves + h) * GROUP + y % GROUP
            lines = cells_ref[pl.ds(first, rows, stride=stride), :]
            for g in range(groups):
                at = y * deep + g * tall + h * GROUP
                current[pl.ds(pl.multiple_of(at, GROUP), GROUP), :] = lines[
                    g * GROUP : (g + 1) * GROUP, :
                ]
        return carry

    def make_tables():
        def body(m, carry):
            lines = jnp.concatenate(
                [
                    cos_ref[pl.ds(k, 1), :] * cas_ref[...] + sin_ref[pl.ds(k, 1), :] * case_ref[...]
                    for k in (2 * m, 2 * m + 1)
                ],
                axis=0,
            )
            at = pl.ds(pl.multiple_of(m * 2 * GROUP, 2 * GROUP), 2 * GROUP)
            x_high[at, :], x_low[at, :] = split(lines)
            return carry

        lax.fori_loop(0, nx // (2 * GROUP), body, 0)

    def make_filter():
        columns, lines = tilt_ref.shape
        code[...] = jnp.zeros_like(code)
        code[0:columns, 0:lines] = jnp.where(wedge_ref[...] == 0, 0, tilt_ref[...] + 1).astype(f32)
        width, depth = code.shape
        kz = lax.broadcasted_iota(jnp.int32, (nz, width), 0)
        pick_z = jnp.where(
            lax.broadcasted_iota(jnp.int32, (nz, width), 1) == jnp.minimum(kz, nz - kz), 1.0, 0.0
        ).astype(bf16)
        spread = jnp.dot(pick_z, code[...].astype(bf16), preferred_element_type=f32).astype(bf16)

        def body(b, carry):
            line = b * block + lax.broadcasted_iota(jnp.int32, (block, depth), 0)
            c = line // span_rows
            slot = line % part // GROUP
            place = line % span_rows // part * groups + c * slots + slot - 1
            kx = (place * GROUP + line % GROUP + nx) % nx
            column = lax.broadcasted_iota(jnp.int32, (block, depth), 1)
            pick_x = jnp.where(column == jnp.minimum(kx, nx - kx), 1.0, 0.0).astype(bf16)
            which = lax.dot_general(
                pick_x, spread, (((1,), (1,)), ((), ())), preferred_element_type=f32
            )
            response = jnp.zeros_like(which)
            for level in range(table_ref.shape[0]):
                response = jnp.where(which == level + 1.0, table_ref[level], response)
            prior = 1.0 / (response * response + 1.0)
            at = pl.ds(pl.multiple_of(b * block, block), block)
            prior_gain[at, :] = prior
            data_term[at, :] = response * prior
            return carry

        lax.fori_loop(0, row_blocks, body, 0)

    def filtered(outer):
        for c in turns:
            for batch in batches:
                if batch[0] % chunks == c and outer == 0:
                    first_arrived(batch)
                elif batch[0] % chunks == c:
                    forward_bulk(batch, n - 1).wait_recv()
            pieces = gathered[c].reshape(n * slots, halves, GROUP, LANES)
            lines = [pieces[:, h].reshape(span_rows, LANES) for h in range(halves)]
            high, low = split(jnp.concatenate(lines, axis=1))
            high, low = split(dot3(high, low, zh_ref[...], zl_ref[...]))

            def body(b, carry):
                at = pl.ds(pl.multiple_of(b * block, block), block)
                span = pl.ds(c * span_rows, span_rows)
                spectrum = dot3(x_high[at, span], x_low[at, span], high, low)
                if c != turns[0]:
                    spectrum = total[at, :] + spectrum
                if c != turns[-1]:
                    total[at, :] = spectrum
                    return carry
                if outer == 0:
                    spectrum = spectrum * gain
                    data_term[at, :] = data_term[at, :] * spectrum
                a_high, a_low = split(data_term[at, :] + prior_gain[at, :] * spectrum)
                m_high[at, :], m_low[at, :] = split(dot3(a_high, a_low, zh_ref[...], zl_ref[...]))
                return carry

            lax.fori_loop(0, row_blocks, body, 0, unroll=True)

    def send_back(c):
        step = math.gcd(span_rows, 256)

        def body(b, carry):
            line = pl.ds(pl.multiple_of(c * span_rows + b * step, step), step)
            lines = dot3(x_high[line, :], x_low[line, :], m_high[...], m_low[...])
            pieces = [
                lines[:, h * LANES : (h + 1) * LANES].reshape(step // GROUP, 1, GROUP, LANES)
                for h in range(halves)
            ]
            count = step * halves
            at = pl.ds(pl.multiple_of(b * count, count), count)
            back[c, at] = jnp.concatenate(pieces, axis=1).reshape(count, LANES)
            return carry

        lax.fori_loop(0, span_rows // step, body, 0)
        start_back(c)

    def start_back(j):
        every_other(me, lambda slab: back_copy(j, slab).start())
        target[extent_of(who, j)] = back[j % chunks, block_of(j, me)]

    def sum_y(value):
        pieces = [value[y : y + GROUP, :] for y in range(0, ny, GROUP)]
        nothing = jnp.zeros_like(pieces[0])
        line = lax.broadcasted_iota(jnp.int32, pieces[0].shape, 0)
        ups = [nothing] + [pltpu.roll(piece, 1, 0) for piece in pieces]
        downs = [pltpu.roll(piece, GROUP - 1, 0) for piece in pieces] + [nothing]
        return jnp.concatenate(
            [
                jnp.where(line == 0, ups[y], ups[y + 1])
                + jnp.where(line == GROUP - 1, downs[y + 1], downs[y])
                for y in range(len(pieces))
            ],
            axis=0,
        )

    def sum_z(value):
        pieces = [value[:, z : z + LANES] for z in range(0, nz, LANES)]
        nothing = jnp.zeros_like(pieces[0])
        lane = lax.broadcasted_iota(jnp.int32, pieces[0].shape, 1)
        ups = [nothing] + [pltpu.roll(piece, 1, 1) for piece in pieces]
        downs = [pltpu.roll(piece, LANES - 1, 1) for piece in pieces] + [nothing]
        return jnp.concatenate(
            [
                jnp.where(lane == 0, ups[z], ups[z + 1])
                + jnp.where(lane == LANES - 1, downs[z + 1], downs[z])
                for z in range(len(pieces))
            ],
            axis=1,
        )

    def collect(j):
        def gather(e):
            def body(r, carry):
                for h in range(halves):
                    for y in range(0, ny, GROUP):
                        goal[
                            PAD + (e - 1) * GROUP + r,
                            y : y + GROUP,
                            h * LANES : (h + 1) * LANES,
                        ] = target[pl.ds(y * wide + e * tall + h * GROUP + r, GROUP, stride=wide), :]
                return carry

            lax.fori_loop(0, GROUP, body, 0)

        for e in range(j * slots, (j + 1) * slots):
            if e == 0:
                pl.when(me > 0)(functools.partial(gather, e))
            elif e == groups + 1:
                pl.when(me < n - 1)(functools.partial(gather, e))
            else:
                gather(e)

    def rise_load(origin, x, fresh):
        here, before, after = origin[x], origin[x - 1], origin[x + 1]
        olds = None if fresh else [dual[x] for dual in duals]
        return here, before, after, olds

    def rise(loaded, keep):
        here, before, after, olds = loaded
        twice = here + here
        raised = [before + after - twice, sum_y(here) - twice, sum_z(here) - twice]
        if olds is not None:
            raised = [old + bend for old, bend in zip(olds, raised)]
        norm = raised[0] * raised[0] + raised[1] * raised[1] + raised[2] * raised[2]
        shrink = lax.rsqrt(jnp.maximum(1.0 / relax**2, norm * (1.0 / (bound_dual * relax) ** 2)))
        if keep is not None:
            shrink = shrink * keep
        return [part_of * shrink for part_of in raised]

    def fall_load(x):
        dual_x, dual_y, dual_z = duals
        return (
            dual_x[x], dual_x[x - 1], dual_x[x + 1],
            dual_y[x], dual_z[x], goal[x],
        )

    def fall(loaded):
        in_x, before, after, in_y, in_z, _ = loaded
        middle = in_x + in_y + in_z
        return (before + after + sum_y(in_y) + sum_z(in_z) - (middle + middle)) * (
            step_primal * step_dual / (1.0 + step_primal)
        )

    def sweep_rows(outer, start, stop):
        def run(first, last):
            masked = first < DELAY or last > rows - WIDE + 1
            ends = first >= DELAY and last <= rows + DELAY
            lines = range(WIDE)

            def keep(x):
                whole = me * rows + PAD + x
                return jnp.where(jnp.logical_and(whole >= 2 * PAD, whole < nx + 2 * PAD), 1.0, 0.0)

            def body(k, carry):
                x = k * WIDE + (first + PAD)
                low = [rise_load(goal, x + i, outer == 0) for i in lines]
                mid = [fall_load(x - LAG + i) for i in lines]
                high = [rise_load(lead, x - 2 * LAG + i, False) for i in lines]
                if ends:
                    top = [fall_load(x - DELAY + i) for i in lines]
                    old = [field[x - DELAY + i] for i in lines]
                fresh = [rise(low[i], keep(x + i) if masked else None) for i in lines]
                updated = [mid[i][-1] - fall(mid[i]) for i in lines]
                if masked:
                    updated = [updated[i] * keep(x - LAG + i) for i in lines]
                again = [
                    rise(high[i], keep(x - 2 * LAG + i) if masked else None) for i in lines
                ]
                if ends:
                    final = [
                        old[i] * (1.0 / (1.0 + step_primal))
                        + top[i][-1] * (step_primal / (1.0 + step_primal))
                        - fall(top[i])
                        for i in lines
                    ]
                for i in lines:
                    for dual, value in zip(duals, fresh[i]):
                        dual[x + i] = value
                    lead[x - LAG + i] = updated[i] + updated[i] - mid[i][-1]
                    field[x - LAG + i] = updated[i]
                    for dual, value in zip(duals, again[i]):
                        dual[x - 2 * LAG + i] = value
                for i in lines:
                    at_x = x + i - PAD - DELAY
                    if ends and outer == OUTER - 1:
                        result[at_x] = final[i] * (1.0 / gain)
                    elif ends:
                        for h in range(halves):
                            at = cell_row(at_x, h)
                            for y in range(0, ny, GROUP):
                                current[pl.ds(at + y * deep, GROUP, stride=deep), :] = final[i][
                                    y : y + GROUP, h * LANES : (h + 1) * LANES
                                ]
                return carry

            lax.fori_loop(0, (last - first) // WIDE, body, 0)

        cuts = {x for x in (DELAY, rows - WIDE + 1, rows + DELAY) if start < x < stop}
        marks = sorted(cuts | {start, stop})
        for first, last in zip(marks[:-1], marks[1:]):
            run(first, last)

    homes = [(x, x + GROUP) for x in range(0, rows, GROUP)]

    def denoise(outer, sent):
        stop = rows + DELAY + (1 if WIDE == 1 and outer < OUTER - 1 else 0)
        held = []
        done = -5 if outer < OUTER - 1 else -3
        if outer < OUTER - 1:
            ready = {batch[2] * GROUP + DELAY: batch for batch in batches}
        else:
            ready = {last + DELAY: (first, last) for first, last in homes}
        def later(j):
            if j < chunks:
                send_back(j)
            elif j < extents:
                start_back(j)

        if sent == chunks:
            for j in range(sent, extents):
                later(j)
            sent = extents
        for j in range(extents):
            back_bulk(j).wait_recv()
            collect(j)
            limit = stop if j == extents - 1 else ((j + 1) * slots - 1) * GROUP - 1
            for x in sorted(ready):
                if done < x <= limit:
                    sweep_rows(outer, done, x)
                    if outer < OUTER - 1:
                        send_forward(ready[x], 0)
                        for batch in held:
                            send_forward(batch, 1)
                        held = [ready[x]]
                    else:
                        deliver(*ready[x])
                    done = x
            if done < limit:
                sweep_rows(outer, done, limit)
                done = limit
            later(j + sent)
        for batch in held:
            send_forward(batch, 1)

    turns = list(range(1, chunks)) + [0]
    loads[0].wait()
    lax.fori_loop(0, ny, stage, 0)
    pl.semaphore_wait(barrier, greeted - 1)
    asides = [(batch, side) for side in range(WAVES) for batch in aside]
    for turn in asides[:2]:
        send_aside(*turn)
    for side in range(WAVES):
        for i, batch in enumerate(first_turn):
            send_direct(batch, side)
            at = side * len(aside) + i + 2
            for turn in asides[at : at + 1] if i < len(aside) else []:
                send_aside(*turn)

    @pl.when(me == 0)
    def _():
        goal[PAD - GROUP : PAD] = jnp.zeros((GROUP, ny, nz), f32)

    @pl.when(me == n - 1)
    def _():
        goal[PAD + rows : PAD + rows + GROUP] = jnp.zeros((GROUP, ny, nz), f32)

    for load in loads[1:]:
        load.wait()
    make_tables()
    for turn in asides[:1]:
        pass_along(*turn)
    make_filter()
    for turn in asides[1:]:
        pass_along(*turn)
    for outer in range(OUTER):
        filtered(outer)
        lead_in = chunks if outer < OUTER - 1 else min(chunks, 3)
        for j in range(lead_in):
            send_back(j)
        for batch in batches:
            if outer == 0:
                first_sent(batch)
            else:
                forward_bulk(batch, n - 1).wait_send()
        denoise(outer, lead_in)
        for j in range(extents):
            back_bulk(j).wait_send()
    delivered()


def constants(n, rows, slots, nz):
    nx = n * rows
    groups = rows // GROUP
    place = np.array(
        [
            ((d * groups + c + slot - 1) * GROUP + r) % nx
            for c in range(0, groups, slots)
            for d in range(n)
            for slot in range(slots)
            for r in range(GROUP)
        ]
    )
    turn = 2.0 * math.pi / nx
    coarse = (place[::GROUP, None] * place[None, :] % nx) * turn
    fine = (np.arange(GROUP)[:, None] * place[None, :] % nx) * turn
    norm = 1.0 / math.sqrt(nx)
    tables = (
        np.cos(coarse),
        np.sin(coarse),
        (np.cos(fine) + np.sin(fine)) * norm,
        (np.cos(fine) - np.sin(fine)) * norm,
    )
    k = np.arange(nz)
    angle = (k[:, None] * k[None, :] % nz) * (2.0 * math.pi / nz)
    cas_z = ((np.cos(angle) + np.sin(angle)) / math.sqrt(nz)).astype(np.float32)
    z_high = cas_z.astype(bf16)
    z_low = (cas_z - z_high.astype(np.float32)).astype(bf16)
    return [jnp.asarray(t, f32) for t in tables] + [jnp.asarray(z_high), jnp.asarray(z_low)]


def local(n, cross, observed, tf_table, tilt_index, wedge):
    rows, ny, nz = observed.shape
    nx = n * rows
    groups = rows // GROUP
    slots = 2 if groups % 2 == 0 else 1
    chunks = groups // slots
    extents = (groups + 2) // slots
    lines, columns = tilt_index.shape
    depth, width = -(-lines // 128) * 128, -(-columns // 128) * 128
    tables = constants(n, rows, slots, nz)
    tiles = observed.reshape(rows, ny // GROUP, GROUP, nz // LANES, LANES)
    tiles = tiles.transpose(0, 1, 3, 2, 4).reshape(-1, LANES)
    vmem = pl.BlockSpec(memory_space=pltpu.VMEM)
    smem = pl.BlockSpec(memory_space=pltpu.SMEM)
    hbm = pl.BlockSpec(memory_space=pltpu.HBM)
    operands = (tiles, tilt_index.T, wedge.T, *tables)
    grid_rows = pltpu.VMEM((rows + 2 * PAD, ny, nz), f32)
    plane = pltpu.VMEM((nx, nz), f32)
    blocks = pltpu.VMEM((chunks, n * slots * GROUP * nz // LANES, LANES), f32)
    cells = pltpu.VMEM((rows * ny * nz // LANES, LANES), f32)
    semaphores = pltpu.SemaphoreType.DMA((extents,))
    landing = pltpu.VMEM((ny * (groups + 2) * GROUP * nz // LANES, LANES), f32)
    result = pl.pallas_call(
        functools.partial(kernel, n, rows, slots, cross),
        out_shape=pltpu.VMEM((rows, ny, nz), f32),
        in_specs=[hbm, smem] + [hbm] * 8,
        out_specs=vmem,
        scratch_shapes=[pltpu.VMEM(operand.shape, operand.dtype) for operand in operands]
        + [
            pltpu.SemaphoreType.DMA((len(operands),)),
            blocks,
            plane,
            plane,
            plane,
            pltpu.VMEM((nx, nx), bf16),
            pltpu.VMEM((nx, nx), bf16),
            pltpu.VMEM((nx, nz), bf16),
            pltpu.VMEM((nx, nz), bf16),
            blocks,
            landing,
            grid_rows,
            grid_rows,
            grid_rows,
            [grid_rows] * 3,
            cells,
            pltpu.VMEM((width, depth), f32),
            pltpu.VMEM((rows * ny * nz // LANES // 2, LANES), f32),
            pltpu.VMEM((rows, ny, nz), f32),
            semaphores,
            semaphores,
            semaphores,
            semaphores,
            pltpu.SemaphoreType.DMA((WAVES, extents)),
            pltpu.SemaphoreType.DMA((WAVES, extents)),
            semaphores,
            pltpu.SemaphoreType.DMA(()),
            pltpu.SemaphoreType.DMA(()),
            pltpu.SemaphoreType.DMA(()),
        ],
        compiler_params=pltpu.CompilerParams(
            collective_id=0, has_side_effects=True, vmem_limit_bytes=60 * 1024 * 1024
        ),
    )(operands[0], tf_table, *operands[1:])
    return result


def solution(mesh):
    in_specs = (P(("groups", "gy"), None, None), P(), P(), P())
    out_specs = P(("groups", "gy"), None, None)
    n = mesh.shape["gy"]
    cross = mesh.shape["groups"] == 2 and n % (2 * WAVES) == 0
    body = functools.partial(local, n, cross)
    return jax.shard_map(body, mesh=mesh, in_specs=in_specs, out_specs=out_specs, check_vma=False)
```

```python
import functools
import math

import jax
import jax.numpy as jnp
import numpy as np
from jax import lax
from jax.experimental import pallas as pl
from jax.experimental.pallas import tpu as pltpu
from jax.sharding import PartitionSpec as P

WAVES = 2
OUTER = 2
PASSES = 2
GROUP = 8
LANES = 128
WIDE = 2
LAG = WIDE + 1
DELAY = 3 * LAG
PAD = 12

step_dual = 0.14
step_primal = 0.14
huber_eps = 0.05
bound_dual = 0.5
relax = 1.0 / (1.0 + step_dual * huber_eps / bound_dual)
gain = step_dual * relax
MESH = pl.DeviceIdType.MESH
f32 = jnp.float32
bf16 = jnp.bfloat16


def split(value):
    high = value.astype(bf16)
    low = (value - high.astype(f32)).astype(bf16)
    return high, low


def dot3(a_high, a_low, b_high, b_low):
    dot = functools.partial(jnp.dot, preferred_element_type=f32)
    return dot(a_high, b_high) + (dot(a_high, b_low) + dot(a_low, b_high))


def kernel(
    n, rows, slots, cross,
    cells_in, table_ref, tilt_in, wedge_in, cos_in, sin_in, cas_in, case_in, zh_in, zl_in,
    out_ref,
    cells_ref, tilt_ref, wedge_ref, cos_ref, sin_ref, cas_ref, case_ref, zh_ref, zl_ref, load_sem,
    gathered, total, data_term, prior_gain, x_high, x_low, m_high, m_low, back,
    target, goal, field, lead, duals, current, code, passing, result,
    send_sem, recv_sem, back_send, back_recv,
    pass_send, pass_recv, pass_on, home_send, home_recv, own_sem,
):
    gx, gy = lax.axis_index("groups"), lax.axis_index("gy")
    half = n // 2
    high, low = gy // half, gy % half
    if cross:
        near = gx == high
        who = gx * half + low
        me = low % 2 * half + low // 2 * 2 + gx
    else:
        near = gx == gx
        who = gy
        me = gy
    far = jnp.logical_not(near)

    def owner_device(owner, first):
        if not cross:
            return {"gy": owner}
        block = gx if first else high
        return {"groups": owner // half, "gy": block * half + owner % half}

    def slab_device(slab):
        if not cross:
            return {"gy": slab}
        return {"groups": slab % 2, "gy": high * half + slab % half // 2 * 2 + slab // half}

    groups = rows // GROUP
    chunks = groups // slots
    extents = (groups + 2) // slots
    part = slots * GROUP
    ny, nz = out_ref.shape[1], out_ref.shape[2]
    halves = nz // LANES
    tall = GROUP * halves
    deep = groups * tall
    wide = (groups + 2) * tall
    share = slots * tall
    batches = [
        (m, max(m * slots - 1, 0), min((m + 1) * slots - 1, groups))
        for m in range(1 // slots, groups // slots + 1)
    ]
    aside = batches[:-1]
    first_turn = [batch for batch in batches if batch[0] % chunks > 0]
    first_turn += [batch for batch in batches if batch[0] % chunks == 0]
    nx = n * rows
    span_rows = n * part
    block = math.gcd(nx, 256)
    row_blocks = nx // block

    barrier = pltpu.get_barrier_semaphore()

    def greet(o, carry):
        if cross:
            other = lax.rem(gx * n + gy + o, 2 * n)
            device = {"groups": other // n, "gy": other % n}
        else:
            device = {"gy": lax.rem(gy + o, n)}
        pl.semaphore_signal(barrier, inc=1, device_id=device, device_id_type=MESH)
        return carry

    greeted = 2 * n if cross else n
    loads = [
        pltpu.make_async_copy(source, place, load_sem.at[i])
        for i, (source, place) in enumerate(
            [
                (cells_in, cells_ref),
                (cos_in, cos_ref),
                (sin_in, sin_ref),
                (cas_in, cas_ref),
                (case_in, case_ref),
                (tilt_in, tilt_ref),
                (wedge_in, wedge_ref),
                (zh_in, zh_ref),
                (zl_in, zl_ref),
            ]
        )
    ]
    for load in loads:
        load.start()
    lax.fori_loop(1, greeted, greet, 0)

    def every_other(mine, action):
        def step(o, carry):
            action(lax.rem(mine + o, n))
            return carry

        lax.fori_loop(1, n, step, 0)

    def every_half(side, action):
        count = half // WAVES

        def step(o, carry):
            action(lax.rem(low // WAVES + o, count) * WAVES + side)
            return carry

        lax.fori_loop(0, count, step, 0)

    def cells_of(y, batch, depth):
        _, low_group, high_group = batch
        return pl.ds(pl.multiple_of(y * depth + low_group * tall, tall), (high_group - low_group) * tall)

    def seat_of(slab, batch):
        m, low_group, high_group = batch
        line = lax.rem(slab + m // chunks, n) * slots + (low_group + 1) % slots
        return pl.ds(pl.multiple_of(line * tall, tall), (high_group - low_group) * tall)

    def block_of(j, slab):
        return pl.ds(pl.multiple_of(lax.rem(slab + j // chunks, n) * share, share), share)

    def extent_of(y, j):
        return pl.ds(pl.multiple_of(y * wide + j * share, tall), share)

    def cell_row(x, h):
        return (x // GROUP * halves + h) * GROUP + lax.rem(x, GROUP)

    def forward_copy(batch, owner, slab, first):
        m = batch[0]
        return pltpu.make_async_remote_copy(
            src_ref=current.at[cells_of(owner, batch, deep)],
            dst_ref=gathered.at[m % chunks, seat_of(slab, batch)],
            send_sem=send_sem.at[m],
            recv_sem=recv_sem.at[m],
            device_id=owner_device(owner, first),
            device_id_type=MESH,
        )

    def pass_copy(batch, side, k):
        m = batch[0]
        return pltpu.make_async_remote_copy(
            src_ref=current.at[cells_of((1 - gx) * half + k, batch, deep)],
            dst_ref=passing.at[cells_of(k, batch, deep)],
            send_sem=pass_send.at[side, m],
            recv_sem=pass_recv.at[side, m],
            device_id={"groups": 1 - gx, "gy": gy},
            device_id_type=MESH,
        )

    def pass_on_copy(batch, k):
        m = batch[0]
        return pltpu.make_async_remote_copy(
            src_ref=passing.at[cells_of(k, batch, deep)],
            dst_ref=gathered.at[m % chunks, seat_of(gy, batch)],
            send_sem=pass_on.at[m],
            recv_sem=recv_sem.at[m],
            device_id={"groups": gx, "gy": (1 - gx) * half + k},
            device_id_type=MESH,
        )

    def back_copy(j, slab):
        return pltpu.make_async_remote_copy(
            src_ref=back.at[j % chunks, block_of(j, slab)],
            dst_ref=target.at[extent_of(who, j)],
            send_sem=back_send.at[j],
            recv_sem=back_recv.at[j],
            device_id=slab_device(slab),
            device_id_type=MESH,
        )

    def home_copy(first, last):
        span = pl.ds(first, last - first)
        return pltpu.make_async_remote_copy(
            src_ref=result.at[span],
            dst_ref=out_ref.at[span],
            send_sem=home_send,
            recv_sem=home_recv,
            device_id={"groups": high, "gy": me},
            device_id_type=MESH,
        )

    def own_copy(first, last):
        span = pl.ds(first, last - first)
        return pltpu.make_async_copy(result.at[span], out_ref.at[span], own_sem)

    if cross:
        home = jnp.logical_and(gx == high, gy == me)
        away = jnp.logical_not(home)
    else:
        home, away = near, far

    def deliver(first, last):
        if cross:

            @pl.when(away)
            def _():
                home_copy(first, last).start()

        @pl.when(home)
        def _():
            own_copy(first, last).start()

    def delivered():
        if cross:

            @pl.when(away)
            def _():
                home_copy(0, rows).wait_send()
                home_copy(0, rows).wait_recv()

        @pl.when(home)
        def _():
            own_copy(0, rows).wait()

    def bulk(ref, lines, send, recv):
        span = ref.at[pl.ds(0, lines)]
        return pltpu.make_async_remote_copy(
            src_ref=span,
            dst_ref=span,
            send_sem=send,
            recv_sem=recv,
            device_id=owner_device(who, False),
            device_id_type=MESH,
        )

    def lines_of(batch):
        return (batch[2] - batch[1]) * tall

    def forward_bulk(batch, count):
        m = batch[0]
        return bulk(current, count * lines_of(batch), send_sem.at[m], recv_sem.at[m])

    def pass_bulk(batch, side):
        lines = half // WAVES * lines_of(batch)
        return bulk(passing, lines, pass_send.at[side, batch[0]], pass_recv.at[side, batch[0]])

    def pass_on_bulk(batch):
        m = batch[0]
        return bulk(passing, half * lines_of(batch), pass_on.at[m], pass_recv.at[0, m])

    def back_bulk(j):
        return bulk(target, (n - 1) * share, back_send.at[j], back_recv.at[j])

    def keep_own(batch, slab):
        gathered[batch[0] % chunks, seat_of(slab, batch)] = current[cells_of(who, batch, deep)]

    def send_direct(batch, side):
        if not cross:
            if side == 0:
                every_other(who, lambda owner: forward_copy(batch, owner, gy, True).start())
                keep_own(batch, gy)
            return

        @pl.when(far)
        def _():
            every_half(side, lambda k: forward_copy(batch, gx * half + k, gy, True).start())
            if batch not in aside:
                every_half(
                    side, lambda k: forward_copy(batch, (1 - gx) * half + k, gy, True).start()
                )

        @pl.when(near)
        def _():
            every_half(side, lambda k: forward_copy(batch, (1 - gx) * half + k, gy, True).start())

            def own_row(k):
                @pl.when(k != low)
                def _():
                    forward_copy(batch, gx * half + k, gy, True).start()

            every_half(side, own_row)
            if side == 0:
                keep_own(batch, gy)

    def send_aside(batch, side):
        if cross:

            @pl.when(far)
            def _():
                every_half(side, lambda k: pass_copy(batch, side, k).start())

    def pass_along(batch, side):
        if cross:

            @pl.when(near)
            def _():
                pass_bulk(batch, side).wait_recv()
                every_half(side, lambda k: pass_on_copy(batch, k).start())

    def first_arrived(batch):
        @pl.when(near)
        def _():
            forward_bulk(batch, n - 1).wait_recv()

        if cross:

            @pl.when(far)
            def _():
                forward_bulk(batch, n).wait_recv()

    def first_sent(batch):
        relayed = cross and batch in aside

        @pl.when(near)
        def _():
            forward_bulk(batch, n - 1).wait_send()
            if relayed:
                pass_on_bulk(batch).wait_send()

        if cross:

            @pl.when(far)
            def _():
                forward_bulk(batch, half if relayed else n).wait_send()
                if relayed:
                    for side in range(WAVES):
                        pass_bulk(batch, side).wait_send()

    def send_forward(batch, side):
        def step(o, carry):
            owner = lax.rem(who // 2 + o, half) * 2 + side

            @pl.when(owner != who)
            def _():
                forward_copy(batch, owner, me, False).start()

            return carry

        lax.fori_loop(0, half, step, 0)
        if side == 0:
            keep_own(batch, me)

    def stage(y, carry):
        stride = ny * halves
        for h in range(halves):
            first = (y // GROUP * halves + h) * GROUP + y % GROUP
            lines = cells_ref[pl.ds(first, rows, stride=stride), :]
            for g in range(groups):
                at = y * deep + g * tall + h * GROUP
                current[pl.ds(pl.multiple_of(at, GROUP), GROUP), :] = lines[
                    g * GROUP : (g + 1) * GROUP, :
                ]
        return carry

    def make_tables():
        def body(m, carry):
            lines = jnp.concatenate(
                [
                    cos_ref[pl.ds(k, 1), :] * cas_ref[...] + sin_ref[pl.ds(k, 1), :] * case_ref[...]
                    for k in (2 * m, 2 * m + 1)
                ],
                axis=0,
            )
            at = pl.ds(pl.multiple_of(m * 2 * GROUP, 2 * GROUP), 2 * GROUP)
            x_high[at, :], x_low[at, :] = split(lines)
            return carry

        lax.fori_loop(0, nx // (2 * GROUP), body, 0)

    def make_filter():
        columns, lines = tilt_ref.shape
        code[...] = jnp.zeros_like(code)
        code[0:columns, 0:lines] = jnp.where(wedge_ref[...] == 0, 0, tilt_ref[...] + 1).astype(f32)
        width, depth = code.shape
        kz = lax.broadcasted_iota(jnp.int32, (nz, width), 0)
        pick_z = jnp.where(
            lax.broadcasted_iota(jnp.int32, (nz, width), 1) == jnp.minimum(kz, nz - kz), 1.0, 0.0
        ).astype(bf16)
        spread = jnp.dot(pick_z, code[...].astype(bf16), preferred_element_type=f32).astype(bf16)

        def body(b, carry):
            line = b * block + lax.broadcasted_iota(jnp.int32, (block, depth), 0)
            c = line // span_rows
            slot = line % part // GROUP
            place = line % span_rows // part * groups + c * slots + slot - 1
            kx = (place * GROUP + line % GROUP + nx) % nx
            column = lax.broadcasted_iota(jnp.int32, (block, depth), 1)
            pick_x = jnp.where(column == jnp.minimum(kx, nx - kx), 1.0, 0.0).astype(bf16)
            which = lax.dot_general(
                pick_x, spread, (((1,), (1,)), ((), ())), preferred_element_type=f32
            )
            response = jnp.zeros_like(which)
            for level in range(table_ref.shape[0]):
                response = jnp.where(which == level + 1.0, table_ref[level], response)
            prior = 1.0 / (response * response + 1.0)
            at = pl.ds(pl.multiple_of(b * block, block), block)
            prior_gain[at, :] = prior
            data_term[at, :] = response * prior
            return carry

        lax.fori_loop(0, row_blocks, body, 0)

    def filtered(outer):
        for c in turns:
            for batch in batches:
                if batch[0] % chunks == c and outer == 0:
                    first_arrived(batch)
                elif batch[0] % chunks == c:
                    forward_bulk(batch, n - 1).wait_recv()
            pieces = gathered[c].reshape(n * slots, halves, GROUP, LANES)
            lines = [pieces[:, h].reshape(span_rows, LANES) for h in range(halves)]
            high, low = split(jnp.concatenate(lines, axis=1))
            high, low = split(dot3(high, low, zh_ref[...], zl_ref[...]))

            def body(b, carry):
                at = pl.ds(pl.multiple_of(b * block, block), block)
                span = pl.ds(c * span_rows, span_rows)
                spectrum = dot3(x_high[at, span], x_low[at, span], high, low)
                if c != turns[0]:
                    spectrum = total[at, :] + spectrum
                if c != turns[-1]:
                    total[at, :] = spectrum
                    return carry
                if outer == 0:
                    spectrum = spectrum * gain
                    data_term[at, :] = data_term[at, :] * spectrum
                a_high, a_low = split(data_term[at, :] + prior_gain[at, :] * spectrum)
                m_high[at, :], m_low[at, :] = split(dot3(a_high, a_low, zh_ref[...], zl_ref[...]))
                return carry

            lax.fori_loop(0, row_blocks, body, 0, unroll=True)

    def send_back(c):
        step = math.gcd(span_rows, 256)

        def body(b, carry):
            line = pl.ds(pl.multiple_of(c * span_rows + b * step, step), step)
            lines = dot3(x_high[line, :], x_low[line, :], m_high[...], m_low[...])
            pieces = [
                lines[:, h * LANES : (h + 1) * LANES].reshape(step // GROUP, 1, GROUP, LANES)
                for h in range(halves)
            ]
            count = step * halves
            at = pl.ds(pl.multiple_of(b * count, count), count)
            back[c, at] = jnp.concatenate(pieces, axis=1).reshape(count, LANES)
            return carry

        lax.fori_loop(0, span_rows // step, body, 0)
        start_back(c)

    def start_back(j):
        every_other(me, lambda slab: back_copy(j, slab).start())
        target[extent_of(who, j)] = back[j % chunks, block_of(j, me)]

    def sum_y(value):
        pieces = [value[y : y + GROUP, :] for y in range(0, ny, GROUP)]
        nothing = jnp.zeros_like(pieces[0])
        line = lax.broadcasted_iota(jnp.int32, pieces[0].shape, 0)
        ups = [nothing] + [pltpu.roll(piece, 1, 0) for piece in pieces]
        downs = [pltpu.roll(piece, GROUP - 1, 0) for piece in pieces] + [nothing]
        return jnp.concatenate(
            [
                jnp.where(line == 0, ups[y], ups[y + 1])
                + jnp.where(line == GROUP - 1, downs[y + 1], downs[y])
                for y in range(len(pieces))
            ],
            axis=0,
        )

    def sum_z(value):
        pieces = [value[:, z : z + LANES] for z in range(0, nz, LANES)]
        nothing = jnp.zeros_like(pieces[0])
        lane = lax.broadcasted_iota(jnp.int32, pieces[0].shape, 1)
        ups = [nothing] + [pltpu.roll(piece, 1, 1) for piece in pieces]
        downs = [pltpu.roll(piece, LANES - 1, 1) for piece in pieces] + [nothing]
        return jnp.concatenate(
            [
                jnp.where(lane == 0, ups[z], ups[z + 1])
                + jnp.where(lane == LANES - 1, downs[z + 1], downs[z])
                for z in range(len(pieces))
            ],
            axis=1,
        )

    def collect(j):
        def gather(e):
            def body(r, carry):
                for h in range(halves):
                    for y in range(0, ny, GROUP):
                        goal[
                            PAD + (e - 1) * GROUP + r,
                            y : y + GROUP,
                            h * LANES : (h + 1) * LANES,
                        ] = target[pl.ds(y * wide + e * tall + h * GROUP + r, GROUP, stride=wide), :]
                return carry

            lax.fori_loop(0, GROUP, body, 0)

        for e in range(j * slots, (j + 1) * slots):
            if e == 0:
                pl.when(me > 0)(functools.partial(gather, e))
            elif e == groups + 1:
                pl.when(me < n - 1)(functools.partial(gather, e))
            else:
                gather(e)

    def rise_load(origin, x, fresh):
        here, before, after = origin[x], origin[x - 1], origin[x + 1]
        olds = None if fresh else [dual[x] for dual in duals]
        return here, before, after, olds

    def rise(loaded, keep):
        here, before, after, olds = loaded
        twice = here + here
        raised = [before + after - twice, sum_y(here) - twice, sum_z(here) - twice]
        if olds is not None:
            raised = [old + bend for old, bend in zip(olds, raised)]
        norm = raised[0] * raised[0] + raised[1] * raised[1] + raised[2] * raised[2]
        shrink = lax.rsqrt(jnp.maximum(1.0 / relax**2, norm * (1.0 / (bound_dual * relax) ** 2)))
        if keep is not None:
            shrink = shrink * keep
        return [part_of * shrink for part_of in raised]

    def fall_load(x):
        dual_x, dual_y, dual_z = duals
        return (
            dual_x[x], dual_x[x - 1], dual_x[x + 1],
            dual_y[x], dual_z[x], goal[x],
        )

    def fall(loaded):
        in_x, before, after, in_y, in_z, _ = loaded
        middle = in_x + in_y + in_z
        return (before + after + sum_y(in_y) + sum_z(in_z) - (middle + middle)) * (
            step_primal * step_dual / (1.0 + step_primal)
        )

    def sweep_rows(outer, start, stop):
        def run(first, last):
            masked = first < DELAY or last > rows - WIDE + 1
            ends = first >= DELAY and last <= rows + DELAY
            lines = range(WIDE)

            def keep(x):
                whole = me * rows + PAD + x
                return jnp.where(jnp.logical_and(whole >= 2 * PAD, whole < nx + 2 * PAD), 1.0, 0.0)

            def body(k, carry):
                x = k * WIDE + (first + PAD)
                low = [rise_load(goal, x + i, outer == 0) for i in lines]
                mid = [fall_load(x - LAG + i) for i in lines]
                high = [rise_load(lead, x - 2 * LAG + i, False) for i in lines]
                if ends:
                    top = [fall_load(x - DELAY + i) for i in lines]
                    old = [field[x - DELAY + i] for i in lines]
                fresh = [rise(low[i], keep(x + i) if masked else None) for i in lines]
                updated = [mid[i][-1] - fall(mid[i]) for i in lines]
                if masked:
                    updated = [updated[i] * keep(x - LAG + i) for i in lines]
                again = [
                    rise(high[i], keep(x - 2 * LAG + i) if masked else None) for i in lines
                ]
                if ends:
                    final = [
                        old[i] * (1.0 / (1.0 + step_primal))
                        + top[i][-1] * (step_primal / (1.0 + step_primal))
                        - fall(top[i])
                        for i in lines
                    ]
                for i in lines:
                    for dual, value in zip(duals, fresh[i]):
                        dual[x + i] = value
                    lead[x - LAG + i] = updated[i] + updated[i] - mid[i][-1]
                    field[x - LAG + i] = updated[i]
                    for dual, value in zip(duals, again[i]):
                        dual[x - 2 * LAG + i] = value
                for i in lines:
                    at_x = x + i - PAD - DELAY
                    if ends and outer == OUTER - 1:
                        result[at_x] = final[i] * (1.0 / gain)
                    elif ends:
                        for h in range(halves):
                            at = cell_row(at_x, h)
                            for y in range(0, ny, GROUP):
                                current[pl.ds(at + y * deep, GROUP, stride=deep), :] = final[i][
                                    y : y + GROUP, h * LANES : (h + 1) * LANES
                                ]
                return carry

            lax.fori_loop(0, (last - first) // WIDE, body, 0)

        cuts = {x for x in (DELAY, rows - WIDE + 1, rows + DELAY) if start < x < stop}
        marks = sorted(cuts | {start, stop})
        for first, last in zip(marks[:-1], marks[1:]):
            run(first, last)

    homes = [(x, x + GROUP) for x in range(0, rows, GROUP)]

    def denoise(outer, sent):
        stop = rows + DELAY + (1 if WIDE == 1 and outer < OUTER - 1 else 0)
        held = []
        done = -5 if outer < OUTER - 1 else -3
        if outer < OUTER - 1:
            ready = {batch[2] * GROUP + DELAY: batch for batch in batches}
        else:
            ready = {last + DELAY: (first, last) for first, last in homes}
        def later(j):
            if j < chunks:
                send_back(j)
            elif j < extents:
                start_back(j)

        if sent == chunks:
            for j in range(sent, extents):
                later(j)
            sent = extents
        for j in range(extents):
            back_bulk(j).wait_recv()
            collect(j)
            limit = stop if j == extents - 1 else ((j + 1) * slots - 1) * GROUP - 1
            for x in sorted(ready):
                if done < x <= limit:
                    sweep_rows(outer, done, x)
                    if outer < OUTER - 1:
                        send_forward(ready[x], 0)
                        held.append(ready[x])
                    else:
                        deliver(*ready[x])
                    done = x
            if done < limit:
                sweep_rows(outer, done, limit)
                done = limit
            later(j + sent)
        for batch in held:
            send_forward(batch, 1)

    turns = list(range(1, chunks)) + [0]
    loads[0].wait()
    lax.fori_loop(0, ny, stage, 0)
    pl.semaphore_wait(barrier, greeted - 1)
    asides = [(batch, side) for side in range(WAVES) for batch in aside]
    for turn in asides[:2]:
        send_aside(*turn)
    for side in range(WAVES):
        for i, batch in enumerate(first_turn):
            send_direct(batch, side)
            at = side * len(aside) + i + 2
            for turn in asides[at : at + 1] if i < len(aside) else []:
                send_aside(*turn)

    @pl.when(me == 0)
    def _():
        goal[PAD - GROUP : PAD] = jnp.zeros((GROUP, ny, nz), f32)

    @pl.when(me == n - 1)
    def _():
        goal[PAD + rows : PAD + rows + GROUP] = jnp.zeros((GROUP, ny, nz), f32)

    for load in loads[1:]:
        load.wait()
    make_tables()
    for turn in asides[:1]:
        pass_along(*turn)
    make_filter()
    for turn in asides[1:]:
        pass_along(*turn)
    for outer in range(OUTER):
        filtered(outer)
        lead_in = chunks if outer < OUTER - 1 else min(chunks, 3)
        for j in range(lead_in):
            send_back(j)
        for batch in batches:
            if outer == 0:
                first_sent(batch)
            else:
                forward_bulk(batch, n - 1).wait_send()
        denoise(outer, lead_in)
        for j in range(extents):
            back_bulk(j).wait_send()
    delivered()


def constants(n, rows, slots, nz):
    nx = n * rows
    groups = rows // GROUP
    place = np.array(
        [
            ((d * groups + c + slot - 1) * GROUP + r) % nx
            for c in range(0, groups, slots)
            for d in range(n)
            for slot in range(slots)
            for r in range(GROUP)
        ]
    )
    turn = 2.0 * math.pi / nx
    coarse = (place[::GROUP, None] * place[None, :] % nx) * turn
    fine = (np.arange(GROUP)[:, None] * place[None, :] % nx) * turn
    norm = 1.0 / math.sqrt(nx)
    tables = (
        np.cos(coarse),
        np.sin(coarse),
        (np.cos(fine) + np.sin(fine)) * norm,
        (np.cos(fine) - np.sin(fine)) * norm,
    )
    k = np.arange(nz)
    angle = (k[:, None] * k[None, :] % nz) * (2.0 * math.pi / nz)
    cas_z = ((np.cos(angle) + np.sin(angle)) / math.sqrt(nz)).astype(np.float32)
    z_high = cas_z.astype(bf16)
    z_low = (cas_z - z_high.astype(np.float32)).astype(bf16)
    return [jnp.asarray(t, f32) for t in tables] + [jnp.asarray(z_high), jnp.asarray(z_low)]


def local(n, cross, observed, tf_table, tilt_index, wedge):
    rows, ny, nz = observed.shape
    nx = n * rows
    groups = rows // GROUP
    slots = 2 if groups % 2 == 0 else 1
    chunks = groups // slots
    extents = (groups + 2) // slots
    lines, columns = tilt_index.shape
    depth, width = -(-lines // 128) * 128, -(-columns // 128) * 128
    tables = constants(n, rows, slots, nz)
    tiles = observed.reshape(rows, ny // GROUP, GROUP, nz // LANES, LANES)
    tiles = tiles.transpose(0, 1, 3, 2, 4).reshape(-1, LANES)
    vmem = pl.BlockSpec(memory_space=pltpu.VMEM)
    smem = pl.BlockSpec(memory_space=pltpu.SMEM)
    hbm = pl.BlockSpec(memory_space=pltpu.HBM)
    operands = (tiles, tilt_index.T, wedge.T, *tables)
    grid_rows = pltpu.VMEM((rows + 2 * PAD, ny, nz), f32)
    plane = pltpu.VMEM((nx, nz), f32)
    blocks = pltpu.VMEM((chunks, n * slots * GROUP * nz // LANES, LANES), f32)
    cells = pltpu.VMEM((rows * ny * nz // LANES, LANES), f32)
    semaphores = pltpu.SemaphoreType.DMA((extents,))
    landing = pltpu.VMEM((ny * (groups + 2) * GROUP * nz // LANES, LANES), f32)
    result = pl.pallas_call(
        functools.partial(kernel, n, rows, slots, cross),
        out_shape=pltpu.VMEM((rows, ny, nz), f32),
        in_specs=[hbm, smem] + [hbm] * 8,
        out_specs=vmem,
        scratch_shapes=[pltpu.VMEM(operand.shape, operand.dtype) for operand in operands]
        + [
            pltpu.SemaphoreType.DMA((len(operands),)),
            blocks,
            plane,
            plane,
            plane,
            pltpu.VMEM((nx, nx), bf16),
            pltpu.VMEM((nx, nx), bf16),
            pltpu.VMEM((nx, nz), bf16),
            pltpu.VMEM((nx, nz), bf16),
            blocks,
            landing,
            grid_rows,
            grid_rows,
            grid_rows,
            [grid_rows] * 3,
            cells,
            pltpu.VMEM((width, depth), f32),
            pltpu.VMEM((rows * ny * nz // LANES // 2, LANES), f32),
            pltpu.VMEM((rows, ny, nz), f32),
            semaphores,
            semaphores,
            semaphores,
            semaphores,
            pltpu.SemaphoreType.DMA((WAVES, extents)),
            pltpu.SemaphoreType.DMA((WAVES, extents)),
            semaphores,
            pltpu.SemaphoreType.DMA(()),
            pltpu.SemaphoreType.DMA(()),
            pltpu.SemaphoreType.DMA(()),
        ],
        compiler_params=pltpu.CompilerParams(
            collective_id=0, has_side_effects=True, vmem_limit_bytes=60 * 1024 * 1024
        ),
    )(operands[0], tf_table, *operands[1:])
    return result


def solution(mesh):
    in_specs = (P(("groups", "gy"), None, None), P(), P(), P())
    out_specs = P(("groups", "gy"), None, None)
    n = mesh.shape["gy"]
    cross = mesh.shape["groups"] == 2 and n % (2 * WAVES) == 0
    body = functools.partial(local, n, cross)
    return jax.shard_map(body, mesh=mesh, in_specs=in_specs, out_specs=out_specs, check_vma=False)
```

```python
import functools
import math

import jax
import jax.numpy as jnp
import numpy as np
from jax import lax
from jax.experimental import pallas as pl
from jax.experimental.pallas import tpu as pltpu
from jax.sharding import PartitionSpec as P

WAVES = 2
OUTER = 2
PASSES = 2
GROUP = 8
LANES = 128
WIDE = 2
LAG = WIDE + 1
DELAY = 3 * LAG
PAD = 12

step_dual = 0.14
step_primal = 0.14
huber_eps = 0.05
bound_dual = 0.5
relax = 1.0 / (1.0 + step_dual * huber_eps / bound_dual)
gain = step_dual * relax
MESH = pl.DeviceIdType.MESH
f32 = jnp.float32
bf16 = jnp.bfloat16


def split(value):
    high = value.astype(bf16)
    low = (value - high.astype(f32)).astype(bf16)
    return high, low


def dot3(a_high, a_low, b_high, b_low):
    dot = functools.partial(jnp.dot, preferred_element_type=f32)
    return dot(a_high, b_high) + (dot(a_high, b_low) + dot(a_low, b_high))


def kernel(
    n, rows, slots, cross,
    cells_in, table_ref, tilt_in, wedge_in, cos_in, sin_in, cas_in, case_in, zh_in, zl_in,
    out_ref,
    cells_ref, tilt_ref, wedge_ref, cos_ref, sin_ref, cas_ref, case_ref, zh_ref, zl_ref, load_sem,
    gathered, total, data_term, prior_gain, x_high, x_low, m_high, m_low, back,
    target, goal, field, lead, duals, current, code, passing, result,
    send_sem, recv_sem, back_send, back_recv,
    pass_send, pass_recv, pass_on, home_send, home_recv, own_sem,
):
    gx, gy = lax.axis_index("groups"), lax.axis_index("gy")
    half = n // 2
    high, low = gy // half, gy % half
    if cross:
        near = gx == high
        who = gx * half + low
        me = low % 2 * half + low // 2 * 2 + gx
    else:
        near = gx == gx
        who = gy
        me = gy
    far = jnp.logical_not(near)

    def owner_device(owner, first):
        if not cross:
            return {"gy": owner}
        block = gx if first else high
        return {"groups": owner // half, "gy": block * half + owner % half}

    def slab_device(slab):
        if not cross:
            return {"gy": slab}
        return {"groups": slab % 2, "gy": high * half + slab % half // 2 * 2 + slab // half}

    groups = rows // GROUP
    chunks = groups // slots
    extents = (groups + 2) // slots
    part = slots * GROUP
    ny, nz = out_ref.shape[1], out_ref.shape[2]
    halves = nz // LANES
    tall = GROUP * halves
    deep = groups * tall
    wide = (groups + 2) * tall
    share = slots * tall
    batches = [
        (m, max(m * slots - 1, 0), min((m + 1) * slots - 1, groups))
        for m in range(1 // slots, groups // slots + 1)
    ]
    aside = batches[:-1]
    first_turn = [batch for batch in batches if batch[0] % chunks > 0]
    first_turn += [batch for batch in batches if batch[0] % chunks == 0]
    nx = n * rows
    span_rows = n * part
    block = math.gcd(nx, 256)
    row_blocks = nx // block

    barrier = pltpu.get_barrier_semaphore()

    def greet(o, carry):
        if cross:
            other = lax.rem(gx * n + gy + o, 2 * n)
            device = {"groups": other // n, "gy": other % n}
        else:
            device = {"gy": lax.rem(gy + o, n)}
        pl.semaphore_signal(barrier, inc=1, device_id=device, device_id_type=MESH)
        return carry

    greeted = 2 * n if cross else n
    loads = [
        pltpu.make_async_copy(source, place, load_sem.at[i])
        for i, (source, place) in enumerate(
            [
                (cells_in, cells_ref),
                (cos_in, cos_ref),
                (sin_in, sin_ref),
                (cas_in, cas_ref),
                (case_in, case_ref),
                (tilt_in, tilt_ref),
                (wedge_in, wedge_ref),
                (zh_in, zh_ref),
                (zl_in, zl_ref),
            ]
        )
    ]
    for load in loads:
        load.start()
    lax.fori_loop(1, greeted, greet, 0)

    def every_other(mine, action):
        def step(o, carry):
            action(lax.rem(mine + o, n))
            return carry

        lax.fori_loop(1, n, step, 0, unroll=5 if n % 5 == 1 else 1)

    def every_half(side, action):
        count = half // WAVES

        def step(o, carry):
            action(lax.rem(low // WAVES + o, count) * WAVES + side)
            return carry

        lax.fori_loop(0, count, step, 0)

    def cells_of(y, batch, depth):
        _, low_group, high_group = batch
        return pl.ds(pl.multiple_of(y * depth + low_group * tall, tall), (high_group - low_group) * tall)

    def seat_of(slab, batch):
        m, low_group, high_group = batch
        line = lax.rem(slab + m // chunks, n) * slots + (low_group + 1) % slots
        return pl.ds(pl.multiple_of(line * tall, tall), (high_group - low_group) * tall)

    def block_of(j, slab):
        return pl.ds(pl.multiple_of(lax.rem(slab + j // chunks, n) * share, share), share)

    def extent_of(y, j):
        return pl.ds(pl.multiple_of(y * wide + j * share, tall), share)

    def cell_row(x, h):
        return (x // GROUP * halves + h) * GROUP + lax.rem(x, GROUP)

    def forward_copy(batch, owner, slab, first):
        m = batch[0]
        return pltpu.make_async_remote_copy(
            src_ref=current.at[cells_of(owner, batch, deep)],
            dst_ref=gathered.at[m % chunks, seat_of(slab, batch)],
            send_sem=send_sem.at[m],
            recv_sem=recv_sem.at[m],
            device_id=owner_device(owner, first),
            device_id_type=MESH,
        )

    def pass_copy(batch, side, k):
        m = batch[0]
        return pltpu.make_async_remote_copy(
            src_ref=current.at[cells_of((1 - gx) * half + k, batch, deep)],
            dst_ref=passing.at[cells_of(k, batch, deep)],
            send_sem=pass_send.at[side, m],
            recv_sem=pass_recv.at[side, m],
            device_id={"groups": 1 - gx, "gy": gy},
            device_id_type=MESH,
        )

    def pass_on_copy(batch, k):
        m = batch[0]
        return pltpu.make_async_remote_copy(
            src_ref=passing.at[cells_of(k, batch, deep)],
            dst_ref=gathered.at[m % chunks, seat_of(gy, batch)],
            send_sem=pass_on.at[m],
            recv_sem=recv_sem.at[m],
            device_id={"groups": gx, "gy": (1 - gx) * half + k},
            device_id_type=MESH,
        )

    def back_copy(j, slab):
        return pltpu.make_async_remote_copy(
            src_ref=back.at[j % chunks, block_of(j, slab)],
            dst_ref=target.at[extent_of(who, j)],
            send_sem=back_send.at[j],
            recv_sem=back_recv.at[j],
            device_id=slab_device(slab),
            device_id_type=MESH,
        )

    def home_copy(first, last):
        span = pl.ds(first, last - first)
        return pltpu.make_async_remote_copy(
            src_ref=result.at[span],
            dst_ref=out_ref.at[span],
            send_sem=home_send,
            recv_sem=home_recv,
            device_id={"groups": high, "gy": me},
            device_id_type=MESH,
        )

    def own_copy(first, last):
        span = pl.ds(first, last - first)
        return pltpu.make_async_copy(result.at[span], out_ref.at[span], own_sem)

    if cross:
        home = jnp.logical_and(gx == high, gy == me)
        away = jnp.logical_not(home)
    else:
        home, away = near, far

    def deliver(first, last):
        if cross:

            @pl.when(away)
            def _():
                home_copy(first, last).start()

        @pl.when(home)
        def _():
            own_copy(first, last).start()

    def delivered():
        if cross:

            @pl.when(away)
            def _():
                home_copy(0, rows).wait_send()
                home_copy(0, rows).wait_recv()

        @pl.when(home)
        def _():
            own_copy(0, rows).wait()

    def bulk(ref, lines, send, recv):
        span = ref.at[pl.ds(0, lines)]
        return pltpu.make_async_remote_copy(
            src_ref=span,
            dst_ref=span,
            send_sem=send,
            recv_sem=recv,
            device_id=owner_device(who, False),
            device_id_type=MESH,
        )

    def lines_of(batch):
        return (batch[2] - batch[1]) * tall

    def forward_bulk(batch, count):
        m = batch[0]
        return bulk(current, count * lines_of(batch), send_sem.at[m], recv_sem.at[m])

    def pass_bulk(batch, side):
        lines = half // WAVES * lines_of(batch)
        return bulk(passing, lines, pass_send.at[side, batch[0]], pass_recv.at[side, batch[0]])

    def pass_on_bulk(batch):
        m = batch[0]
        return bulk(passing, half * lines_of(batch), pass_on.at[m], pass_recv.at[0, m])

    def back_bulk(j):
        return bulk(target, (n - 1) * share, back_send.at[j], back_recv.at[j])

    def keep_own(batch, slab):
        gathered[batch[0] % chunks, seat_of(slab, batch)] = current[cells_of(who, batch, deep)]

    def send_direct(batch, side):
        if not cross:
            if side == 0:
                every_other(who, lambda owner: forward_copy(batch, owner, gy, True).start())
                keep_own(batch, gy)
            return

        @pl.when(far)
        def _():
            every_half(side, lambda k: forward_copy(batch, gx * half + k, gy, True).start())
            if batch not in aside:
                every_half(
                    side, lambda k: forward_copy(batch, (1 - gx) * half + k, gy, True).start()
                )

        @pl.when(near)
        def _():
            every_half(side, lambda k: forward_copy(batch, (1 - gx) * half + k, gy, True).start())

            def own_row(k):
                @pl.when(k != low)
                def _():
                    forward_copy(batch, gx * half + k, gy, True).start()

            every_half(side, own_row)
            if side == 0:
                keep_own(batch, gy)

    def send_aside(batch, side):
        if cross:

            @pl.when(far)
            def _():
                every_half(side, lambda k: pass_copy(batch, side, k).start())

    def pass_along(batch, side):
        if cross:

            @pl.when(near)
            def _():
                pass_bulk(batch, side).wait_recv()
                every_half(side, lambda k: pass_on_copy(batch, k).start())

    def first_arrived(batch):
        @pl.when(near)
        def _():
            forward_bulk(batch, n - 1).wait_recv()

        if cross:

            @pl.when(far)
            def _():
                forward_bulk(batch, n).wait_recv()

    def first_sent(batch):
        relayed = cross and batch in aside

        @pl.when(near)
        def _():
            forward_bulk(batch, n - 1).wait_send()
            if relayed:
                pass_on_bulk(batch).wait_send()

        if cross:

            @pl.when(far)
            def _():
                forward_bulk(batch, half if relayed else n).wait_send()
                if relayed:
                    for side in range(WAVES):
                        pass_bulk(batch, side).wait_send()

    def send_forward(batch, side):
        def step(o, carry):
            owner = lax.rem(who // 2 + o, half) * 2 + side

            @pl.when(owner != who)
            def _():
                forward_copy(batch, owner, me, False).start()

            return carry

        lax.fori_loop(0, half, step, 0)
        if side == 0:
            keep_own(batch, me)

    def stage(y, carry):
        stride = ny * halves
        for h in range(halves):
            first = (y // GROUP * halves + h) * GROUP + y % GROUP
            lines = cells_ref[pl.ds(first, rows, stride=stride), :]
            for g in range(groups):
                at = y * deep + g * tall + h * GROUP
                current[pl.ds(pl.multiple_of(at, GROUP), GROUP), :] = lines[
                    g * GROUP : (g + 1) * GROUP, :
                ]
        return carry

    def make_tables():
        def body(m, carry):
            lines = jnp.concatenate(
                [
                    cos_ref[pl.ds(k, 1), :] * cas_ref[...] + sin_ref[pl.ds(k, 1), :] * case_ref[...]
                    for k in (2 * m, 2 * m + 1)
                ],
                axis=0,
            )
            at = pl.ds(pl.multiple_of(m * 2 * GROUP, 2 * GROUP), 2 * GROUP)
            x_high[at, :], x_low[at, :] = split(lines)
            return carry

        lax.fori_loop(0, nx // (2 * GROUP), body, 0)

    def make_filter():
        columns, lines = tilt_ref.shape
        code[...] = jnp.zeros_like(code)
        code[0:columns, 0:lines] = jnp.where(wedge_ref[...] == 0, 0, tilt_ref[...] + 1).astype(f32)
        width, depth = code.shape
        kz = lax.broadcasted_iota(jnp.int32, (nz, width), 0)
        pick_z = jnp.where(
            lax.broadcasted_iota(jnp.int32, (nz, width), 1) == jnp.minimum(kz, nz - kz), 1.0, 0.0
        ).astype(bf16)
        spread = jnp.dot(pick_z, code[...].astype(bf16), preferred_element_type=f32).astype(bf16)

        def body(b, carry):
            line = b * block + lax.broadcasted_iota(jnp.int32, (block, depth), 0)
            c = line // span_rows
            slot = line % part // GROUP
            place = line % span_rows // part * groups + c * slots + slot - 1
            kx = (place * GROUP + line % GROUP + nx) % nx
            column = lax.broadcasted_iota(jnp.int32, (block, depth), 1)
            pick_x = jnp.where(column == jnp.minimum(kx, nx - kx), 1.0, 0.0).astype(bf16)
            which = lax.dot_general(
                pick_x, spread, (((1,), (1,)), ((), ())), preferred_element_type=f32
            )
            response = jnp.zeros_like(which)
            for level in range(table_ref.shape[0]):
                response = jnp.where(which == level + 1.0, table_ref[level], response)
            prior = 1.0 / (response * response + 1.0)
            at = pl.ds(pl.multiple_of(b * block, block), block)
            prior_gain[at, :] = prior
            data_term[at, :] = response * prior
            return carry

        lax.fori_loop(0, row_blocks, body, 0)

    def filtered(outer):
        for c in turns:
            for batch in batches:
                if batch[0] % chunks == c and outer == 0:
                    first_arrived(batch)
                elif batch[0] % chunks == c:
                    forward_bulk(batch, n - 1).wait_recv()
            pieces = gathered[c].reshape(n * slots, halves, GROUP, LANES)
            lines = [pieces[:, h].reshape(span_rows, LANES) for h in range(halves)]
            high, low = split(jnp.concatenate(lines, axis=1))
            high, low = split(dot3(high, low, zh_ref[...], zl_ref[...]))

            def body(b, carry):
                at = pl.ds(pl.multiple_of(b * block, block), block)
                span = pl.ds(c * span_rows, span_rows)
                spectrum = dot3(x_high[at, span], x_low[at, span], high, low)
                if c != turns[0]:
                    spectrum = total[at, :] + spectrum
                if c != turns[-1]:
                    total[at, :] = spectrum
                    return carry
                if outer == 0:
                    spectrum = spectrum * gain
                    data_term[at, :] = data_term[at, :] * spectrum
                a_high, a_low = split(data_term[at, :] + prior_gain[at, :] * spectrum)
                m_high[at, :], m_low[at, :] = split(dot3(a_high, a_low, zh_ref[...], zl_ref[...]))
                return carry

            lax.fori_loop(0, row_blocks, body, 0, unroll=True)

    def send_back(c):
        step = math.gcd(span_rows, 256)

        def body(b, carry):
            line = pl.ds(pl.multiple_of(c * span_rows + b * step, step), step)
            lines = dot3(x_high[line, :], x_low[line, :], m_high[...], m_low[...])
            pieces = [
                lines[:, h * LANES : (h + 1) * LANES].reshape(step // GROUP, 1, GROUP, LANES)
                for h in range(halves)
            ]
            count = step * halves
            at = pl.ds(pl.multiple_of(b * count, count), count)
            back[c, at] = jnp.concatenate(pieces, axis=1).reshape(count, LANES)
            return carry

        lax.fori_loop(0, span_rows // step, body, 0)
        start_back(c)

    def start_back(j):
        every_other(me, lambda slab: back_copy(j, slab).start())
        target[extent_of(who, j)] = back[j % chunks, block_of(j, me)]

    def sum_y(value):
        pieces = [value[y : y + GROUP, :] for y in range(0, ny, GROUP)]
        nothing = jnp.zeros_like(pieces[0])
        line = lax.broadcasted_iota(jnp.int32, pieces[0].shape, 0)
        ups = [nothing] + [pltpu.roll(piece, 1, 0) for piece in pieces]
        downs = [pltpu.roll(piece, GROUP - 1, 0) for piece in pieces] + [nothing]
        return jnp.concatenate(
            [
                jnp.where(line == 0, ups[y], ups[y + 1])
                + jnp.where(line == GROUP - 1, downs[y + 1], downs[y])
                for y in range(len(pieces))
            ],
            axis=0,
        )

    def sum_z(value):
        pieces = [value[:, z : z + LANES] for z in range(0, nz, LANES)]
        nothing = jnp.zeros_like(pieces[0])
        lane = lax.broadcasted_iota(jnp.int32, pieces[0].shape, 1)
        ups = [nothing] + [pltpu.roll(piece, 1, 1) for piece in pieces]
        downs = [pltpu.roll(piece, LANES - 1, 1) for piece in pieces] + [nothing]
        return jnp.concatenate(
            [
                jnp.where(lane == 0, ups[z], ups[z + 1])
                + jnp.where(lane == LANES - 1, downs[z + 1], downs[z])
                for z in range(len(pieces))
            ],
            axis=1,
        )

    def collect(j):
        def gather(e):
            def body(r, carry):
                for h in range(halves):
                    for y in range(0, ny, GROUP):
                        goal[
                            PAD + (e - 1) * GROUP + r,
                            y : y + GROUP,
                            h * LANES : (h + 1) * LANES,
                        ] = target[pl.ds(y * wide + e * tall + h * GROUP + r, GROUP, stride=wide), :]
                return carry

            lax.fori_loop(0, GROUP, body, 0)

        for e in range(j * slots, (j + 1) * slots):
            if e == 0:
                pl.when(me > 0)(functools.partial(gather, e))
            elif e == groups + 1:
                pl.when(me < n - 1)(functools.partial(gather, e))
            else:
                gather(e)

    def rise_load(origin, x, fresh):
        here, before, after = origin[x], origin[x - 1], origin[x + 1]
        olds = None if fresh else [dual[x] for dual in duals]
        return here, before, after, olds

    def rise(loaded, keep):
        here, before, after, olds = loaded
        twice = here + here
        raised = [before + after - twice, sum_y(here) - twice, sum_z(here) - twice]
        if olds is not None:
            raised = [old + bend for old, bend in zip(olds, raised)]
        norm = raised[0] * raised[0] + raised[1] * raised[1] + raised[2] * raised[2]
        shrink = lax.rsqrt(jnp.maximum(1.0 / relax**2, norm * (1.0 / (bound_dual * relax) ** 2)))
        if keep is not None:
            shrink = shrink * keep
        return [part_of * shrink for part_of in raised]

    def fall_load(x):
        dual_x, dual_y, dual_z = duals
        return (
            dual_x[x], dual_x[x - 1], dual_x[x + 1],
            dual_y[x], dual_z[x], goal[x],
        )

    def fall(loaded):
        in_x, before, after, in_y, in_z, _ = loaded
        middle = in_x + in_y + in_z
        return (before + after + sum_y(in_y) + sum_z(in_z) - (middle + middle)) * (
            step_primal * step_dual / (1.0 + step_primal)
        )

    def sweep_rows(outer, start, stop):
        def run(first, last):
            masked = first < DELAY or last > rows - WIDE + 1
            ends = first >= DELAY and last <= rows + DELAY
            lines = range(WIDE)

            def keep(x):
                whole = me * rows + PAD + x
                return jnp.where(jnp.logical_and(whole >= 2 * PAD, whole < nx + 2 * PAD), 1.0, 0.0)

            def body(k, carry):
                x = k * WIDE + (first + PAD)
                low = [rise_load(goal, x + i, outer == 0) for i in lines]
                mid = [fall_load(x - LAG + i) for i in lines]
                high = [rise_load(lead, x - 2 * LAG + i, False) for i in lines]
                if ends:
                    top = [fall_load(x - DELAY + i) for i in lines]
                    old = [field[x - DELAY + i] for i in lines]
                fresh = [rise(low[i], keep(x + i) if masked else None) for i in lines]
                updated = [mid[i][-1] - fall(mid[i]) for i in lines]
                if masked:
                    updated = [updated[i] * keep(x - LAG + i) for i in lines]
                again = [
                    rise(high[i], keep(x - 2 * LAG + i) if masked else None) for i in lines
                ]
                if ends:
                    final = [
                        old[i] * (1.0 / (1.0 + step_primal))
                        + top[i][-1] * (step_primal / (1.0 + step_primal))
                        - fall(top[i])
                        for i in lines
                    ]
                for i in lines:
                    for dual, value in zip(duals, fresh[i]):
                        dual[x + i] = value
                    lead[x - LAG + i] = updated[i] + updated[i] - mid[i][-1]
                    field[x - LAG + i] = updated[i]
                    for dual, value in zip(duals, again[i]):
                        dual[x - 2 * LAG + i] = value
                for i in lines:
                    at_x = x + i - PAD - DELAY
                    if ends and outer == OUTER - 1:
                        result[at_x] = final[i] * (1.0 / gain)
                    elif ends:
                        for h in range(halves):
                            at = cell_row(at_x, h)
                            for y in range(0, ny, GROUP):
                                current[pl.ds(at + y * deep, GROUP, stride=deep), :] = final[i][
                                    y : y + GROUP, h * LANES : (h + 1) * LANES
                                ]
                return carry

            lax.fori_loop(0, (last - first) // WIDE, body, 0)

        cuts = {x for x in (DELAY, rows - WIDE + 1, rows + DELAY) if start < x < stop}
        marks = sorted(cuts | {start, stop})
        for first, last in zip(marks[:-1], marks[1:]):
            run(first, last)

    homes = [(x, x + GROUP) for x in range(0, rows, GROUP)]

    def denoise(outer, sent):
        stop = rows + DELAY + (1 if WIDE == 1 and outer < OUTER - 1 else 0)
        held = []
        done = -5 if outer < OUTER - 1 else -3
        if outer < OUTER - 1:
            ready = {batch[2] * GROUP + DELAY: batch for batch in batches}
        else:
            ready = {last + DELAY: (first, last) for first, last in homes}
        def later(j):
            if j < chunks:
                send_back(j)
            elif j < extents:
                start_back(j)

        if sent == chunks:
            for j in range(sent, extents):
                later(j)
            sent = extents
        for j in range(extents):
            back_bulk(j).wait_recv()
            collect(j)
            limit = stop if j == extents - 1 else ((j + 1) * slots - 1) * GROUP - 1
            for x in sorted(ready):
                if done < x <= limit:
                    sweep_rows(outer, done, x)
                    if outer < OUTER - 1:
                        send_forward(ready[x], 0)
                        held.append(ready[x])
                    else:
                        deliver(*ready[x])
                    done = x
            if done < limit:
                sweep_rows(outer, done, limit)
                done = limit
            later(j + sent)
        for batch in held:
            send_forward(batch, 1)

    turns = list(range(1, chunks)) + [0]
    loads[0].wait()
    lax.fori_loop(0, ny, stage, 0)
    pl.semaphore_wait(barrier, greeted - 1)
    asides = [(batch, side) for side in range(WAVES) for batch in aside]
    for turn in asides[:2]:
        send_aside(*turn)
    for side in range(WAVES):
        for i, batch in enumerate(first_turn):
            send_direct(batch, side)
            at = side * len(aside) + i + 2
            for turn in asides[at : at + 1] if i < len(aside) else []:
                send_aside(*turn)

    @pl.when(me == 0)
    def _():
        goal[PAD - GROUP : PAD] = jnp.zeros((GROUP, ny, nz), f32)

    @pl.when(me == n - 1)
    def _():
        goal[PAD + rows : PAD + rows + GROUP] = jnp.zeros((GROUP, ny, nz), f32)

    for load in loads[1:]:
        load.wait()
    make_tables()
    for turn in asides[:1]:
        pass_along(*turn)
    make_filter()
    for turn in asides[1:]:
        pass_along(*turn)
    for outer in range(OUTER):
        filtered(outer)
        lead_in = chunks if outer < OUTER - 1 else min(chunks, 3)
        for j in range(lead_in):
            send_back(j)
        for batch in batches:
            if outer == 0:
                first_sent(batch)
            else:
                forward_bulk(batch, n - 1).wait_send()
        denoise(outer, lead_in)
        for j in range(extents):
            back_bulk(j).wait_send()
    delivered()


def constants(n, rows, slots, nz):
    nx = n * rows
    groups = rows // GROUP
    place = np.array(
        [
            ((d * groups + c + slot - 1) * GROUP + r) % nx
            for c in range(0, groups, slots)
            for d in range(n)
            for slot in range(slots)
            for r in range(GROUP)
        ]
    )
    turn = 2.0 * math.pi / nx
    coarse = (place[::GROUP, None] * place[None, :] % nx) * turn
    fine = (np.arange(GROUP)[:, None] * place[None, :] % nx) * turn
    norm = 1.0 / math.sqrt(nx)
    tables = (
        np.cos(coarse),
        np.sin(coarse),
        (np.cos(fine) + np.sin(fine)) * norm,
        (np.cos(fine) - np.sin(fine)) * norm,
    )
    k = np.arange(nz)
    angle = (k[:, None] * k[None, :] % nz) * (2.0 * math.pi / nz)
    cas_z = ((np.cos(angle) + np.sin(angle)) / math.sqrt(nz)).astype(np.float32)
    z_high = cas_z.astype(bf16)
    z_low = (cas_z - z_high.astype(np.float32)).astype(bf16)
    return [jnp.asarray(t, f32) for t in tables] + [jnp.asarray(z_high), jnp.asarray(z_low)]


def local(n, cross, observed, tf_table, tilt_index, wedge):
    rows, ny, nz = observed.shape
    nx = n * rows
    groups = rows // GROUP
    slots = 2 if groups % 2 == 0 else 1
    chunks = groups // slots
    extents = (groups + 2) // slots
    lines, columns = tilt_index.shape
    depth, width = -(-lines // 128) * 128, -(-columns // 128) * 128
    tables = constants(n, rows, slots, nz)
    tiles = observed.reshape(rows, ny // GROUP, GROUP, nz // LANES, LANES)
    tiles = tiles.transpose(0, 1, 3, 2, 4).reshape(-1, LANES)
    vmem = pl.BlockSpec(memory_space=pltpu.VMEM)
    smem = pl.BlockSpec(memory_space=pltpu.SMEM)
    hbm = pl.BlockSpec(memory_space=pltpu.HBM)
    operands = (tiles, tilt_index.T, wedge.T, *tables)
    grid_rows = pltpu.VMEM((rows + 2 * PAD, ny, nz), f32)
    plane = pltpu.VMEM((nx, nz), f32)
    blocks = pltpu.VMEM((chunks, n * slots * GROUP * nz // LANES, LANES), f32)
    cells = pltpu.VMEM((rows * ny * nz // LANES, LANES), f32)
    semaphores = pltpu.SemaphoreType.DMA((extents,))
    landing = pltpu.VMEM((ny * (groups + 2) * GROUP * nz // LANES, LANES), f32)
    result = pl.pallas_call(
        functools.partial(kernel, n, rows, slots, cross),
        out_shape=pltpu.VMEM((rows, ny, nz), f32),
        in_specs=[hbm, smem] + [hbm] * 8,
        out_specs=vmem,
        scratch_shapes=[pltpu.VMEM(operand.shape, operand.dtype) for operand in operands]
        + [
            pltpu.SemaphoreType.DMA((len(operands),)),
            blocks,
            plane,
            plane,
            plane,
            pltpu.VMEM((nx, nx), bf16),
            pltpu.VMEM((nx, nx), bf16),
            pltpu.VMEM((nx, nz), bf16),
            pltpu.VMEM((nx, nz), bf16),
            blocks,
            landing,
            grid_rows,
            grid_rows,
            grid_rows,
            [grid_rows] * 3,
            cells,
            pltpu.VMEM((width, depth), f32),
            pltpu.VMEM((rows * ny * nz // LANES // 2, LANES), f32),
            pltpu.VMEM((rows, ny, nz), f32),
            semaphores,
            semaphores,
            semaphores,
            semaphores,
            pltpu.SemaphoreType.DMA((WAVES, extents)),
            pltpu.SemaphoreType.DMA((WAVES, extents)),
            semaphores,
            pltpu.SemaphoreType.DMA(()),
            pltpu.SemaphoreType.DMA(()),
            pltpu.SemaphoreType.DMA(()),
        ],
        compiler_params=pltpu.CompilerParams(
            collective_id=0, has_side_effects=True, vmem_limit_bytes=60 * 1024 * 1024
        ),
    )(operands[0], tf_table, *operands[1:])
    return result


def solution(mesh):
    in_specs = (P(("groups", "gy"), None, None), P(), P(), P())
    out_specs = P(("groups", "gy"), None, None)
    n = mesh.shape["gy"]
    cross = mesh.shape["groups"] == 2 and n % (2 * WAVES) == 0
    body = functools.partial(local, n, cross)
    return jax.shard_map(body, mesh=mesh, in_specs=in_specs, out_specs=out_specs, check_vma=False)
```
